256 devices in a mesh: section: 16 (over y_lo, z), dp: 16 (over x, y_hi, core).
Axes of the slice: x: 4, y: 4 (y_hi: 2, y_lo: 2; y = y_hi * 2 + y_lo), z: 8, core: 2. Of those that a mesh axis runs over, the one named last changes fastest.
Arguments:
- entering: bfloat16 [16, 2048, 8192], P('section', 'dp'), may hold values from -6 to 6
- returning: bfloat16 [16, 2048, 8192], P('section', 'dp'), may hold values from -6 to 6
- adapter_down: bfloat16 [2, 16, 64, 8192], P(None, 'section'), may hold values from -0.0625 to 0.0625
- adapter_up: bfloat16 [2, 16, 64, 8192], P(None, 'section'), may hold values from -0.75 to 0.75
- stashed: float32 [16, 3, 64, 2048], P('section', None, None, 'dp'), may hold values from -6 to 6
- doc_ids: int32 [16, 2048], P(None, 'dp'), may hold values from 0 to 31, never falling along the last dimension, each value on 1 to 256 neighbouring positions
- input_factor: float32 [16, 8192, 1024], P('section', 'dp'), may hold values from -3 to 3
- output_factor: float32 [2, 16, 64, 64], P(None, 'section'), may hold values from -3 to 3
Outputs:
- input_factor_new: float32 [16, 8192, 1024], P('section', 'dp')
- output_factor_new: float32 [2, 16, 64, 64], P(None, 'section')
The draws below stay inside these ranges and needn't reach their ends.
Inputs may be any that keep to these rules, and one draw needn't show every extreme that they name: `doc_ids`: each row packs 32 documents in order: document numbers never fall along a row, every document has 1 to 256 tokens, and some document of every row has exactly 256.
All inputs are finite; a program needn't handle non-finite values.
Results may differ from the reference program's by a relative error of at most 0.0044.
Values may be sent and summed in bfloat16 or wider, within the bound.
No kernel may reach another device: no remote copies, remote signals or barrier semaphores. Data moves between devices by JAX's collectives and lax.ppermute only.
A program may use at most 128 MiB of HBM per device.

```python
import math
import jax
import jax.numpy as jnp
import numpy as np
from jax import lax

D = 8192
R = 64
BLK = 1024
TOK = 128
STEPS = 3
SECTIONS = 16
TOKENS = 2048
DOCS = 32
DOC_MAX = 256
N_DP = 16


def block_levels(rng, shape, cuts, low, top_value):
    def one(axis_at, shards_of):
        heights = jax.random.uniform(jax.random.fold_in(jax.random.fold_in(rng, 6), axis_at), (shards_of,), jnp.float32, low / len(cuts), top_value / len(cuts))
        return jnp.repeat(jnp.exp(heights), shape[axis_at] // shards_of).reshape((-1,) + (1,) * (len(shape) - axis_at - 1))

    factor_of = one(*cuts[0])
    for cut in cuts[1:]:
        factor_of = factor_of * one(*cut)
    return factor_of


def split_up(count, total, limit, slope):
    loads = [(1 << 20) // math.isqrt(grade ** slope) + 1 for grade in range(2, count + 1)]
    spare, given = total - limit - (count - 1), [1] * (count - 1)
    while spare > 0:
        candidates = [i for i in range(count - 1) if given[i] < limit]
        mass, remaining = sum([loads[i] for i in candidates]), spare
        for i in candidates:
            addition = min(limit - given[i], max(1, remaining * loads[i] // mass), spare)
            given[i] = given[i] + addition
            spare = spare - addition
    return np.array([limit] + given)


def ragged(own_key, number_of, total, reach, slope):
    if number_of == 2:
        one = jax.random.randint(own_key, (), max(1, total - reach), min(reach, total - 1) + 1)
        return jnp.stack([one, total - one])
    lengths = jnp.asarray(split_up(number_of, total, reach, slope), jnp.int32)
    pairs = (number_of - 1) // 2
    donor, receiver = lengths[1:1 + 2 * pairs:2], lengths[2:2 + 2 * pairs:2]
    margin = jnp.minimum(donor - 1, reach - receiver)
    moved = jax.random.randint(jax.random.fold_in(own_key, 1), (pairs,), 0, 1 << 20) % (margin + 1)
    lengths = lengths.at[1:1 + 2 * pairs:2].set(donor - moved).at[2:2 + 2 * pairs:2].set(receiver + moved)
    return lengths[jax.random.permutation(jax.random.fold_in(own_key, 2), number_of)]


def bell_draw(key, extent, width, reach, pieces=(), kind=jnp.bfloat16):
    level = block_levels(key, extent, pieces, -0.22, 0.18) if pieces else 1.0
    result = jax.random.normal(key, extent, jnp.float32) * width * level
    return jnp.minimum(jnp.maximum(result, -reach), reach).astype(kind)


def setup_inputs(seed: int = 0) -> dict:
    splits = jax.random.split(jax.random.key(seed), 9)
    entering = bell_draw(splits[0], (SECTIONS, TOKENS, D), 1.0, 6.0, ((0, 16), (1, 16)))
    returning = bell_draw(splits[1], (SECTIONS, TOKENS, D), 1.0, 6.0, ((0, 16), (1, 16)))
    adapter_down = bell_draw(splits[2], (2, SECTIONS, R, D), D ** -0.5, 0.0625, ((1, 16),))
    adapter_up = bell_draw(splits[3], (2, SECTIONS, R, D), R ** -0.5, 0.75, ((1, 16),))
    stashed = bell_draw(splits[4], (SECTIONS, STEPS, R, TOKENS), 1.5, 6.0, ((0, 16), (3, 16)), jnp.float32)
    doc_ids = jax.vmap(lambda own: jnp.searchsorted(jnp.cumsum(ragged(own, DOCS, TOKENS, DOC_MAX, 2)), jnp.arange(TOKENS), side="right"))(jax.random.split(splits[5], SECTIONS)).reshape((SECTIONS, TOKENS)).astype(jnp.int32)
    input_factor = bell_draw(splits[6], (SECTIONS, D, BLK), 0.5, 3.0, ((0, 16), (1, 16)), jnp.float32)
    output_factor = bell_draw(splits[7], (2, SECTIONS, R, R), 0.5, 3.0, ((1, 16),), jnp.float32)
    return {"entering": entering, "returning": returning, "adapter_down": adapter_down, "adapter_up": adapter_up, "stashed": stashed, "doc_ids": doc_ids, "input_factor": input_factor, "output_factor": output_factor}


def layer_apply(current, down_proj, up_proj):
    pre_act = jnp.dot(current, down_proj.T, preferred_element_type=jnp.float32)
    gated = jax.nn.silu(pre_act).astype(jnp.bfloat16)
    mixed = jnp.dot(gated, up_proj, preferred_element_type=jnp.float32)
    return (current.astype(jnp.float32) + mixed).astype(jnp.bfloat16)

def replica_part(carry, replica_rows):
    grouped = replica_rows.astype(jnp.float32).reshape(replica_rows.shape[0], D // BLK, BLK)
    product = jnp.einsum('tki,tkj->kij', grouped, grouped, precision=lax.Precision.HIGHEST)
    rounded = lax.optimization_barrier(product.reshape(D, BLK).astype(jnp.bfloat16))
    return (carry + rounded.astype(jnp.float32), None)

def reference(entering, returning, adapter_down, adapter_up, stashed, doc_ids, input_factor, output_factor):
    section_count = SECTIONS
    doc_range = jnp.arange(DOCS, dtype=jnp.int32)
    onehot = (doc_ids[:, :, None] == doc_range[None, None, :]).astype(jnp.float32)
    counts = lax.optimization_barrier(jnp.sum(onehot, axis=1))
    doc_length = lax.optimization_barrier(jnp.sum(onehot * counts[:, None, :], axis=2))
    weight = jnp.sqrt(TOK / doc_length)
    first = [1 if anchor < section_count // 2 else 0 for anchor in range(section_count)]
    current = [entering[section_idx] for section_idx in range(section_count)]
    row_lists = [[] for section_idx in range(section_count)]
    for step_idx in range(STEPS):
        advanced = []
        for section_idx in range(section_count):
            anchor = (section_idx - step_idx) % section_count
            span_id = first[anchor] + (1 if section_idx < step_idx else 0)
            scaled = jnp.sqrt(weight[anchor])[:, None] * current[section_idx].astype(jnp.float32)
            row_lists[section_idx].append(scaled.astype(jnp.bfloat16))
            if step_idx + 1 < STEPS:
                advanced.append(layer_apply(current[section_idx], adapter_down[span_id, section_idx], adapter_up[span_id, section_idx]))
        if step_idx + 1 < STEPS:
            current = [advanced[(section_idx - 1) % section_count] for section_idx in range(section_count)]
    new_blocks = []
    for section_idx in range(section_count):
        stacked = jnp.stack(row_lists[section_idx])
        held = stacked.shape[0]
        by_replica = jnp.transpose(stacked.reshape(held, N_DP, TOK, D), (1, 0, 2, 3)).reshape(N_DP, held * TOK, D)
        summed, _ = lax.scan(replica_part, jnp.zeros((D, BLK), jnp.float32), by_replica)
        new_blocks.append(0.75 * input_factor[section_idx] + 0.25 * summed / (STEPS * TOKENS))
    input_factor_new = jnp.stack(new_blocks)
    gradient = [returning[section_idx] for section_idx in range(section_count)]
    curv_sums = [[jnp.zeros((R, R), jnp.float32) for section_idx in range(section_count)] for span_idx in range(2)]
    step_counts = [[0 for section_idx in range(section_count)] for span_idx in range(2)]
    for step_idx in range(STEPS):
        passed = []
        for section_idx in range(section_count):
            span_id = 1 if section_idx + step_idx < section_count else 0
            stash_now = stashed[section_idx, step_idx].T
            grad_act = jnp.dot(gradient[section_idx], adapter_up[span_id, section_idx].T, preferred_element_type=jnp.float32)
            sigmoid_z = jax.nn.sigmoid(stash_now)
            grad_pre = (grad_act * sigmoid_z * (1.0 + stash_now * (1.0 - sigmoid_z))).astype(jnp.bfloat16)
            curv_sums[span_id][section_idx] = curv_sums[span_id][section_idx] + jnp.dot(grad_pre.T, grad_pre, preferred_element_type=jnp.float32)
            step_counts[span_id][section_idx] += 1
            if step_idx + 1 < STEPS:
                branch = jnp.dot(grad_pre, adapter_down[span_id, section_idx], preferred_element_type=jnp.float32)
                passed.append((gradient[section_idx].astype(jnp.float32) + branch).astype(jnp.bfloat16))
        if step_idx + 1 < STEPS:
            gradient = [passed[(section_idx + 1) % section_count] for section_idx in range(section_count)]
    span_rows = []
    for span_idx in range(2):
        section_rows = []
        for section_idx in range(section_count):
            held = step_counts[span_idx][section_idx]
            if held > 0:
                section_rows.append(0.75 * output_factor[span_idx, section_idx] + 0.25 * curv_sums[span_idx][section_idx] / (held * TOKENS))
            else:
                section_rows.append(output_factor[span_idx, section_idx])
        span_rows.append(jnp.stack(section_rows))
    output_factor_new = jnp.stack(span_rows)
    return (input_factor_new, output_factor_new)
```

```python
import jax
import jax.numpy as jnp
from jax import lax
from jax.sharding import PartitionSpec as P

F32 = jnp.float32
BF16 = jnp.bfloat16


def shift(block, axis, distance):
    count = lax.axis_size(axis)
    return lax.ppermute(block, axis, [(i, (i + distance) % count) for i in range(count)])


def swap_cores(block):
    count = lax.axis_size("dp")
    return lax.ppermute(block, "dp", [(i, i ^ 1) for i in range(count)])


def gather_dp(block):
    count = lax.axis_size("dp")
    return lax.all_to_all(jnp.broadcast_to(block[None], (count,) + block.shape), "dp", 0, 0)


def pick(weights, span_id):
    return lax.dynamic_index_in_dim(weights[:, 0], span_id, 0, keepdims=False)


def nt(a, b):
    return lax.dot_general(a, b, (((1,), (1,)), ((), ())), preferred_element_type=F32)


def shards(
    entering, returning, adapter_down, adapter_up, stashed, doc_ids, input_factor, output_factor
):
    sec = lax.axis_index("section")
    rep = lax.axis_index("dp")
    sections = lax.axis_size("section")
    replicas = lax.axis_size("dp")
    core = rep % 2
    tok = entering.shape[1]
    width = entering.shape[2]
    steps_count = stashed.shape[1]
    rank = stashed.shape[2]
    block = input_factor.shape[2]
    rows = input_factor.shape[1]
    half = width // 2
    tokens = tok * replicas

    def first(home):
        return (home < sections // 2).astype(jnp.int32)

    x0 = entering[0]
    grad0 = returning[0]

    with jax.named_scope("columns"):
        split = x0.reshape(tok, replicas, rows).transpose(1, 0, 2)
        own = lax.all_to_all(split, "dp", 0, 0).reshape(tokens, rows)
        other = swap_cores(own)

    with jax.named_scope("weights"):
        f_span = first((sec - 1) % sections) + (sec == 0).astype(jnp.int32)
        down_f = lax.dynamic_slice_in_dim(pick(adapter_down, f_span), core * half, half, 1)
        up_f = lax.dynamic_slice_in_dim(pick(adapter_up, f_span), (rep // 2) * block, block, 1)
        ahead = shift(jnp.concatenate([down_f, up_f], axis=1), "section", -1)
        up1_cols = ahead[:, half:]
        b1 = (sec + 1 < sections).astype(jnp.int32)
        b2 = (sec + 2 < sections).astype(jnp.int32)
        up_b1 = lax.dynamic_slice_in_dim(pick(adapter_up, b1), core * half, half, 1)
        down_b1 = lax.dynamic_slice_in_dim(pick(adapter_down, b1), core * half, half, 1)
        up_b2 = lax.dynamic_slice_in_dim(pick(adapter_up, b2), core * half, half, 1)
        behind1 = shift(jnp.concatenate([up_b1, down_b1], axis=0), "section", 1)
        behind2 = shift(up_b2, "section", 2)
        stash1 = shift(stashed[0, 1], "section", 1)
        stash2 = shift(stashed[0, 2], "section", 2)
        ahead_mine = ahead[:, :half]
        ahead_sib = swap_cores(ahead_mine)
        down1_lo = jnp.where(core == 0, ahead_mine, ahead_sib)
        down1_hi = jnp.where(core == 0, ahead_sib, ahead_mine)
        mine = jnp.concatenate([behind1, behind2], axis=0)
        sib = swap_cores(mine)
        back_lo = jnp.where(core == 0, mine, sib)
        back_hi = jnp.where(core == 0, sib, mine)

    with jax.named_scope("gates"):
        c0 = first(sec)
        up0 = pick(adapter_up, c0)
        gate0 = jax.nn.silu(nt(x0, pick(adapter_down, c0))).astype(BF16)
        ids = pick(doc_ids[:, None], sec).astype(BF16)
        sent = jnp.concatenate([gate0, jnp.broadcast_to(ids[:, None], (tok, rank))], axis=1)
        got0 = gather_dp(sent).reshape(tokens, 2 * rank)
        x1 = (x0.astype(F32) + jnp.dot(gate0, up0, preferred_element_type=F32)).astype(BF16)
        z1 = nt(x1[:, :half], down1_lo) + nt(x1[:, half:], down1_hi)
        gate1 = jax.nn.silu(z1).astype(BF16)
        got1 = gather_dp(gate1).reshape(tokens, rank)

    with jax.named_scope("scale"):
        docs = jnp.arange(2 * replicas, dtype=jnp.int32).astype(F32)
        onehot = (got0[:, rank:rank + 1].astype(F32) == docs[None, :]).astype(F32)
        counts = jnp.sum(onehot, axis=0, keepdims=True)
        length = jnp.sum(onehot * counts, axis=1, keepdims=True)
        scale = jnp.sqrt(jnp.sqrt(tok / length))

    with jax.named_scope("grams"):
        up0_cols = lax.dynamic_slice_in_dim(up0, (rep // 2) * block, block, 1)
        lo = jnp.where(core == 0, own, other)
        hi = jnp.where(core == 0, other, own)
        a0 = jnp.concatenate([lo, hi], axis=1)
        g0 = got0[:, :rank]
        a1 = (a0.astype(F32) + jnp.dot(g0, up0_cols, preferred_element_type=F32)).astype(BF16)
        a2 = (a1.astype(F32) + jnp.dot(got1, up1_cols, preferred_element_type=F32)).astype(BF16)

        def gram(act):
            scaled = (scale * act.astype(F32)).astype(BF16)
            mine_cols = lax.dynamic_slice_in_dim(scaled, core * rows, rows, 1)
            return lax.dot_general(
                mine_cols, scaled, (((0,), (0,)), ((), ())), preferred_element_type=F32
            )

        here = gram(a0)
        from1 = shift(gram(a1).astype(BF16), "section", 1).astype(F32)
        from2 = shift(gram(a2).astype(BF16), "section", 2).astype(F32)
        norm_count = steps_count * tokens
        input_factor_new = 0.75 * input_factor + 0.25 * (here + from1 + from2)[None] / norm_count

    with jax.named_scope("backward"):
        b0 = (sec < sections).astype(jnp.int32)
        upb0 = pick(adapter_up, b0)
        downb0 = pick(adapter_down, b0)
        proj0 = nt(upb0, grad0)
        r2 = 2 * rank
        ups_lo = jnp.concatenate([back_lo[:rank], back_lo[r2:]], axis=0)
        ups_hi = jnp.concatenate([back_hi[:rank], back_hi[r2:]], axis=0)
        proj12 = nt(ups_lo, grad0[:, :half]) + nt(ups_hi, grad0[:, half:])
        m0 = nt(ups_lo, downb0[:, :half]) + nt(ups_hi, downb0[:, half:])
        m12 = nt(back_lo[r2:], back_lo[rank:r2]) + nt(back_hi[r2:], back_hi[rank:r2])

        def dz_of(grad_act, q):
            sigma = jax.nn.sigmoid(q)
            return (grad_act * sigma * (1.0 + q * (1.0 - sigma))).astype(BF16)

        def exact(m, d):
            return jnp.dot(m, d.astype(F32), precision=lax.Precision.HIGHEST)

        dz0 = dz_of(proj0, stashed[0, 0])
        dz1 = dz_of(proj12[:rank] + exact(m0[:rank], dz0), stash1)
        dz2 = dz_of(proj12[rank:] + exact(m0[rank:], dz0) + exact(m12, dz1), stash2)
        outer0 = nt(dz0, dz0)
        outer1 = shift(nt(dz1, dz1), "section", -1)
        outer2 = shift(nt(dz2, dz2), "section", -2)
        f1 = b1.astype(F32)
        f2 = b2.astype(F32)
        curv = jnp.stack([outer1 * (1.0 - f1) + outer2 * (1.0 - f2), outer0 + outer1 * f1 + outer2 * f2])
        step_totals = jnp.stack([2.0 - f1 - f2, 1.0 + f1 + f2])
        curv_total = jnp.sum(gather_dp(curv.reshape(rank, 2 * rank)), axis=0).reshape(2, rank, rank)
        divisor = (jnp.maximum(step_totals, 1.0) * tokens)[:, None, None]
        updated = 0.75 * output_factor[:, 0] + 0.25 * curv_total / divisor
        output_factor_new = jnp.where(
            (step_totals > 0.0)[:, None, None], updated, output_factor[:, 0]
        )[:, None]
    return (input_factor_new, output_factor_new)


def solution(mesh):
    in_specs = (
        P("section", "dp", None),
        P("section", "dp", None),
        P(None, "section", None, None),
        P(None, "section", None, None),
        P("section", None, None, "dp"),
        P(None, "dp"),
        P("section", "dp", None),
        P(None, "section", None, None),
    )
    out_specs = (P("section", "dp", None), P(None, "section", None, None))
    return jax.shard_map(shards, mesh=mesh, in_specs=in_specs, out_specs=out_specs, check_vma=False)
```

```python
import functools

import jax
import jax.numpy as jnp
from jax import lax
from jax.experimental import pallas as pl
from jax.experimental.pallas import tpu as pltpu
from jax.sharding import PartitionSpec as P

F32 = jnp.float32
BF16 = jnp.bfloat16


def shift(block, axis, distance):
    count = lax.axis_size(axis)
    return lax.ppermute(block, axis, [(i, (i + distance) % count) for i in range(count)])


def swap_cores(block):
    count = lax.axis_size("dp")
    return lax.ppermute(block, "dp", [(i, i ^ 1) for i in range(count)])


def gather_dp(block):
    count = lax.axis_size("dp")
    return lax.all_to_all(jnp.broadcast_to(block[None], (count,) + block.shape), "dp", 0, 0)


def gather_chips(block):
    chips = lax.axis_size("dp") // 2
    return jnp.stack([block] + [shift(block, "dp", 2 * m) for m in range(1, chips)])


def pick(weights, span_id):
    return lax.dynamic_index_in_dim(weights[:, 0], span_id, 0, keepdims=False)


def nt(a, b):
    return lax.dot_general(a, b, (((1,), (1,)), ((), ())), preferred_element_type=F32)


def tn(a, b):
    return lax.dot_general(a, b, (((0,), (0,)), ((), ())), preferred_element_type=F32)


def gram_kernel(steps, where, own, other, mine, sibs, up0_own, up0_oth, up1_own, up1_oth, table, *rest):
    outs, accs = rest[: len(steps)], rest[len(steps):]
    core = where[1]
    rank = up0_own.shape[2]
    hlf = own.shape[2] // 2
    rows = own.shape[2]

    @pl.when(pl.program_id(0) == 0)
    def _():
        for acc in accs:
            acc[...] = jnp.zeros_like(acc)

    gates = jnp.concatenate([mine[0], sibs[0]], axis=0)
    ids = gates[:, 2 * rank:].astype(F32)
    lane = lax.broadcasted_iota(jnp.int32, ids.shape, 1).astype(F32)
    scale = jnp.sum(jnp.where(ids == lane, table[...], 0.0), axis=1, keepdims=True)
    g0, g1 = gates[:, :rank], gates[:, rank:2 * rank]

    def rebuilt(ref, up0, up1):
        act = jnp.concatenate([ref[core], ref[1 - core]], axis=0)
        acts = [act]
        for gate, up in ((g0, up0), (g1, up1))[: max(steps)]:
            add = jnp.dot(gate, up, preferred_element_type=F32)
            act = (act.astype(F32) + add).astype(BF16)
            acts.append(act)
        return [(scale * acts[j].astype(F32)).astype(BF16) for j in steps]

    r_all = rebuilt(own, up0_own[0, 0], up1_own[...])
    q_all = rebuilt(other, up0_oth[0, 0], up1_oth[...])
    for acc, r, q in zip(accs, r_all, q_all):
        acc[:, :rows] += tn(r[:, :hlf], r)
        acc[:, rows:rows + hlf] += tn(r[:, hlf:], r[:, hlf:])

        @pl.when(core == 0)
        def _():
            acc[:, rows + hlf:] += tn(r[:, :hlf], q)

        @pl.when(core == 1)
        def _():
            acc[:, rows + hlf:] += tn(q[:, hlf:], r)

    @pl.when(pl.program_id(0) == pl.num_programs(0) - 1)
    def _():
        for out, acc in zip(outs, accs):
            out[...] = acc[...].astype(out.dtype)


def grams(steps, dtypes, where, own, other, mine, sibs, adapter_up, up1, table):
    chips, tok, lanes = mine.shape
    rows = own.shape[2]
    rank = adapter_up.shape[2]
    packed = (rows // 2, rows * 5 // 2)
    tokens = own.shape[0] * tok
    one_up = lambda pick_cols: pl.BlockSpec(
        (1, 1, rank, rows), lambda i, w: (w[2], 0, 0, pick_cols(w))
    )
    cols = pl.BlockSpec((2, tok, rows), lambda i, w: (i, 0, 0))
    gate = pl.BlockSpec((1, tok, lanes), lambda i, w: ((w[0] + chips - i) % chips, 0, 0))
    spec = pltpu.PrefetchScalarGridSpec(
        num_scalar_prefetch=1,
        grid=(chips,),
        in_specs=[
            cols,
            cols,
            gate,
            gate,
            one_up(lambda w: 2 * w[0] + w[1]),
            one_up(lambda w: 2 * w[0] + 1 - w[1]),
            pl.BlockSpec((rank, rows), lambda i, w: (0, w[1])),
            pl.BlockSpec((rank, rows), lambda i, w: (0, 1 - w[1])),
            pl.BlockSpec((1, lanes - 2 * rank), lambda i, w: (0, 0)),
        ],
        out_specs=[pl.BlockSpec(packed, lambda i, w: (0, 0)) for _ in steps],
        scratch_shapes=[pltpu.VMEM(packed, F32) for _ in steps],
    )
    return pl.pallas_call(
        functools.partial(gram_kernel, steps),
        grid_spec=spec,
        out_shape=[jax.ShapeDtypeStruct(packed, d) for d in dtypes],
        compiler_params=pltpu.CompilerParams(dimension_semantics=("arbitrary",)),
        cost_estimate=pl.CostEstimate(
            flops=2 * tokens * packed[0] * packed[1] * len(steps),
            transcendentals=0,
            bytes_accessed=2 * own.size * 2,
        ),
    )(where, own, other, mine, sibs, adapter_up, adapter_up, up1, up1, table)


def update_kernel(factor_scale, where, old, here, came, cross, out):
    i = pl.program_id(0)
    core = where[1]
    hlf = out.shape[0]
    rows = 2 * hlf

    def put(lo, hi, val):
        out[:, lo:hi] = 0.75 * old[:, lo:hi] + factor_scale * val

    def packed(lo, hi):
        return here[:, lo:hi] + came[:, lo:hi].astype(F32)

    for c in range(2):
        base = c * rows

        @pl.when(jnp.logical_and(core == c, i == 0))
        def _():
            put(base, base + rows, packed(0, rows))

        @pl.when(jnp.logical_and(core == c, i == 1))
        def _():
            put(base, base + hlf, packed(hlf, rows).T)
            put(base + hlf, base + rows, packed(rows, rows + hlf))

    @pl.when(jnp.logical_and(core == 0, i == 0))
    def _():
        put(rows, 2 * rows, packed(rows + hlf, 2 * rows + hlf))

    @pl.when(jnp.logical_and(core == 0, i == 1))
    def _():
        put(rows, 2 * rows, cross[...])

    for k in range(2):
        a, b = k * hlf, (k + 1) * hlf

        @pl.when(jnp.logical_and(core == 1, i == k))
        def _():
            put(0, hlf, cross[:, a:b].T)
            put(hlf, rows, packed(rows + hlf + a, rows + hlf + b).T)


def update(factor_scale, where, old, here, came, cross):
    total, block = old.shape
    hlf = total // 2
    whole = lambda x: pl.BlockSpec(x.shape, lambda i, w: (0, 0))
    part = pl.BlockSpec((hlf, block), lambda i, w: (i, 0))
    spec = pltpu.PrefetchScalarGridSpec(
        num_scalar_prefetch=1,
        grid=(2,),
        in_specs=[part, whole(here), whole(came), whole(cross)],
        out_specs=part,
    )
    return pl.pallas_call(
        functools.partial(update_kernel, factor_scale),
        grid_spec=spec,
        out_shape=jax.ShapeDtypeStruct(old.shape, F32),
        compiler_params=pltpu.CompilerParams(dimension_semantics=("arbitrary",)),
        cost_estimate=pl.CostEstimate(
            flops=4 * old.size, transcendentals=0, bytes_accessed=12 * old.size
        ),
    )(where, old, here, came, cross)


def shards(
    entering, returning, adapter_down, adapter_up, stashed, doc_ids, input_factor, output_factor
):
    sec = lax.axis_index("section")
    rep = lax.axis_index("dp")
    sections = lax.axis_size("section")
    replicas = lax.axis_size("dp")
    core = rep % 2
    tok = entering.shape[1]
    width = entering.shape[2]
    steps_count = stashed.shape[1]
    rank = stashed.shape[2]
    block = input_factor.shape[2]
    rows = input_factor.shape[1]
    half = width // 2
    tokens = tok * replicas

    def first(home):
        return (home < sections // 2).astype(jnp.int32)

    x0 = entering[0]
    grad0 = returning[0]

    with jax.named_scope("columns"):
        split = x0.reshape(tok, replicas, rows).transpose(1, 0, 2)
        own = lax.all_to_all(split, "dp", 0, 0)
        other = swap_cores(own)

    with jax.named_scope("weights"):
        f_span = first((sec - 1) % sections) + (sec == 0).astype(jnp.int32)
        down_f = lax.dynamic_slice_in_dim(pick(adapter_down, f_span), core * half, half, 1)
        up_f = lax.dynamic_slice_in_dim(pick(adapter_up, f_span), (rep // 2) * block, block, 1)
        ahead = shift(jnp.concatenate([down_f, up_f], axis=1), "section", -1)
        up1_cols = ahead[:, half:]
        b1 = (sec + 1 < sections).astype(jnp.int32)
        b2 = (sec + 2 < sections).astype(jnp.int32)
        up_b1 = lax.dynamic_slice_in_dim(pick(adapter_up, b1), core * half, half, 1)
        down_b1 = lax.dynamic_slice_in_dim(pick(adapter_down, b1), core * half, half, 1)
        up_b2 = lax.dynamic_slice_in_dim(pick(adapter_up, b2), core * half, half, 1)
        behind1 = shift(jnp.concatenate([up_b1, down_b1], axis=0), "section", 1)
        behind2 = shift(up_b2, "section", 2)
        stash1 = shift(stashed[0, 1], "section", 1)
        stash2 = shift(stashed[0, 2], "section", 2)
        ahead_mine = ahead[:, :half]
        ahead_sib = swap_cores(ahead_mine)
        down1_lo = jnp.where(core == 0, ahead_mine, ahead_sib)
        down1_hi = jnp.where(core == 0, ahead_sib, ahead_mine)
        mine = jnp.concatenate([behind1, behind2], axis=0)
        sib = swap_cores(mine)
        back_lo = jnp.where(core == 0, mine, sib)
        back_hi = jnp.where(core == 0, sib, mine)

    with jax.named_scope("gates"):
        c0 = first(sec)
        up0 = pick(adapter_up, c0)
        gate0 = jax.nn.silu(nt(x0, pick(adapter_down, c0))).astype(BF16)
        x1 = (x0.astype(F32) + jnp.dot(gate0, up0, preferred_element_type=F32)).astype(BF16)
        z1 = nt(x1[:, :half], down1_lo) + nt(x1[:, half:], down1_hi)
        gate1 = jax.nn.silu(z1).astype(BF16)
        ids = jnp.broadcast_to(pick(doc_ids[:, None], sec).astype(BF16)[:, None], (tok, 2 * rank))
        gates = gather_chips(jnp.concatenate([gate0, gate1, ids], axis=1))
        gates_sib = swap_cores(gates)

    with jax.named_scope("scale"):
        lane = jnp.arange(2 * rank, dtype=jnp.int32).astype(F32)

        def tally(held):
            return jnp.sum((held[:, :, 2 * rank:].astype(F32) == lane).astype(F32), axis=(0, 1))

        counts = jnp.maximum(tally(gates) + tally(gates_sib), 1.0)
        table = jnp.sqrt(jnp.sqrt(tok / counts))[None]

    with jax.named_scope("factor"):
        where = jnp.stack([rep // 2, core, c0])
        common = (where, own, other, gates, gates_sib, adapter_up, up1_cols, table)
        (step2,) = grams((2,), (BF16,), *common)
        step0, step1 = grams((0, 1), (F32, F32), *common)
        from2 = shift(step2, "section", 1)
        from1 = shift((step1 + from2.astype(F32)).astype(BF16), "section", 1)
        cut = rows + rows // 2
        cross = swap_cores(step0[:, cut:] + from1[:, cut:].astype(F32))
        factor_scale = 0.25 / (steps_count * tokens)
        input_factor_new = update(factor_scale, where, input_factor[0], step0, from1, cross)[None]

    with jax.named_scope("backward"):
        b0 = (sec < sections).astype(jnp.int32)
        upb0 = pick(adapter_up, b0)
        downb0 = pick(adapter_down, b0)
        proj0 = nt(upb0, grad0)
        r2 = 2 * rank
        ups_lo = jnp.concatenate([back_lo[:rank], back_lo[r2:]], axis=0)
        ups_hi = jnp.concatenate([back_hi[:rank], back_hi[r2:]], axis=0)
        proj12 = nt(ups_lo, grad0[:, :half]) + nt(ups_hi, grad0[:, half:])
        m0 = nt(ups_lo, downb0[:, :half]) + nt(ups_hi, downb0[:, half:])
        m12 = nt(back_lo[r2:], back_lo[rank:r2]) + nt(back_hi[r2:], back_hi[rank:r2])

        def dz_of(grad_act, q):
            sigma = jax.nn.sigmoid(q)
            return (grad_act * sigma * (1.0 + q * (1.0 - sigma))).astype(BF16)

        def exact(m, d):
            return jnp.dot(m, d.astype(F32), precision=lax.Precision.HIGHEST)

        dz0 = dz_of(proj0, stashed[0, 0])
        dz1 = dz_of(proj12[:rank] + exact(m0[:rank], dz0), stash1)
        dz2 = dz_of(proj12[rank:] + exact(m0[rank:], dz0) + exact(m12, dz1), stash2)
        outer0 = nt(dz0, dz0)
        outer1 = shift(nt(dz1, dz1), "section", -1)
        outer2 = shift(nt(dz2, dz2), "section", -2)
        f1 = b1.astype(F32)
        f2 = b2.astype(F32)
        curv = jnp.stack([outer1 * (1.0 - f1) + outer2 * (1.0 - f2), outer0 + outer1 * f1 + outer2 * f2])
        step_totals = jnp.stack([2.0 - f1 - f2, 1.0 + f1 + f2])
        curv_total = jnp.sum(gather_dp(curv.reshape(rank, 2 * rank)), axis=0).reshape(2, rank, rank)
        divisor = (jnp.maximum(step_totals, 1.0) * tokens)[:, None, None]
        updated = 0.75 * output_factor[:, 0] + 0.25 * curv_total / divisor
        output_factor_new = jnp.where(
            (step_totals > 0.0)[:, None, None], updated, output_factor[:, 0]
        )[:, None]
    return (input_factor_new, output_factor_new)


def solution(mesh):
    in_specs = (
        P("section", "dp", None),
        P("section", "dp", None),
        P(None, "section", None, None),
        P(None, "section", None, None),
        P("section", None, None, "dp"),
        P(None, "dp"),
        P("section", "dp", None),
        P(None, "section", None, None),
    )
    out_specs = (P("section", "dp", None), P(None, "section", None, None))
    return jax.shard_map(shards, mesh=mesh, in_specs=in_specs, out_specs=out_specs, check_vma=False)
```

```python
import functools

import jax
import jax.numpy as jnp
from jax import lax
from jax.experimental import pallas as pl
from jax.experimental.pallas import tpu as pltpu
from jax.sharding import PartitionSpec as P

F32 = jnp.float32
BF16 = jnp.bfloat16
ANY = pl.BlockSpec(memory_space=pl.ANY)


def shift(block, axis, distance):
    count = lax.axis_size(axis)
    return lax.ppermute(block, axis, [(i, (i + distance) % count) for i in range(count)])


def swap_cores(block):
    count = lax.axis_size("dp")
    return lax.ppermute(block, "dp", [(i, i ^ 1) for i in range(count)])


def nt(a, b):
    return lax.dot_general(a, b, (((1,), (1,)), ((), ())), preferred_element_type=F32)


def tn(a, b):
    return lax.dot_general(a, b, (((0,), (0,)), ((), ())), preferred_element_type=F32)


def call(kernel, where, operands, in_specs, outs, out_specs, grid, scratch, cost, aliases={}):
    spec = pltpu.PrefetchScalarGridSpec(
        num_scalar_prefetch=1,
        grid=grid,
        in_specs=in_specs,
        out_specs=out_specs,
        scratch_shapes=list(scratch),
    )
    flops, moved = cost
    return pl.pallas_call(
        kernel,
        grid_spec=spec,
        out_shape=outs,
        input_output_aliases=aliases,
        compiler_params=pltpu.CompilerParams(dimension_semantics=("arbitrary",) * len(grid)),
        cost_estimate=pl.CostEstimate(flops=flops, transcendentals=0, bytes_accessed=moved),
    )(where, *operands)


def tie_kernel(x, *rest):
    del x, rest


def tie(x, *after):
    hbm = pl.BlockSpec(memory_space=pltpu.HBM)
    return pl.pallas_call(
        tie_kernel,
        in_specs=[hbm] + [ANY] * len(after),
        out_specs=hbm,
        out_shape=jax.ShapeDtypeStruct(x.shape, x.dtype),
        input_output_aliases={0: 0},
        cost_estimate=pl.CostEstimate(flops=0, transcendentals=0, bytes_accessed=0),
    )(x, *after)


CHIP, CORE, SEC, C0, F1, B1, B2 = range(7)


def split_kernel(where, x, down, ids, out, gate, acc):
    i = pl.program_id(0)
    pieces, _, cols = out.shape
    tok, rank = gate.shape

    @pl.when(i == 0)
    def _():
        acc[...] = jnp.zeros_like(acc)

    acc[...] += nt(x[...], down[0, 0])
    row = ids[pl.ds(where[SEC], 1), :].astype(F32)
    row = jnp.broadcast_to(row, (out.shape[1] - tok, tok)).astype(BF16)
    for k in range(pieces):
        out[k, :tok, :] = x[:, k * cols:(k + 1) * cols]
        out[k, tok:, :tok] = row
        out[k, tok:, tok:] = jnp.zeros((out.shape[1] - tok, cols - tok), BF16)

    @pl.when(i == pl.num_programs(0) - 1)
    def _():
        z = acc[...]
        gate[...] = (z * jax.nn.sigmoid(z)).astype(BF16)


def split(where, x, adapter_down, doc_ids, pieces, extra):
    tok, width = x.shape
    rank = adapter_down.shape[2]
    cols = width // pieces
    grid = 4
    each = width // grid
    return call(
        split_kernel,
        where,
        (x, adapter_down, doc_ids),
        [
            pl.BlockSpec((tok, each), lambda i, w: (0, i)),
            pl.BlockSpec((1, 1, rank, each), lambda i, w: (w[C0], 0, 0, i)),
            pl.BlockSpec(doc_ids.shape, lambda i, w: (0, 0)),
        ],
        [
            jax.ShapeDtypeStruct((pieces, tok + extra, cols), BF16),
            jax.ShapeDtypeStruct((tok, rank), BF16),
        ],
        [
            pl.BlockSpec((pieces // grid, tok + extra, cols), lambda i, w: (i, 0, 0)),
            pl.BlockSpec((tok, rank), lambda i, w: (0, 0)),
        ],
        (grid,),
        [pltpu.VMEM((tok, rank), F32)],
        (2 * x.size * rank, 5 * x.size),
    )


def pack_kernel(where, up_f, down_f, up_b1, down_b1, up_b2, after, ahead, behind1, behind2):
    rank, cols = up_f.shape[2:]
    ahead[:, :cols] = up_f[0, 0]
    ahead[:, cols:] = down_f[0, 0]
    behind1[:rank] = up_b1[0, 0]
    behind1[rank:] = down_b1[0, 0]
    behind2[...] = up_b2[0, 0]


def pack(where, adapter_down, adapter_up, block, after):
    rank, width = adapter_down.shape[2:]
    half = width // 2
    part = lambda span: pl.BlockSpec(
        (1, 1, rank, half), lambda i, w: (w[span], 0, 0, w[CORE])
    )
    shapes = ((rank, block + half), (2 * rank, half), (rank, half))
    return call(
        pack_kernel,
        where,
        (adapter_up, adapter_down, adapter_up, adapter_down, adapter_up, after),
        [
            pl.BlockSpec((1, 1, rank, block), lambda i, w: (w[F1], 0, 0, w[CHIP])),
            part(F1),
            part(B1),
            part(B1),
            part(B2),
            ANY,
        ],
        [jax.ShapeDtypeStruct(shape, BF16) for shape in shapes],
        [pl.BlockSpec(shape, lambda i, w: (0, 0)) for shape in shapes],
        (1,),
        (),
        (0, 10 * rank * half * 2),
    )


def gate_kernel(where, xm, xs, um, us, dm, ds, gate0, after1, after2, sent, acc):
    i = pl.program_id(0)
    rank = gate0.shape[1]

    @pl.when(i == 0)
    def _():
        acc[...] = jnp.zeros_like(acc)

    for x, u, d in ((xm, um, dm), (xs, us, ds)):
        add = jnp.dot(gate0[...], u[0, 0], preferred_element_type=F32)
        acc[...] += nt((x[...].astype(F32) + add).astype(BF16), d[...])

    @pl.when(i == pl.num_programs(0) - 1)
    def _():
        z = acc[...]
        gate1 = (z * jax.nn.sigmoid(z)).astype(BF16)
        both = jnp.concatenate([gate0[...], gate1], axis=1)
        for k in range(sent.shape[0]):
            sent[k] = both


def gates(where, x, adapter_up, ahead_mine, ahead_sib, gate0, replicas, *after):
    tok, width = x.shape
    rank = gate0.shape[1]
    each = ahead_mine.shape[1] - width // 2
    grid = width // 2 // each
    x_spec = lambda side: pl.BlockSpec((tok, each), lambda i, w: (0, side(w) * grid + i))
    u_spec = lambda side: pl.BlockSpec(
        (1, 1, rank, each), lambda i, w: (w[C0], 0, 0, side(w) * grid + i)
    )
    mine, sib = (lambda w: w[CORE]), (lambda w: 1 - w[CORE])
    d_spec = pl.BlockSpec((rank, each), lambda i, w: (0, i + 1))
    shape = (replicas, tok, 2 * rank)
    return call(
        gate_kernel,
        where,
        (x, x, adapter_up, adapter_up, ahead_mine, ahead_sib, gate0, *after),
        [
            x_spec(mine),
            x_spec(sib),
            u_spec(mine),
            u_spec(sib),
            d_spec,
            d_spec,
            pl.BlockSpec((tok, rank), lambda i, w: (0, 0)),
            ANY,
            ANY,
        ],
        jax.ShapeDtypeStruct(shape, BF16),
        pl.BlockSpec(shape, lambda i, w: (0, 0, 0)),
        (grid,),
        [pltpu.VMEM((tok, rank), F32)],
        (4 * x.size * rank, 5 * x.size),
    )


def gram_kernel(step, where, own, other, ids, *rest):
    ups, (out, acc) = rest[:-2], rest[-2:]
    core = where[CORE]
    pieces, _, rows = own.shape
    tok = ids.shape[2]
    hlf = rows // 2
    i = pl.program_id(0)

    @pl.when(i == 0)
    def _():
        acc[...] = jnp.zeros_like(acc)

    same = lax.broadcasted_iota(jnp.int32, (tok, tok), 0) == lax.broadcasted_iota(
        jnp.int32, (tok, tok), 1
    )
    everyone = ids[:, 0, :].astype(F32)
    scales = []
    for k in range(pieces):
        mine = own[k, tok:tok + 1, :tok].astype(F32)
        column = jnp.sum(jnp.where(same, mine, 0.0), axis=1, keepdims=True)
        hits = jnp.zeros((tok, tok), F32)
        for m in range(everyone.shape[0]):
            hits += (column == everyone[m:m + 1, :]).astype(F32)
        scales.append(jnp.sqrt(jnp.sqrt(tok / jnp.sum(hits, axis=1, keepdims=True))))
    scale = jnp.concatenate(scales, axis=0)

    def rebuilt(ref, up):
        act = jnp.concatenate([ref[k, :tok, :] for k in range(pieces)], axis=0).astype(F32)
        if step:
            add = jnp.dot(gate, up, preferred_element_type=F32)
            act = (act + add).astype(BF16).astype(F32)
        return (scale * act).astype(BF16)

    if step == 0:
        up_own = up_oth = None
    else:
        got = ups[0]
        gate = jnp.concatenate([got[k] for k in range(pieces)], axis=0)
        if step == 1:
            gate = gate[:, :gate.shape[1] // 2]
            up_own, up_oth = ups[1][0, 0], ups[2][0, 0]
        else:
            up_own = jnp.concatenate([ups[1][0, 0], ups[3][...]], axis=0)
            up_oth = jnp.concatenate([ups[2][0, 0], ups[4][...]], axis=0)
    r = rebuilt(own, up_own)
    q = rebuilt(other, up_oth)
    acc[:, :rows] += tn(r[:, :hlf], r)
    acc[:, rows:rows + hlf] += tn(r[:, hlf:], r[:, hlf:])

    @pl.when(core == 0)
    def _():
        acc[:, rows + hlf:] += tn(r[:, :hlf], q)

    @pl.when(core == 1)
    def _():
        acc[:, rows + hlf:] += tn(q[:, hlf:], r)

    @pl.when(i == pl.num_programs(0) - 1)
    def _():
        out[...] = acc[...].astype(out.dtype)


def gram(step, dtype, where, own, other, got=None, adapter_up=None, up1=None, after=None):
    replicas, long, rows = own.shape
    tok = long - 8
    grid = 4
    pieces = replicas // grid
    packed = (rows // 2, rows * 5 // 2)
    cols = pl.BlockSpec((pieces, long, rows), lambda i, w: (i, 0, 0))
    operands = [own, other, own]
    specs = [cols, cols, pl.BlockSpec((replicas, 8, tok), lambda i, w: (0, tok // 8, 0))]
    if step:
        rank = adapter_up.shape[2]
        up = lambda side: pl.BlockSpec(
            (1, 1, rank, rows), lambda i, w: (w[C0], 0, 0, 2 * w[CHIP] + side(w))
        )
        mine, sib = (lambda w: w[CORE]), (lambda w: 1 - w[CORE])
        operands += [got, adapter_up, adapter_up]
        specs += [pl.BlockSpec((pieces, tok, 2 * rank), lambda i, w: (i, 0, 0)), up(mine), up(sib)]
    if step == 2:
        one = lambda side: pl.BlockSpec((rank, rows), lambda i, w: (0, side(w)))
        operands += [up1, up1]
        specs += [one(mine), one(sib)]
    if after is not None:
        operands.append(after)
        specs.append(ANY)
    return call(
        functools.partial(gram_kernel, step),
        where,
        operands,
        specs,
        jax.ShapeDtypeStruct(packed, dtype),
        pl.BlockSpec(packed, lambda i, w: (0, 0)),
        (grid,),
        [pltpu.VMEM(packed, F32)],
        (2 * replicas * tok * packed[0] * packed[1], 4 * own.size),
    )


def back_kernel(where, gm, gs, um, us, dm, ds, b1m, b1s, b2m, b2s, q0, q1, q2, after, *rest):
    outs, (proj, m0, m12) = rest[:3], rest[3:]
    i = pl.program_id(0)
    rank = b2m.shape[0]

    @pl.when(i == 0)
    def _():
        for acc in (proj, m0, m12):
            acc[...] = jnp.zeros_like(acc)

    for g, u, d, b1, b2 in ((gm, um, dm, b1m, b2m), (gs, us, ds, b1s, b2s)):
        two = jnp.concatenate([b1[:rank], b2[...]], axis=0)
        proj[:rank] += nt(u[0, 0], g[...])
        proj[rank:] += nt(two, g[...])
        m0[...] += nt(two, d[0, 0])
        m12[...] += nt(b2[...], b1[rank:])

    def dz_of(grad_act, q):
        sigma = jax.nn.sigmoid(q)
        return (grad_act * sigma * (1.0 + q * (1.0 - sigma))).astype(BF16)

    def exact(m, d):
        return jnp.dot(
            m, d.astype(F32), precision=lax.Precision.HIGHEST, preferred_element_type=F32
        )

    @pl.when(i == pl.num_programs(0) - 1)
    def _():
        dz0 = dz_of(proj[:rank], q0[0, 0])
        dz1 = dz_of(proj[rank:2 * rank] + exact(m0[:rank], dz0), q1[...])
        dz2 = dz_of(proj[2 * rank:] + exact(m0[rank:], dz0) + exact(m12[...], dz1), q2[...])
        for out, dz in zip(outs, (dz0, dz1, dz2)):
            out[...] = nt(dz, dz)


def back(where, grad, adapter_down, adapter_up, b1, b1s, b2, b2s, stashed, q1, q2, after):
    tok, width = grad.shape
    rank = adapter_up.shape[2]
    grid = 4
    each = width // 2 // grid
    mine, sib = (lambda w: w[CORE]), (lambda w: 1 - w[CORE])
    g_spec = lambda side: pl.BlockSpec((tok, each), lambda i, w: (0, side(w) * grid + i))
    a_spec = lambda side: pl.BlockSpec(
        (1, 1, rank, each), lambda i, w: (1, 0, 0, side(w) * grid + i)
    )
    got = lambda x: pl.BlockSpec((x.shape[0], each), lambda i, w: (0, i))
    q_spec = pl.BlockSpec((rank, tok), lambda i, w: (0, 0))
    return call(
        back_kernel,
        where,
        (
            grad, grad, adapter_up, adapter_up, adapter_down, adapter_down,
            b1, b1s, b2, b2s, stashed, q1, q2, after,
        ),
        [
            g_spec(mine), g_spec(sib), a_spec(mine), a_spec(sib), a_spec(mine), a_spec(sib),
            got(b1), got(b1s), got(b2), got(b2s),
            pl.BlockSpec((1, 1, rank, tok), lambda i, w: (0, 0, 0, 0)), q_spec, q_spec, ANY,
        ],
        [jax.ShapeDtypeStruct((rank, rank), F32)] * 3,
        [pl.BlockSpec((rank, rank), lambda i, w: (0, 0))] * 3,
        (grid,),
        [
            pltpu.VMEM((3 * rank, tok), F32),
            pltpu.VMEM((2 * rank, rank), F32),
            pltpu.VMEM((rank, rank), F32),
        ],
        (12 * grad.size * rank, 8 * grad.size),
    )


def merge_kernel(a, b, after, out):
    out[...] = (a[...] + b[...].astype(F32)).astype(BF16)


def merge(a, b, after):
    grid = 2
    part = pl.BlockSpec((a.shape[0] // grid, a.shape[1]), lambda i: (i, 0))
    return pl.pallas_call(
        merge_kernel,
        grid=(grid,),
        in_specs=[part, part, ANY],
        out_specs=part,
        out_shape=jax.ShapeDtypeStruct(a.shape, BF16),
        compiler_params=pltpu.CompilerParams(dimension_semantics=("arbitrary",)),
        cost_estimate=pl.CostEstimate(flops=a.size, transcendentals=0, bytes_accessed=8 * a.size),
    )(a, b, after)


def square_kernel(factor_scale, where, old, here, came, out):
    i = pl.program_id(0)
    hlf = out.shape[0]
    rows = 2 * hlf

    def put(lo, hi, val):
        out[:, lo:hi] = 0.75 * old[:, lo:hi] + factor_scale * val

    def packed(lo, hi):
        return here[:, lo:hi] + came[:, lo:hi].astype(F32)

    @pl.when(i == 0)
    def _():
        put(0, rows, packed(0, rows))

    @pl.when(i == 1)
    def _():
        put(0, hlf, packed(hlf, rows).T)
        put(hlf, rows, packed(rows, rows + hlf))


def cross_kernel(factor_scale, where, old, mine, sib, done, out):
    i = pl.program_id(0)
    core = where[CORE]
    hlf = out.shape[0]

    def put(lo, hi, val):
        out[:, lo:hi] = 0.75 * old[:, lo:hi] + factor_scale * val

    for k, part in enumerate((mine, sib)):
        @pl.when(jnp.logical_and(core == 0, i == k))
        def _():
            put(0, 2 * hlf, part[...])

    for k in range(2):
        a, b = k * hlf, (k + 1) * hlf

        @pl.when(jnp.logical_and(core == 1, i == k))
        def _():
            put(0, hlf, sib[:, a:b].T)
            put(hlf, 2 * hlf, mine[:, a:b].T)


def update(factor_scale, where, old, here, came, mine, sib):
    total, block = old.shape
    hlf = total // 2
    whole = lambda x: pl.BlockSpec(x.shape, lambda i, w: (0, 0))
    own = pl.BlockSpec((hlf, total), lambda i, w: (i, w[CORE]))
    oth = pl.BlockSpec((hlf, total), lambda i, w: (i, 1 - w[CORE]))
    shape = jax.ShapeDtypeStruct(old.shape, F32)
    cost = (2 * old.size, 6 * old.size)
    done = call(
        functools.partial(square_kernel, factor_scale), where, (old, here, came),
        [own, whole(here), whole(came)], shape, own, (2,), (), cost,
    )
    return call(
        functools.partial(cross_kernel, factor_scale), where, (old, mine, sib, done),
        [oth, whole(mine), whole(sib), ANY], shape, oth, (2,), (), cost, {4: 0},
    )


def shards(
    entering, returning, adapter_down, adapter_up, stashed, doc_ids, input_factor, output_factor
):
    sec = lax.axis_index("section")
    rep = lax.axis_index("dp")
    sections = lax.axis_size("section")
    replicas = lax.axis_size("dp")
    tok = entering.shape[1]
    steps_count = stashed.shape[1]
    rank = stashed.shape[2]
    rows, block = input_factor.shape[1:]
    tokens = tok * replicas

    def first(home):
        return (home < sections // 2).astype(jnp.int32)

    x0 = entering[0]
    f1 = first((sec + sections - 1) % sections) + (sec == 0).astype(jnp.int32)
    b1 = (sec + 1 < sections).astype(jnp.int32)
    b2 = (sec + 2 < sections).astype(jnp.int32)
    where = jnp.stack([rep // 2, rep % 2, sec, first(sec), f1, b1, b2]).astype(jnp.int32)

    with jax.named_scope("weights"):
        pieces, gate0 = split(where, x0, adapter_down, doc_ids, replicas, 8)
        ahead, behind1, behind2 = pack(where, adapter_down, adapter_up, block, gate0)
        ahead = shift(ahead, "section", -1)
        ahead_sib = swap_cores(ahead)
        behind1 = shift(behind1, "section", 1)
        behind2 = shift(behind2, "section", 2)
        stash1 = shift(stashed[0, 1], "section", 1)
        stash2 = shift(stashed[0, 2], "section", 2)
        behind1_sib = swap_cores(behind1)
        behind2_sib = swap_cores(behind2)

    with jax.named_scope("gates"):
        sent = gates(where, x0, adapter_up, ahead, ahead_sib, gate0, replicas, stash1, stash2)

    with jax.named_scope("columns"):
        own = tie(lax.all_to_all(pieces, "dp", 0, 0), sent)
        other = swap_cores(own)
        got = lax.all_to_all(sent, "dp", 0, 0)

    with jax.named_scope("factor"):
        step0 = gram(0, F32, where, own, other)
        step2 = gram(2, BF16, where, own, other, got, adapter_up, ahead, step0)
        from2 = shift(step2, "section", 1)
        step1 = gram(1, F32, where, own, other, got, adapter_up, None, step2)

    with jax.named_scope("backward"):
        outer0, outer1, outer2 = back(
            where, returning[0], adapter_down, adapter_up, behind1, behind1_sib, behind2,
            behind2_sib, stashed, stash1, stash2, step1,
        )

    with jax.named_scope("factor"):
        from1 = shift(merge(step1, from2, outer0), "section", 1)
        cut = rows + rows // 2
        mine = step0[:, cut:] + from1[:, cut:].astype(F32)
        sib = swap_cores(mine)
        factor_scale = 0.25 / (steps_count * tokens)
        input_factor_new = update(
            factor_scale, where, input_factor[0], step0, from1, mine, sib
        )[None]

    with jax.named_scope("backward"):
        outer1 = shift(outer1, "section", -1)
        outer2 = shift(outer2, "section", -2)
        g1 = b1.astype(F32)
        g2 = b2.astype(F32)
        curv = jnp.concatenate(
            [
                outer1 * (1.0 - g1) + outer2 * (1.0 - g2),
                outer0 + outer1 * g1 + outer2 * g2,
            ],
            axis=1,
        )
        curv_all = lax.all_to_all(
            jnp.broadcast_to(curv[None], (replicas,) + curv.shape), "dp", 0, 0
        )
        curv_total = jnp.sum(curv_all, axis=0)
        curv_total = jnp.stack([curv_total[:, :rank], curv_total[:, rank:]])
        step_totals = jnp.stack([2.0 - g1 - g2, 1.0 + g1 + g2])
        divisor = (jnp.maximum(step_totals, 1.0) * tokens)[:, None, None]
        updated = 0.75 * output_factor[:, 0] + 0.25 * curv_total / divisor
        output_factor_new = jnp.where(
            (step_totals > 0.0)[:, None, None], updated, output_factor[:, 0]
        )[:, None]
    return (input_factor_new, output_factor_new)


def solution(mesh):
    in_specs = (
        P("section", "dp", None),
        P("section", "dp", None),
        P(None, "section", None, None),
        P(None, "section", None, None),
        P("section", None, None, "dp"),
        P(None, "dp"),
        P("section", "dp", None),
        P(None, "section", None, None),
    )
    out_specs = (P("section", "dp", None), P(None, "section", None, None))
    return jax.shard_map(shards, mesh=mesh, in_specs=in_specs, out_specs=out_specs, check_vma=False)
```

```python
import functools

import jax
import jax.numpy as jnp
from jax import lax
from jax.experimental import pallas as pl
from jax.experimental.pallas import tpu as pltpu
from jax.sharding import PartitionSpec as P

F32 = jnp.float32
BF16 = jnp.bfloat16
ANY = pl.BlockSpec(memory_space=pl.ANY)


def shift(block, axis, distance):
    count = lax.axis_size(axis)
    return lax.ppermute(block, axis, [(i, (i + distance) % count) for i in range(count)])


def swap_cores(block):
    count = lax.axis_size("dp")
    return lax.ppermute(block, "dp", [(i, i ^ 1) for i in range(count)])


def nt(a, b):
    return lax.dot_general(a, b, (((1,), (1,)), ((), ())), preferred_element_type=F32)


def tn(a, b):
    return lax.dot_general(a, b, (((0,), (0,)), ((), ())), preferred_element_type=F32)


def call(kernel, where, operands, in_specs, outs, out_specs, grid, scratch, cost, aliases={}):
    spec = pltpu.PrefetchScalarGridSpec(
        num_scalar_prefetch=1,
        grid=grid,
        in_specs=in_specs,
        out_specs=out_specs,
        scratch_shapes=list(scratch),
    )
    flops, moved = cost
    return pl.pallas_call(
        kernel,
        grid_spec=spec,
        out_shape=outs,
        input_output_aliases=aliases,
        compiler_params=pltpu.CompilerParams(dimension_semantics=("arbitrary",) * len(grid)),
        cost_estimate=pl.CostEstimate(flops=flops, transcendentals=0, bytes_accessed=moved),
    )(where, *operands)


def tie_kernel(x, *rest):
    del x, rest


def tie(x, *after, space=pltpu.HBM):
    spec = pl.BlockSpec(memory_space=space)
    return pl.pallas_call(
        tie_kernel,
        in_specs=[spec] + [ANY] * len(after),
        out_specs=spec,
        out_shape=jax.ShapeDtypeStruct(x.shape, x.dtype),
        input_output_aliases={0: 0},
        compiler_params=pltpu.CompilerParams(vmem_limit_bytes=8 << 20),
        cost_estimate=pl.CostEstimate(flops=0, transcendentals=0, bytes_accessed=0),
    )(x, *after)


CHIP, CORE, SEC, C0, F1, B1, B2 = range(7)


def split_kernel(where, x, down, ids, after, out, gate, acc):
    i = pl.program_id(0)
    pieces, _, cols = out.shape
    tok, rank = gate.shape

    @pl.when(i == 0)
    def _():
        acc[...] = jnp.zeros_like(acc)

    acc[...] += nt(x[...], down[0, 0])
    row = ids[pl.ds(where[SEC], 1), :].astype(F32)
    row = jnp.broadcast_to(row, (out.shape[1] - tok, tok)).astype(BF16)
    for k in range(pieces):
        out[k, :tok, :] = x[:, k * cols:(k + 1) * cols]
        out[k, tok:, :tok] = row
        out[k, tok:, tok:] = jnp.zeros((out.shape[1] - tok, cols - tok), BF16)

    @pl.when(i == pl.num_programs(0) - 1)
    def _():
        z = acc[...]
        gate[...] = (z * jax.nn.sigmoid(z)).astype(BF16)


def split(where, x, adapter_down, doc_ids, pieces, extra, after):
    tok, width = x.shape
    rank = adapter_down.shape[2]
    cols = width // pieces
    grid = 4
    each = width // grid
    return call(
        split_kernel,
        where,
        (x, adapter_down, doc_ids, after),
        [
            pl.BlockSpec((tok, each), lambda i, w: (0, i)),
            pl.BlockSpec((1, 1, rank, each), lambda i, w: (w[C0], 0, 0, i)),
            pl.BlockSpec(doc_ids.shape, lambda i, w: (0, 0)),
            ANY,
        ],
        [
            jax.ShapeDtypeStruct((pieces, tok + extra, cols), BF16),
            jax.ShapeDtypeStruct((tok, rank), BF16),
        ],
        [
            pl.BlockSpec((pieces // grid, tok + extra, cols), lambda i, w: (i, 0, 0)),
            pl.BlockSpec((tok, rank), lambda i, w: (0, 0)),
        ],
        (grid,),
        [pltpu.VMEM((tok, rank), F32)],
        (2 * x.size * rank, 5 * x.size),
    )


def pack_kernel(where, up_f, down_f, up_b1, up_b2, ahead, behind1, behind2):
    cols = up_f.shape[3]
    ahead[:, :cols] = up_f[0, 0]
    ahead[:, cols:] = down_f[0, 0]
    behind1[...] = up_b1[0, 0]
    behind2[...] = up_b2[0, 0]


def pack(where, adapter_down, adapter_up, block):
    rank, width = adapter_down.shape[2:]
    half = width // 2
    part = lambda span: pl.BlockSpec((1, 1, rank, half), lambda i, w: (w[span], 0, 0, w[CORE]))
    shapes = ((rank, block + half), (rank, half), (rank, half))
    return call(
        pack_kernel,
        where,
        (adapter_up, adapter_down, adapter_up, adapter_up),
        [
            pl.BlockSpec((1, 1, rank, block), lambda i, w: (w[F1], 0, 0, w[CHIP])),
            part(F1),
            part(B1),
            part(B2),
        ],
        [jax.ShapeDtypeStruct(shape, BF16) for shape in shapes],
        [pl.BlockSpec(shape, lambda i, w: (0, 0)) for shape in shapes],
        (1,),
        (),
        (0, 8 * rank * half * 2),
    )


def gate_kernel(
    where, xm, xs, um, us, dm, ds, gate0, u0o, u0s, u1o, u1s, sent, ups_o, ups_s, acc
):
    i = pl.program_id(0)
    rank = gate0.shape[1]

    @pl.when(i == 0)
    def _():
        acc[...] = jnp.zeros_like(acc)
        for out, zero, one in ((ups_o, u0o, u1o), (ups_s, u0s, u1s)):
            out[:rank] = zero[0, 0]
            out[rank:] = one[...]

    for x, u, d in ((xm, um, dm), (xs, us, ds)):
        add = jnp.dot(gate0[...], u[0, 0], preferred_element_type=F32)
        acc[...] += nt((x[...].astype(F32) + add).astype(BF16), d[...])

    @pl.when(i == pl.num_programs(0) - 1)
    def _():
        z = acc[...]
        gate1 = (z * jax.nn.sigmoid(z)).astype(BF16)
        both = jnp.concatenate([gate0[...], gate1], axis=1)
        for k in range(sent.shape[0]):
            sent[k] = both


def gates(where, x, adapter_up, ahead_mine, ahead_sib, gate0, replicas, rows):
    tok, width = x.shape
    rank = gate0.shape[1]
    each = ahead_mine.shape[1] - width // 2
    grid = width // 2 // each
    mine, sib = (lambda w: w[CORE]), (lambda w: 1 - w[CORE])
    x_spec = lambda side: pl.BlockSpec((tok, each), lambda i, w: (0, side(w) * grid + i))
    u_spec = lambda side: pl.BlockSpec(
        (1, 1, rank, each), lambda i, w: (w[C0], 0, 0, side(w) * grid + i)
    )
    d_spec = pl.BlockSpec((rank, each), lambda i, w: (0, i + 1))
    u0 = lambda side: pl.BlockSpec(
        (1, 1, rank, rows), lambda i, w: (w[C0], 0, 0, 2 * w[CHIP] + side(w))
    )
    u1 = lambda side: pl.BlockSpec((rank, rows), lambda i, w: (0, side(w)))
    shapes = ((replicas, tok, 2 * rank), (2 * rank, rows), (2 * rank, rows))
    return call(
        gate_kernel,
        where,
        (
            x, x, adapter_up, adapter_up, ahead_mine, ahead_sib, gate0,
            adapter_up, adapter_up, ahead_mine, ahead_mine,
        ),
        [
            x_spec(mine), x_spec(sib), u_spec(mine), u_spec(sib), d_spec, d_spec,
            pl.BlockSpec((tok, rank), lambda i, w: (0, 0)),
            u0(mine), u0(sib), u1(mine), u1(sib),
        ],
        [jax.ShapeDtypeStruct(shape, BF16) for shape in shapes],
        [
            pl.BlockSpec(shapes[0], lambda i, w: (0, 0, 0)),
            pl.BlockSpec(shapes[1], lambda i, w: (0, 0)),
            pl.BlockSpec(shapes[2], lambda i, w: (0, 0)),
        ],
        (grid,),
        [pltpu.VMEM((tok, rank), F32)],
        (4 * x.size * rank, 5 * x.size),
    )


def local(kernel, where, operands, outs, scratch=(), after=(), aliases={}, out_specs=None):
    vmem = pl.BlockSpec(memory_space=pltpu.VMEM)
    out_vmem = [vmem] * len(outs) if isinstance(outs, list) else vmem
    return pl.pallas_call(
        kernel,
        in_specs=[pl.BlockSpec(memory_space=pltpu.SMEM)]
        + [vmem] * len(operands)
        + [ANY] * len(after),
        out_specs=out_specs or out_vmem,
        out_shape=outs,
        scratch_shapes=list(scratch),
        input_output_aliases=aliases,
        compiler_params=pltpu.CompilerParams(vmem_limit_bytes=24 << 20),
        cost_estimate=pl.CostEstimate(
            flops=0, transcendentals=0, bytes_accessed=2 * sum(x.size for x in operands)
        ),
    )(where, *operands, *after)


def scale_columns(own, tok):
    replicas = own.shape[0]
    ids = [own[k, tok:tok + 1, :tok].astype(F32) for k in range(replicas)]
    doc = lax.broadcasted_iota(jnp.int32, (2 * replicas, tok), 0).astype(F32)
    hits = jnp.zeros((2 * replicas, tok), F32)
    for row in ids:
        hits += (doc == row).astype(F32)
    count = jnp.maximum(jnp.sum(hits, axis=1, keepdims=True), 1.0)
    table = jnp.sqrt(jnp.sqrt(tok / count))
    scales = [jnp.sum(jnp.where(doc == row, table, 0.0), axis=0, keepdims=True) for row in ids]
    return jnp.concatenate(scales + [jnp.zeros((tok - replicas, tok), F32)], axis=0).T


def gram_kernel(step, where, own, other, *rest):
    if step:
        got, ups_own, ups_oth = rest[:3]
    rest = rest[3 if step else 0:]
    core = where[CORE]
    replicas, long, rows = own.shape
    tok = long - 8
    hlf = rows // 2
    per = 4
    if step == 2:
        out, acc = rest[-2:]
    else:
        out = acc = rest[-1]
    columns = scale_columns(own, tok)

    for i in range(replicas // per):
        ks = range(i * per, (i + 1) * per)

        def rebuilt(ref, ups):
            act = jnp.concatenate([ref[k, :tok, :] for k in ks], axis=0).astype(F32)
            if step:
                rank = ups.shape[0] // 2 * step
                gate = jnp.concatenate([got[k] for k in ks], axis=0)[:, :rank]
                add = jnp.dot(gate, ups[:rank], preferred_element_type=F32)
                act = (act + add).astype(BF16).astype(F32)
            scale = [jnp.broadcast_to(columns[:, k:k + 1], (tok, rows)) for k in ks]
            return (jnp.concatenate(scale, axis=0) * act).astype(BF16)

        def put(lo, hi, val):
            acc[:, lo:hi] = val if i == 0 else acc[:, lo:hi] + val

        r = rebuilt(own, ups_own if step else None)
        q = rebuilt(other, ups_oth if step else None)
        put(0, rows, tn(r[:, :hlf], r))
        put(rows, rows + hlf, tn(r[:, hlf:], r[:, hlf:]))

        @pl.when(core == 0)
        def _():
            put(rows + hlf, 2 * rows + hlf, tn(r[:, :hlf], q))

        @pl.when(core == 1)
        def _():
            put(rows + hlf, 2 * rows + hlf, tn(q[:, hlf:], r))

    if step == 2:
        out[...] = acc[...].astype(BF16)


def gram(step, where, own, other, ups=(), after=()):
    rows = own.shape[2]
    packed = (rows // 2, rows * 5 // 2)
    return local(
        functools.partial(gram_kernel, step),
        where,
        (own, other, *ups),
        jax.ShapeDtypeStruct(packed, BF16 if step == 2 else F32),
        [pltpu.VMEM(packed, F32)] if step == 2 else [],
        after,
    )


def project_kernel(where, *refs):
    ins, stash, (proj, m0, by1, by2) = refs[:16], refs[16], refs[17:]
    i = pl.program_id(0)
    rank = stash.shape[2]

    @pl.when(i == 0)
    def _():
        for acc in (proj, m0, by1, by2):
            acc[...] = jnp.zeros_like(acc)
        by1[:rank] = stash[0, 1]
        by2[:rank] = stash[0, 2]

    for g, u, d, d1, u2, b1, b2, a in (ins[0::2], ins[1::2]):
        two = jnp.concatenate([b1[...], b2[...]], axis=0)
        proj[:rank] += nt(u[0, 0], g[...])
        proj[rank:] += nt(two, g[...])
        m0[...] += nt(two, d[0, 0])
        by1[rank:, :rank] += nt(b1[...], d1[0, 0])
        by2[rank:, :rank] += nt(u2[0, 0], a[...])


def project(where, grad, adapter_down, adapter_up, b1, b1s, b2, b2s, ahead, ahead_sib, stashed):
    tok, width = grad.shape
    rank = adapter_up.shape[2]
    each = ahead.shape[1] - width // 2
    grid = width // 2 // each
    mine, sib = (lambda w: w[CORE]), (lambda w: 1 - w[CORE])

    def half(span, side):
        return pl.BlockSpec(
            (1, 1, rank, each), lambda i, w: (span(w), 0, 0, side(w) * grid + i)
        )

    def weights(span):
        return [half(span, mine), half(span, sib)]

    g_spec = lambda side: pl.BlockSpec((tok, each), lambda i, w: (0, side(w) * grid + i))
    got = lambda skip: pl.BlockSpec((rank, each), lambda i, w: (0, i + skip))
    one = lambda w: 1
    shapes = ((3 * rank, tok), (2 * rank, rank), (2 * rank, tok), (2 * rank, tok))
    return call(
        project_kernel,
        where,
        (
            grad, grad, adapter_up, adapter_up, adapter_down, adapter_down,
            adapter_down, adapter_down, adapter_up, adapter_up,
            b1, b1s, b2, b2s, ahead, ahead_sib, stashed,
        ),
        [g_spec(mine), g_spec(sib)]
        + weights(one)
        + weights(one)
        + weights(lambda w: w[B1])
        + weights(lambda w: w[B2])
        + [got(0)] * 4
        + [got(1)] * 2
        + [pl.BlockSpec(stashed.shape, lambda i, w: (0, 0, 0, 0))],
        [jax.ShapeDtypeStruct(shape, F32) for shape in shapes],
        [pl.BlockSpec(shape, lambda i, w: (0, 0)) for shape in shapes],
        (grid,),
        (),
        (14 * grad.size * rank, 12 * grad.size),
    )


def back_kernel(where, proj, m0, by1, by2, q0, *rest):
    outs = rest[-3:]
    rank = m0.shape[1]

    def dz_of(grad_act, q):
        sigma = jax.nn.sigmoid(q)
        return (grad_act * sigma * (1.0 + q * (1.0 - sigma))).astype(BF16)

    def exact(m, d):
        return jnp.dot(
            m, d.astype(F32), precision=lax.Precision.HIGHEST, preferred_element_type=F32
        )

    m12 = jnp.where(where[SEC] == 0, by2[rank:, :rank], by1[rank:, :rank])
    dz0 = dz_of(proj[:rank], q0[0, 0])
    dz1 = dz_of(proj[rank:2 * rank] + exact(m0[:rank], dz0), by1[:rank])
    dz2 = dz_of(proj[2 * rank:] + exact(m0[rank:], dz0) + exact(m12, dz1), by2[:rank])
    for out, dz in zip(outs, (dz0, dz1, dz2)):
        out[...] = nt(dz, dz)


def back(where, proj, m0, by1, by2, stashed, after):
    rank = m0.shape[1]
    return local(
        back_kernel,
        where,
        (proj, m0, by1, by2, stashed),
        [jax.ShapeDtypeStruct((rank, rank), F32)] * 3,
        (),
        (after,),
    )


def merge_kernel(where, a, b, *rest):
    rest[-1][...] = (a[...] + b[...].astype(F32)).astype(BF16)


def merge(where, a, b, after):
    return local(merge_kernel, where, (a, b), jax.ShapeDtypeStruct(a.shape, BF16), (), after)


def put_rows(factor_scale, old, out, buf, sems, first_col, pieces):
    hlf = buf.shape[0] // 2
    cols = pl.ds(pl.multiple_of(first_col, 2 * hlf), 2 * hlf)
    sent = []
    for i, values in enumerate(pieces):
        rows = pl.ds(i * hlf, hlf)
        at = 0
        for value in values():
            here = slice(at, at + value.shape[1])
            was = old[rows, pl.ds(pl.multiple_of(first_col + at, hlf), value.shape[1])]
            buf[rows, here] = 0.75 * was + factor_scale * value
            at += value.shape[1]
        copy = pltpu.make_async_copy(buf.at[rows], out.at[rows, cols], sems.at[i])
        copy.start()
        sent.append(copy)
    for copy in sent:
        copy.wait()


def square_kernel(factor_scale, where, old, here, came, after, out, buf, sems):
    hlf = here.shape[0]
    rows = 2 * hlf

    def packed(lo, hi):
        return here[:, lo:hi] + came[:, lo:hi].astype(F32)

    put_rows(
        factor_scale, old, out, buf, sems, where[CORE] * rows,
        (
            lambda: [packed(0, hlf), packed(hlf, rows)],
            lambda: [packed(hlf, rows).T, packed(rows, rows + hlf)],
        ),
    )


def cross_kernel(factor_scale, where, old, mine, sib, done, out, buf, sems):
    core = where[CORE]
    hlf, rows = mine.shape

    def put(pieces):
        put_rows(factor_scale, old, out, buf, sems, (1 - core) * rows, pieces)

    @pl.when(core == 0)
    def _():
        put(tuple((lambda part=part: [part[:, :hlf], part[:, hlf:]]) for part in (mine, sib)))

    @pl.when(core == 1)
    def _():
        put(
            tuple(
                (lambda a=a: [sib[:, a:a + hlf].T, mine[:, a:a + hlf].T]) for a in (0, hlf)
            )
        )


def update(factor_scale, where, old, here, came, mine, sib, after):
    total = old.shape[0]
    shape = jax.ShapeDtypeStruct(old.shape, F32)
    scratch = [pltpu.VMEM((total, total), F32), pltpu.SemaphoreType.DMA((2,))]
    done = local(
        functools.partial(square_kernel, factor_scale), where, (old, here, came), shape, scratch,
        (after,), out_specs=ANY,
    )
    return local(
        functools.partial(cross_kernel, factor_scale), where, (old, mine, sib), shape, scratch,
        (done,), {4: 0}, ANY,
    )


def shards(
    entering, returning, adapter_down, adapter_up, stashed, doc_ids, input_factor, output_factor
):
    sec = lax.axis_index("section")
    rep = lax.axis_index("dp")
    sections = lax.axis_size("section")
    replicas = lax.axis_size("dp")
    tok = entering.shape[1]
    steps_count = stashed.shape[1]
    rank = stashed.shape[2]
    rows, block = input_factor.shape[1:]
    tokens = tok * replicas

    def first(home):
        return (home < sections // 2).astype(jnp.int32)

    x0 = entering[0]
    f1 = first((sec + sections - 1) % sections) + (sec == 0).astype(jnp.int32)
    b1 = (sec + 1 < sections).astype(jnp.int32)
    b2 = (sec + 2 < sections).astype(jnp.int32)
    where = jnp.stack([rep // 2, rep % 2, sec, first(sec), f1, b1, b2]).astype(jnp.int32)

    with jax.named_scope("weights"):
        ahead, behind1, behind2 = pack(where, adapter_down, adapter_up, block)
        pieces, gate0 = split(where, x0, adapter_down, doc_ids, replicas, 8, ahead)
        ahead = shift(ahead, "section", -1)
        ahead_sib = swap_cores(ahead)
        behind1 = shift(behind1, "section", 1)
        behind2 = shift(behind2, "section", 2)
        behind1_sib = swap_cores(behind1)
        behind2_sib = swap_cores(behind2)

    with jax.named_scope("gates"):
        sent, ups_own, ups_oth = gates(
            where, x0, adapter_up, ahead, ahead_sib, gate0, replicas, rows
        )
        sent = tie(sent, behind1_sib, behind2_sib)

    with jax.named_scope("columns"):
        own = tie(lax.all_to_all(pieces, "dp", 0, 0), sent, space=pltpu.VMEM)
        other = swap_cores(own)
        got = lax.all_to_all(sent, "dp", 0, 0)

    with jax.named_scope("backward"):
        proj, m0, by1, by2 = project(
            where, returning[0], adapter_down, adapter_up, behind1, behind1_sib, behind2,
            behind2_sib, ahead, ahead_sib, stashed,
        )
        by1 = shift(by1, "section", 1)
        by2 = shift(by2, "section", 2)

    with jax.named_scope("factor"):
        ups = (got, ups_own, ups_oth)
        step0 = gram(0, where, own, other, (), (proj,))
        step2 = gram(2, where, own, other, ups, (step0, by1, by2))
        from2 = shift(step2, "section", 1)

    with jax.named_scope("backward"):
        outer0, outer1, outer2 = back(where, proj, m0, by1, by2, stashed, step2)

        outer1 = shift(outer1, "section", -1)
        outer2 = shift(outer2, "section", -2)

    with jax.named_scope("factor"):
        step1 = gram(1, where, own, other, ups, (outer0,))
        from1 = shift(merge(where, step1, from2, (outer1, outer2)), "section", 1)

    with jax.named_scope("backward"):
        g1 = b1.astype(F32)
        g2 = b2.astype(F32)
        curv = jnp.concatenate(
            [
                outer1 * (1.0 - g1) + outer2 * (1.0 - g2),
                outer0 + outer1 * g1 + outer2 * g2,
            ],
            axis=1,
        )
        curv_all = lax.all_to_all(
            jnp.broadcast_to(curv[None], (replicas,) + curv.shape), "dp", 0, 0
        )

    with jax.named_scope("factor"):
        cut = rows + rows // 2
        mine = step0[:, cut:] + from1[:, cut:].astype(F32)
        sib = swap_cores(mine)
        factor_scale = 0.25 / (steps_count * tokens)
        input_factor_new = update(
            factor_scale, where, input_factor[0], step0, from1, mine, sib, curv_all
        )[None]

    with jax.named_scope("backward"):
        curv_total = jnp.sum(curv_all, axis=0)
        curv_total = jnp.stack([curv_total[:, :rank], curv_total[:, rank:]])
        step_totals = jnp.stack([2.0 - g1 - g2, 1.0 + g1 + g2])
        divisor = (jnp.maximum(step_totals, 1.0) * tokens)[:, None, None]
        updated = 0.75 * output_factor[:, 0] + 0.25 * curv_total / divisor
        output_factor_new = jnp.where(
            (step_totals > 0.0)[:, None, None], updated, output_factor[:, 0]
        )[:, None]
    return (input_factor_new, output_factor_new)


def solution(mesh):
    in_specs = (
        P("section", "dp", None),
        P("section", "dp", None),
        P(None, "section", None, None),
        P(None, "section", None, None),
        P("section", None, None, "dp"),
        P(None, "dp"),
        P("section", "dp", None),
        P(None, "section", None, None),
    )
    out_specs = (P("section", "dp", None), P(None, "section", None, None))
    return jax.shard_map(shards, mesh=mesh, in_specs=in_specs, out_specs=out_specs, check_vma=False)
```

```python
import functools

import jax
import jax.numpy as jnp
from jax import lax
from jax.experimental import pallas as pl
from jax.experimental.pallas import tpu as pltpu
from jax.sharding import PartitionSpec as P

F32 = jnp.float32
BF16 = jnp.bfloat16
ANY = pl.BlockSpec(memory_space=pl.ANY)


def shift(block, axis, distance):
    count = lax.axis_size(axis)
    return lax.ppermute(block, axis, [(i, (i + distance) % count) for i in range(count)])


def swap_cores(block):
    count = lax.axis_size("dp")
    return lax.ppermute(block, "dp", [(i, i ^ 1) for i in range(count)])


def swap_chips(block):
    count = lax.axis_size("dp")
    return lax.ppermute(block, "dp", [(i, i ^ 4) for i in range(count)])


def nt(a, b):
    return lax.dot_general(a, b, (((1,), (1,)), ((), ())), preferred_element_type=F32)


def tn(a, b):
    return lax.dot_general(a, b, (((0,), (0,)), ((), ())), preferred_element_type=F32)


def call(kernel, where, operands, in_specs, outs, out_specs, grid, scratch=(), aliases={}):
    spec = pltpu.PrefetchScalarGridSpec(
        num_scalar_prefetch=1,
        grid=grid,
        in_specs=in_specs,
        out_specs=out_specs,
        scratch_shapes=list(scratch),
    )
    return pl.pallas_call(
        kernel,
        grid_spec=spec,
        out_shape=outs,
        input_output_aliases=aliases,
        compiler_params=pltpu.CompilerParams(dimension_semantics=("arbitrary",) * len(grid)),
        cost_estimate=pl.CostEstimate(flops=0, transcendentals=0, bytes_accessed=0),
    )(where, *operands)


def tie_kernel(x, *rest):
    del x, rest


def tie(x, *after, space=pltpu.HBM):
    spec = pl.BlockSpec(memory_space=space)
    return pl.pallas_call(
        tie_kernel,
        in_specs=[spec] + [ANY] * len(after),
        out_specs=spec,
        out_shape=jax.ShapeDtypeStruct(x.shape, x.dtype),
        input_output_aliases={0: 0},
        compiler_params=pltpu.CompilerParams(vmem_limit_bytes=8 << 20),
        cost_estimate=pl.CostEstimate(flops=0, transcendentals=0, bytes_accessed=0),
    )(x, *after)


CHIP, CORE, SEC, C0, F1, B1, B2, PAIR = range(8)


def split_kernel(where, x, down, ids, out, gate, acc):
    i = pl.program_id(0)
    pieces, _, cols = out.shape
    tok, rank = gate.shape

    @pl.when(i == 0)
    def _():
        acc[...] = jnp.zeros_like(acc)

    acc[...] += nt(x[...], down[0, 0])
    row = ids[pl.ds(where[SEC], 1), :].astype(F32)
    row = jnp.broadcast_to(row, (out.shape[1] - tok, tok)).astype(BF16)
    for k in range(pieces):
        out[k, :tok, :] = x[:, k * cols:(k + 1) * cols]
        out[k, tok:, :tok] = row
        out[k, tok:, tok:] = jnp.zeros((out.shape[1] - tok, cols - tok), BF16)

    @pl.when(i == pl.num_programs(0) - 1)
    def _():
        z = acc[...]
        gate[...] = (z * jax.nn.sigmoid(z)).astype(BF16)


def split(where, x, adapter_down, doc_ids, pieces, extra):
    tok, width = x.shape
    rank = adapter_down.shape[2]
    cols = width // pieces
    grid = 4
    each = width // grid
    return call(
        split_kernel,
        where,
        (x, adapter_down, doc_ids),
        [
            pl.BlockSpec((tok, each), lambda i, w: (0, i)),
            pl.BlockSpec((1, 1, rank, each), lambda i, w: (w[C0], 0, 0, i)),
            pl.BlockSpec(doc_ids.shape, lambda i, w: (0, 0)),
        ],
        [
            jax.ShapeDtypeStruct((pieces, tok + extra, cols), BF16),
            jax.ShapeDtypeStruct((tok, rank), BF16),
        ],
        [
            pl.BlockSpec((pieces // grid, tok + extra, cols), lambda i, w: (i, 0, 0)),
            pl.BlockSpec((tok, rank), lambda i, w: (0, 0)),
        ],
        (grid,),
        [pltpu.VMEM((tok, rank), F32)],
    )


def pack_kernel(where, up_f, down_f, up_b1, up_b2, after, ahead, behind1, behind2):
    cols = up_f.shape[3]
    ahead[:, :cols] = up_f[0, 0]
    ahead[:, cols:] = down_f[0, 0]
    behind1[...] = up_b1[0, 0]
    behind2[...] = up_b2[0, 0]


def pack(where, adapter_down, adapter_up, block, after):
    rank, width = adapter_down.shape[2:]
    half = width // 2
    part = lambda span: pl.BlockSpec(
        (1, 1, rank, half // 2), lambda i, w: (w[span], 0, 0, 2 * w[CORE] + w[PAIR])
    )
    shapes = ((rank, block + half), (rank, half // 2), (rank, half // 2))
    return call(
        pack_kernel,
        where,
        (adapter_up, adapter_down, adapter_up, adapter_up, after),
        [
            pl.BlockSpec((1, 1, rank, block), lambda i, w: (w[F1], 0, 0, w[CHIP])),
            pl.BlockSpec((1, 1, rank, half), lambda i, w: (w[F1], 0, 0, w[CORE])),
            part(B1),
            part(B2),
            pl.BlockSpec(after.shape, lambda i, w: (0, 0)),
        ],
        [jax.ShapeDtypeStruct(shape, BF16) for shape in shapes],
        [pl.BlockSpec(shape, lambda i, w: (0, 0)) for shape in shapes],
        (1,),
    )


def gate_kernel(
    where, xm, xs, um, us, dm, ds, gate0, u0o, u0s, u1o, u1s, after, sent, ups_o, ups_s, acc
):
    i = pl.program_id(0)
    rank = gate0.shape[1]

    @pl.when(i == 0)
    def _():
        acc[...] = jnp.zeros_like(acc)
        for out, zero, one in ((ups_o, u0o, u1o), (ups_s, u0s, u1s)):
            out[:rank] = zero[0, 0]
            out[rank:] = one[...]

    for x, u, d in ((xm, um, dm), (xs, us, ds)):
        add = jnp.dot(gate0[...], u[0, 0], preferred_element_type=F32)
        acc[...] += nt((x[...].astype(F32) + add).astype(BF16), d[...])

    @pl.when(i == pl.num_programs(0) - 1)
    def _():
        z = acc[...]
        gate1 = (z * jax.nn.sigmoid(z)).astype(BF16)
        both = jnp.concatenate([gate0[...], gate1], axis=1)
        for k in range(sent.shape[0]):
            sent[k] = both


def gates(where, x, adapter_up, ahead_mine, ahead_sib, gate0, replicas, rows, after):
    tok, width = x.shape
    rank = gate0.shape[1]
    each = ahead_mine.shape[1] - width // 2
    grid = width // 2 // each
    mine, sib = (lambda w: w[CORE]), (lambda w: 1 - w[CORE])
    x_spec = lambda side: pl.BlockSpec((tok, each), lambda i, w: (0, side(w) * grid + i))
    u_spec = lambda side: pl.BlockSpec(
        (1, 1, rank, each), lambda i, w: (w[C0], 0, 0, side(w) * grid + i)
    )
    d_spec = pl.BlockSpec((rank, each), lambda i, w: (0, i + 1))
    u0 = lambda side: pl.BlockSpec(
        (1, 1, rank, rows), lambda i, w: (w[C0], 0, 0, 2 * w[CHIP] + side(w))
    )
    u1 = lambda side: pl.BlockSpec((rank, rows), lambda i, w: (0, side(w)))
    shapes = ((replicas, tok, 2 * rank), (2 * rank, rows), (2 * rank, rows))
    return call(
        gate_kernel,
        where,
        (
            x, x, adapter_up, adapter_up, ahead_mine, ahead_sib, gate0,
            adapter_up, adapter_up, ahead_mine, ahead_mine, after,
        ),
        [
            x_spec(mine), x_spec(sib), u_spec(mine), u_spec(sib), d_spec, d_spec,
            pl.BlockSpec((tok, rank), lambda i, w: (0, 0)),
            u0(mine), u0(sib), u1(mine), u1(sib),
            pl.BlockSpec((16, 128), lambda i, w: (0, 0)),
        ],
        [jax.ShapeDtypeStruct(shape, BF16) for shape in shapes],
        [
            pl.BlockSpec(shapes[0], lambda i, w: (0, 0, 0)),
            pl.BlockSpec(shapes[1], lambda i, w: (0, 0)),
            pl.BlockSpec(shapes[2], lambda i, w: (0, 0)),
        ],
        (grid,),
        [pltpu.VMEM((tok, rank), F32)],
    )


def local(kernel, where, operands, outs, scratch=(), after=(), aliases={}, out_specs=None):
    vmem = pl.BlockSpec(memory_space=pltpu.VMEM)
    out_vmem = [vmem] * len(outs) if isinstance(outs, list) else vmem
    return pl.pallas_call(
        kernel,
        in_specs=[pl.BlockSpec(memory_space=pltpu.SMEM)]
        + [vmem] * len(operands)
        + [vmem] * len(after),
        out_specs=out_specs or out_vmem,
        out_shape=outs,
        scratch_shapes=list(scratch),
        input_output_aliases=aliases,
        compiler_params=pltpu.CompilerParams(vmem_limit_bytes=24 << 20),
        cost_estimate=pl.CostEstimate(flops=0, transcendentals=0, bytes_accessed=0),
    )(where, *operands, *after)


def join_kernel(where, a, b, out):
    out[:a.shape[0]] = a[...]
    out[a.shape[0]:] = b[...]


def join(where, a, b):
    shape = (a.shape[0] + b.shape[0], a.shape[1])
    return local(join_kernel, where, (a, b), jax.ShapeDtypeStruct(shape, a.dtype))


def scale_columns(own, tok):
    replicas = own.shape[0]
    ids = [own[k, tok:tok + 1, :tok].astype(F32) for k in range(replicas)]
    doc = lax.broadcasted_iota(jnp.int32, (2 * replicas, tok), 0).astype(F32)
    hits = jnp.zeros((2 * replicas, tok), F32)
    for row in ids:
        hits += (doc == row).astype(F32)
    count = jnp.maximum(jnp.sum(hits, axis=1, keepdims=True), 1.0)
    table = jnp.sqrt(jnp.sqrt(tok / count))
    scales = [jnp.sum(jnp.where(doc == row, table, 0.0), axis=0, keepdims=True) for row in ids]
    return jnp.concatenate(scales + [jnp.zeros((tok - replicas, tok), F32)], axis=0).T


def gram_kernel(step, where, own, other, *rest):
    if step:
        got, ups_own, ups_oth = rest[:3]
    rest = rest[3 if step else 0:]
    core = where[CORE]
    replicas, long, rows = own.shape
    tok = long - 8
    hlf = rows // 2
    per = 4
    if step == 2:
        out, token, acc = rest[-3:]
    else:
        acc, token = rest[-2:]
    columns = scale_columns(own, tok)

    for i in range(replicas // per):
        ks = range(i * per, (i + 1) * per)

        def rebuilt(ref, ups):
            act = jnp.concatenate([ref[k, :tok, :] for k in ks], axis=0).astype(F32)
            if step:
                rank = ups.shape[0] // 2 * step
                gate = jnp.concatenate([got[k] for k in ks], axis=0)[:, :rank]
                add = jnp.dot(gate, ups[:rank], preferred_element_type=F32)
                act = (act + add).astype(BF16).astype(F32)
            scale = [jnp.broadcast_to(columns[:, k:k + 1], (tok, rows)) for k in ks]
            return (jnp.concatenate(scale, axis=0) * act).astype(BF16)

        def put(lo, val):
            hi = lo + val.shape[1]
            acc[:, lo:hi] = val if i == 0 else acc[:, lo:hi] + val

        r = rebuilt(own, ups_own if step else None)
        q = rebuilt(other, ups_oth if step else None)
        put(0, tn(r[:, :hlf], r))
        put(rows, tn(r[:, hlf:], r[:, hlf:]))

        @pl.when(core == 0)
        def _():
            put(rows + hlf, tn(r[:, :hlf], q))

        @pl.when(core == 1)
        def _():
            put(rows + hlf, tn(q[:, hlf:], r))

    token[...] = jnp.zeros_like(token)
    if step == 2:
        out[...] = acc[...].astype(BF16)


TOKEN = jax.ShapeDtypeStruct((8, 128), F32)


def gram(step, where, own, other, ups=(), after=()):
    rows = own.shape[2]
    packed = (rows // 2, rows * 5 // 2)
    return local(
        functools.partial(gram_kernel, step),
        where,
        (own, other, *ups),
        [jax.ShapeDtypeStruct(packed, BF16 if step == 2 else F32), TOKEN],
        [pltpu.VMEM(packed, F32)] if step == 2 else [],
        after,
    )


def project_kernel(where, *refs):
    ins, stash, (proj, m0, by1, by2) = refs[:14], refs[14], refs[16:]
    i = pl.program_id(0)
    rank = stash.shape[2]

    @pl.when(i == 0)
    def _():
        for acc in (proj, m0, by1, by2):
            acc[...] = jnp.zeros_like(acc)
        by1[:rank] = stash[0, 1]
        by2[:rank] = stash[0, 2]

    for g, u, d, d1, u2, b, a in (ins[0::2], ins[1::2]):
        two = b[...]
        proj[:rank] += nt(u[0, 0], g[...])
        proj[rank:] += nt(two, g[...])
        m0[...] += nt(two, d[0, 0])
        by1[rank:, :rank] += nt(b[:rank], d1[0, 0])
        by2[rank:, :rank] += nt(u2[0, 0], a[...])


def project(where, grad, adapter_down, adapter_up, b, b_sib, ahead, ahead_sib, stashed, after):
    tok, width = grad.shape
    rank = adapter_up.shape[2]
    each = ahead.shape[1] - width // 2
    grid = width // 2 // each
    mine, sib = (lambda w: w[CORE]), (lambda w: 1 - w[CORE])

    def half(span, side):
        return pl.BlockSpec(
            (1, 1, rank, each), lambda i, w: (span(w), 0, 0, side(w) * grid + i)
        )

    def weights(span):
        return [half(span, mine), half(span, sib)]

    g_spec = lambda side: pl.BlockSpec((tok, each), lambda i, w: (0, side(w) * grid + i))
    got = lambda skip: pl.BlockSpec((rank, each), lambda i, w: (0, i + skip))
    per = grid // 2
    quarter = pl.BlockSpec((2 * rank, each), lambda i, w: ((i // per + w[PAIR]) % 2, i % per))
    one = lambda w: 1
    shapes = ((3 * rank, tok), (2 * rank, rank), (2 * rank, tok), (2 * rank, tok))
    return call(
        project_kernel,
        where,
        (
            grad, grad, adapter_up, adapter_up, adapter_down, adapter_down,
            adapter_down, adapter_down, adapter_up, adapter_up,
            b, b_sib, ahead, ahead_sib, stashed, after,
        ),
        [g_spec(mine), g_spec(sib)]
        + weights(one)
        + weights(one)
        + weights(lambda w: w[B1])
        + weights(lambda w: w[B2])
        + [quarter] * 2
        + [got(1)] * 2
        + [pl.BlockSpec(stashed.shape, lambda i, w: (0, 0, 0, 0))]
        + [pl.BlockSpec(after.shape, lambda i, w: (0, 0))],
        [jax.ShapeDtypeStruct(shape, F32) for shape in shapes],
        [pl.BlockSpec(shape, lambda i, w: (0, 0)) for shape in shapes],
        (grid,),
    )


def back_kernel(where, proj, m0, by1, by2, q0, *rest):
    outs = rest[-3:]
    rank = m0.shape[1]

    def dz_of(grad_act, q):
        sigma = jax.nn.sigmoid(q)
        return (grad_act * sigma * (1.0 + q * (1.0 - sigma))).astype(BF16)

    def exact(m, d):
        return jnp.dot(
            m, d.astype(F32), precision=lax.Precision.HIGHEST, preferred_element_type=F32
        )

    m12 = jnp.where(where[SEC] == 0, by2[rank:, :rank], by1[rank:, :rank])
    dz0 = dz_of(proj[:rank], q0[0, 0])
    dz1 = dz_of(proj[rank:2 * rank] + exact(m0[:rank], dz0), by1[:rank])
    dz2 = dz_of(proj[2 * rank:] + exact(m0[rank:], dz0) + exact(m12, dz1), by2[:rank])
    for out, dz in zip(outs, (dz0, dz1, dz2)):
        out[...] = nt(dz, dz)


def back(where, proj, m0, by1, by2, stashed, after):
    rank = m0.shape[1]
    return local(
        back_kernel,
        where,
        (proj, m0, by1, by2, stashed),
        [jax.ShapeDtypeStruct((rank, rank), F32)] * 3,
        (),
        (after,),
    )


def merge_kernel(where, a, b, after, out, token):
    out[...] = (a[...] + b[...].astype(F32)).astype(BF16)
    token[...] = jnp.zeros_like(token)


def merge(where, a, b, after):
    return local(
        merge_kernel, where, (a, b), [jax.ShapeDtypeStruct(a.shape, BF16), TOKEN], (), (after,)
    )


def curvature_kernel(where, outer0, outer1, outer2, out, token):
    rank = outer0.shape[0]
    f1 = where[B1].astype(F32)
    f2 = where[B2].astype(F32)
    zero = outer1[...] * (1.0 - f1) + outer2[...] * (1.0 - f2)
    one = outer0[...] + outer1[...] * f1 + outer2[...] * f2
    both = jnp.concatenate([zero, one], axis=1)
    for k in range(out.shape[0]):
        out[k] = both
    token[...] = jnp.zeros_like(token)


def curvature(where, outers, replicas):
    rank = outers[0].shape[0]
    return local(
        curvature_kernel, where, outers,
        [jax.ShapeDtypeStruct((replicas, rank, 2 * rank), F32), TOKEN],
    )


def statistics_kernel(tokens, where, old, parts, after, out):
    rank = old.shape[2]
    total = parts[0]
    for k in range(1, parts.shape[0]):
        total = total + parts[k]
    later = where[B1] + where[B2]
    for span, held in enumerate((2 - later, 1 + later)):
        held = jnp.full((rank, rank), held.astype(F32), F32)
        was = old[span, 0]
        share = total[:, span * rank:(span + 1) * rank] / (jnp.maximum(held, 1.0) * tokens)
        out[span, 0] = jnp.where(held > 0.0, 0.75 * was + 0.25 * share, was)


def statistics(where, old, parts, tokens, after):
    return local(
        functools.partial(statistics_kernel, tokens),
        where,
        (old, parts),
        jax.ShapeDtypeStruct(old.shape, F32),
        (),
        (after,),
    )


def put_rows(factor_scale, old, out, buf, sems, first_col, pieces):
    hlf = buf.shape[0] // 2
    cols = pl.ds(pl.multiple_of(first_col, 2 * hlf), 2 * hlf)
    sent = []
    for i, values in enumerate(pieces):
        rows = pl.ds(i * hlf, hlf)
        at = 0
        for value in values():
            here = slice(at, at + value.shape[1])
            was = old[rows, pl.ds(pl.multiple_of(first_col + at, hlf), value.shape[1])]
            buf[rows, here] = 0.75 * was + factor_scale * value
            at += value.shape[1]
        copy = pltpu.make_async_copy(buf.at[rows], out.at[rows, cols], sems.at[i])
        copy.start()
        sent.append(copy)
    for copy in sent:
        copy.wait()


def add_kernel(cut, where, here, came, after, out):
    out[...] = here[:, cut:] + came[:, cut:].astype(F32)


def cross_part(where, here, came, after):
    hlf, width = here.shape
    cut = 3 * hlf
    return local(
        functools.partial(add_kernel, cut), where, (here, came),
        jax.ShapeDtypeStruct((hlf, width - cut), F32), (), (after,),
    )


def square_kernel(factor_scale, where, old, here, came, after, out, buf, sems):
    hlf = here.shape[0]
    rows = 2 * hlf

    def packed(lo, hi):
        return here[:, lo:hi] + came[:, lo:hi].astype(F32)

    put_rows(
        factor_scale, old, out, buf, sems, where[CORE] * rows,
        (
            lambda: [packed(0, hlf), packed(hlf, rows)],
            lambda: [packed(hlf, rows).T, packed(rows, rows + hlf)],
        ),
    )


def cross_kernel(factor_scale, where, old, mine, sib, done, out, token, buf, sems):
    core = where[CORE]
    hlf, rows = mine.shape

    def put(pieces):
        put_rows(factor_scale, old, out, buf, sems, (1 - core) * rows, pieces)

    @pl.when(core == 0)
    def _():
        put(tuple((lambda part=part: [part[:, :hlf], part[:, hlf:]]) for part in (mine, sib)))

    @pl.when(core == 1)
    def _():
        put(
            tuple(
                (lambda a=a: [sib[:, a:a + hlf].T, mine[:, a:a + hlf].T]) for a in (0, hlf)
            )
        )

    token[...] = jnp.zeros_like(token)


def update(factor_scale, where, old, here, came, mine, sib, after):
    total = old.shape[0]
    shape = jax.ShapeDtypeStruct(old.shape, F32)
    scratch = [pltpu.VMEM((total, total), F32), pltpu.SemaphoreType.DMA((2,))]
    vmem = pl.BlockSpec(memory_space=pltpu.VMEM)
    done = local(
        functools.partial(square_kernel, factor_scale), where, (old, here, came), shape, scratch,
        (after,), out_specs=ANY,
    )
    return pl.pallas_call(
        functools.partial(cross_kernel, factor_scale),
        in_specs=[pl.BlockSpec(memory_space=pltpu.SMEM)] + [vmem] * 3 + [ANY],
        out_specs=[ANY, vmem],
        out_shape=[shape, TOKEN],
        scratch_shapes=scratch,
        input_output_aliases={4: 0},
        compiler_params=pltpu.CompilerParams(vmem_limit_bytes=24 << 20),
        cost_estimate=pl.CostEstimate(flops=0, transcendentals=0, bytes_accessed=0),
    )(where, old, mine, sib, done)


def shards(
    entering, returning, adapter_down, adapter_up, stashed, doc_ids, input_factor, output_factor
):
    sec = lax.axis_index("section")
    rep = lax.axis_index("dp")
    sections = lax.axis_size("section")
    replicas = lax.axis_size("dp")
    tok = entering.shape[1]
    steps_count = stashed.shape[1]
    rank = stashed.shape[2]
    rows, block = input_factor.shape[1:]
    tokens = tok * replicas

    def first(home):
        return (home < sections // 2).astype(jnp.int32)

    x0 = entering[0]
    f1 = first((sec + sections - 1) % sections) + (sec == 0).astype(jnp.int32)
    b1 = (sec + 1 < sections).astype(jnp.int32)
    b2 = (sec + 2 < sections).astype(jnp.int32)
    where = jnp.stack(
        [rep // 2, rep % 2, sec, first(sec), f1, b1, b2, rep // 4 % 2]
    ).astype(jnp.int32)

    with jax.named_scope("weights"):
        pieces, gate0 = split(where, x0, adapter_down, doc_ids, replicas, 8)
        ahead, behind1, behind2 = pack(where, adapter_down, adapter_up, block, gate0)
        ahead = shift(ahead, "section", -1)
        ahead_sib = swap_cores(ahead)
        behind = join(
            where, shift(behind1, "section", 1), shift(behind2, "section", 2)
        )
        behind_pair = swap_chips(behind)

    with jax.named_scope("gates"):
        sent, ups_own, ups_oth = gates(
            where, x0, adapter_up, ahead, ahead_sib, gate0, replicas, rows, behind_pair
        )

    with jax.named_scope("columns"):
        own = tie(lax.all_to_all(pieces, "dp", 0, 0), sent, space=pltpu.VMEM)
        other = swap_cores(own)
        got = lax.all_to_all(sent, "dp", 0, 0)

    with jax.named_scope("backward"):
        behind = join(where, behind, behind_pair)
        behind_sib = swap_cores(behind)
        proj, m0, by1, by2 = project(
            where, returning[0], adapter_down, adapter_up, behind, behind_sib, ahead, ahead_sib,
            stashed, gate0,
        )
        by1 = shift(by1, "section", 1)
        by2 = shift(by2, "section", 2)

    with jax.named_scope("factor"):
        ups = (got, ups_own, ups_oth)
        step2, token2 = gram(2, where, own, other, ups, (by1, by2))
        from2 = shift(step2, "section", 1)
        step1, token1 = gram(1, where, own, other, ups, (token2,))

    with jax.named_scope("backward"):
        outer0, outer1, outer2 = back(where, proj, m0, by1, by2, stashed, token1)
        outer1 = shift(outer1, "section", -1)
        outer2 = shift(outer2, "section", -2)
        share, token4 = curvature(where, (outer0, outer1, outer2), replicas)
        shares = lax.all_to_all(share, "dp", 0, 0)

    with jax.named_scope("factor"):
        from1, token3 = merge(where, step1, from2, token4)
        from1 = shift(from1, "section", 1)
        step0, _ = gram(0, where, own, other, (), (token3,))
        mine = cross_part(where, step0, from1, shares)
        sib = swap_cores(mine)
        factor_scale = 0.25 / (steps_count * tokens)
        input_factor_new, last = update(
            factor_scale, where, input_factor[0], step0, from1, mine, sib, shares
        )

    with jax.named_scope("backward"):
        output_factor_new = statistics(where, output_factor, shares, tokens, last)
    return (input_factor_new[None], output_factor_new)


def solution(mesh):
    in_specs = (
        P("section", "dp", None),
        P("section", "dp", None),
        P(None, "section", None, None),
        P(None, "section", None, None),
        P("section", None, None, "dp"),
        P(None, "dp"),
        P("section", "dp", None),
        P(None, "section", None, None),
    )
    out_specs = (P("section", "dp", None), P(None, "section", None, None))
    return jax.shard_map(shards, mesh=mesh, in_specs=in_specs, out_specs=out_specs, check_vma=False)
```

```python
import functools

import jax
import jax.numpy as jnp
from jax import lax
from jax.experimental import pallas as pl
from jax.experimental.pallas import tpu as pltpu
from jax.sharding import PartitionSpec as P

F32 = jnp.float32
BF16 = jnp.bfloat16
ANY = pl.BlockSpec(memory_space=pl.ANY)


def shift(block, axis, distance):
    count = lax.axis_size(axis)
    return lax.ppermute(block, axis, [(i, (i + distance) % count) for i in range(count)])


def swap_cores(block):
    count = lax.axis_size("dp")
    return lax.ppermute(block, "dp", [(i, i ^ 1) for i in range(count)])


def swap_chips(block):
    count = lax.axis_size("dp")
    return lax.ppermute(block, "dp", [(i, i ^ 4) for i in range(count)])


def nt(a, b):
    return lax.dot_general(a, b, (((1,), (1,)), ((), ())), preferred_element_type=F32)


def tn(a, b):
    return lax.dot_general(a, b, (((0,), (0,)), ((), ())), preferred_element_type=F32)


def call(kernel, where, operands, in_specs, outs, out_specs, grid, scratch=(), aliases={}):
    spec = pltpu.PrefetchScalarGridSpec(
        num_scalar_prefetch=1,
        grid=grid,
        in_specs=in_specs,
        out_specs=out_specs,
        scratch_shapes=list(scratch),
    )
    return pl.pallas_call(
        kernel,
        grid_spec=spec,
        out_shape=outs,
        input_output_aliases=aliases,
        compiler_params=pltpu.CompilerParams(dimension_semantics=("arbitrary",) * len(grid)),
        cost_estimate=pl.CostEstimate(flops=0, transcendentals=0, bytes_accessed=0),
    )(where, *operands)


def tie_kernel(x, *rest):
    del x, rest


def tie(x, *after, space=pltpu.HBM):
    spec = pl.BlockSpec(memory_space=space)
    return pl.pallas_call(
        tie_kernel,
        in_specs=[spec] + [ANY] * len(after),
        out_specs=spec,
        out_shape=jax.ShapeDtypeStruct(x.shape, x.dtype),
        input_output_aliases={0: 0},
        compiler_params=pltpu.CompilerParams(vmem_limit_bytes=8 << 20),
        cost_estimate=pl.CostEstimate(flops=0, transcendentals=0, bytes_accessed=0),
    )(x, *after)


CHIP, CORE, SEC, C0, F1, B1, B2, PAIR = range(8)


def split_kernel(where, x, down, ids, out, gate, acc):
    i = pl.program_id(0)
    pieces, _, cols = out.shape
    tok, rank = gate.shape

    @pl.when(i == 0)
    def _():
        acc[...] = jnp.zeros_like(acc)

    acc[...] += nt(x[...], down[0, 0])
    row = ids[pl.ds(where[SEC], 1), :].astype(F32)
    row = jnp.broadcast_to(row, (out.shape[1] - tok, tok)).astype(BF16)
    for k in range(pieces):
        out[k, :tok, :] = x[:, k * cols:(k + 1) * cols]
        out[k, tok:, :tok] = row
        out[k, tok:, tok:] = jnp.zeros((out.shape[1] - tok, cols - tok), BF16)

    @pl.when(i == pl.num_programs(0) - 1)
    def _():
        z = acc[...]
        gate[...] = (z * jax.nn.sigmoid(z)).astype(BF16)


def split(where, x, adapter_down, doc_ids, pieces, extra):
    tok, width = x.shape
    rank = adapter_down.shape[2]
    cols = width // pieces
    grid = 4
    each = width // grid
    return call(
        split_kernel,
        where,
        (x, adapter_down, doc_ids),
        [
            pl.BlockSpec((tok, each), lambda i, w: (0, i)),
            pl.BlockSpec((1, 1, rank, each), lambda i, w: (w[C0], 0, 0, i)),
            pl.BlockSpec(doc_ids.shape, lambda i, w: (0, 0)),
        ],
        [
            jax.ShapeDtypeStruct((pieces, tok + extra, cols), BF16),
            jax.ShapeDtypeStruct((tok, rank), BF16),
        ],
        [
            pl.BlockSpec((pieces // grid, tok + extra, cols), lambda i, w: (i, 0, 0)),
            pl.BlockSpec((tok, rank), lambda i, w: (0, 0)),
        ],
        (grid,),
        [pltpu.VMEM((tok, rank), F32)],
    )


def pack_kernel(where, up_f, down_f, up_b1, up_b2, after, ahead, behind1, behind2):
    cols = up_f.shape[3]
    ahead[:, :cols] = up_f[0, 0]
    ahead[:, cols:] = down_f[0, 0]
    behind1[...] = up_b1[0, 0]
    behind2[...] = up_b2[0, 0]


def pack(where, adapter_down, adapter_up, block, after):
    rank, width = adapter_down.shape[2:]
    half = width // 2
    part = lambda span: pl.BlockSpec(
        (1, 1, rank, half // 2), lambda i, w: (w[span], 0, 0, 2 * w[CORE] + w[PAIR])
    )
    shapes = ((rank, block + half), (rank, half // 2), (rank, half // 2))
    return call(
        pack_kernel,
        where,
        (adapter_up, adapter_down, adapter_up, adapter_up, after),
        [
            pl.BlockSpec((1, 1, rank, block), lambda i, w: (w[F1], 0, 0, w[CHIP])),
            pl.BlockSpec((1, 1, rank, half), lambda i, w: (w[F1], 0, 0, w[CORE])),
            part(B1),
            part(B2),
            pl.BlockSpec(after.shape, lambda i, w: (0, 0)),
        ],
        [jax.ShapeDtypeStruct(shape, BF16) for shape in shapes],
        [pl.BlockSpec(shape, lambda i, w: (0, 0)) for shape in shapes],
        (1,),
    )


def ahead_kernel(where, x, up, gate0, x1):
    add = jnp.dot(gate0[...], up[0, 0], preferred_element_type=F32)
    x1[...] = (x[...].astype(F32) + add).astype(BF16)


def next_activation(where, x, adapter_up, gate0):
    tok, width = x.shape
    rank = gate0.shape[1]
    grid = 4
    each = width // grid
    return call(
        ahead_kernel,
        where,
        (x, adapter_up, gate0),
        [
            pl.BlockSpec((tok, each), lambda i, w: (0, i)),
            pl.BlockSpec((1, 1, rank, each), lambda i, w: (w[C0], 0, 0, i)),
            pl.BlockSpec((tok, rank), lambda i, w: (0, 0)),
        ],
        jax.ShapeDtypeStruct((tok, width), BF16),
        pl.BlockSpec((tok, each), lambda i, w: (0, i)),
        (grid,),
    )


def gate_kernel(where, x1, mine, sib, gate0, sent):
    core = where[CORE]
    half = x1.shape[1] // 2
    skip = mine.shape[1] - half
    z = nt(x1[:, pl.ds(pl.multiple_of(core * half, half), half)], mine[:, skip:])
    z += nt(x1[:, pl.ds(pl.multiple_of((1 - core) * half, half), half)], sib[:, skip:])
    gate1 = (z * jax.nn.sigmoid(z)).astype(BF16)
    both = jnp.concatenate([gate0[...], gate1], axis=1)
    for k in range(sent.shape[0]):
        sent[k] = both


def gates(where, x1, ahead_mine, ahead_sib, gate0, replicas):
    tok, rank = gate0.shape
    return local(
        gate_kernel,
        where,
        (x1, ahead_mine, ahead_sib, gate0),
        jax.ShapeDtypeStruct((replicas, tok, 2 * rank), BF16),
    )


def columns_kernel(where, u0o, u0s, u1o, u1s, after, ups_o, ups_s):
    rank = u1o.shape[0]
    for out, zero, one in ((ups_o, u0o, u1o), (ups_s, u0s, u1s)):
        out[:rank] = zero[0, 0]
        out[rank:] = one[...]


def up_columns(where, adapter_up, ahead, rows, after):
    rank = ahead.shape[0]
    mine, sib = (lambda w: w[CORE]), (lambda w: 1 - w[CORE])
    u0 = lambda side: pl.BlockSpec(
        (1, 1, rank, rows), lambda i, w: (w[C0], 0, 0, 2 * w[CHIP] + side(w))
    )
    u1 = lambda side: pl.BlockSpec((rank, rows), lambda i, w: (0, side(w)))
    out = pl.BlockSpec((2 * rank, rows), lambda i, w: (0, 0))
    return call(
        columns_kernel,
        where,
        (adapter_up, adapter_up, ahead, ahead, after),
        [u0(mine), u0(sib), u1(mine), u1(sib), ANY],
        [jax.ShapeDtypeStruct((2 * rank, rows), BF16)] * 2,
        [out, out],
        (1,),
    )


def local(kernel, where, operands, outs, scratch=(), after=(), aliases={}, out_specs=None):
    vmem = pl.BlockSpec(memory_space=pltpu.VMEM)
    out_vmem = [vmem] * len(outs) if isinstance(outs, list) else vmem
    return pl.pallas_call(
        kernel,
        in_specs=[pl.BlockSpec(memory_space=pltpu.SMEM)]
        + [vmem] * len(operands)
        + [vmem] * len(after),
        out_specs=out_specs or out_vmem,
        out_shape=outs,
        scratch_shapes=list(scratch),
        input_output_aliases=aliases,
        compiler_params=pltpu.CompilerParams(vmem_limit_bytes=24 << 20),
        cost_estimate=pl.CostEstimate(flops=0, transcendentals=0, bytes_accessed=0),
    )(where, *operands, *after)


def join_kernel(where, a, b, *rest):
    out = rest[-1]
    out[:a.shape[0]] = a[...]
    out[a.shape[0]:] = b[...]


def join(where, a, b, after=()):
    shape = (a.shape[0] + b.shape[0], a.shape[1])
    return local(
        join_kernel, where, (a, b), jax.ShapeDtypeStruct(shape, a.dtype), (), after
    )


def scale_columns(own, tok):
    replicas = own.shape[0]
    ids = [own[k, tok:tok + 1, :tok].astype(F32) for k in range(replicas)]
    doc = lax.broadcasted_iota(jnp.int32, (2 * replicas, tok), 0).astype(F32)
    hits = jnp.zeros((2 * replicas, tok), F32)
    for row in ids:
        hits += (doc == row).astype(F32)
    count = jnp.maximum(jnp.sum(hits, axis=1, keepdims=True), 1.0)
    table = jnp.sqrt(jnp.sqrt(tok / count))
    scales = [jnp.sum(jnp.where(doc == row, table, 0.0), axis=0, keepdims=True) for row in ids]
    return jnp.concatenate(scales + [jnp.zeros((tok - replicas, tok), F32)], axis=0).T


def gram_kernel(step, where, own, other, *rest):
    if step:
        got, ups_own, ups_oth = rest[:3]
    rest = rest[3 if step else 0:]
    core = where[CORE]
    replicas, long, rows = own.shape
    tok = long - 8
    hlf = rows // 2
    per = 4
    if step == 2:
        out, token, acc = rest[-3:]
    else:
        acc, token = rest[-2:]
    columns = scale_columns(own, tok)

    for i in range(replicas // per):
        ks = range(i * per, (i + 1) * per)

        def rebuilt(ref, ups):
            act = jnp.concatenate([ref[k, :tok, :] for k in ks], axis=0).astype(F32)
            if step:
                rank = ups.shape[0] // 2 * step
                gate = jnp.concatenate([got[k] for k in ks], axis=0)[:, :rank]
                add = jnp.dot(gate, ups[:rank], preferred_element_type=F32)
                act = (act + add).astype(BF16).astype(F32)
            scale = [jnp.broadcast_to(columns[:, k:k + 1], (tok, rows)) for k in ks]
            return (jnp.concatenate(scale, axis=0) * act).astype(BF16)

        def put(lo, val):
            hi = lo + val.shape[1]
            acc[:, lo:hi] = val if i == 0 else acc[:, lo:hi] + val

        r = rebuilt(own, ups_own if step else None)
        q = rebuilt(other, ups_oth if step else None)
        put(0, tn(r[:, :hlf], r))
        put(rows, tn(r[:, hlf:], r[:, hlf:]))

        @pl.when(core == 0)
        def _():
            put(rows + hlf, tn(r[:, :hlf], q))

        @pl.when(core == 1)
        def _():
            put(rows + hlf, tn(q[:, hlf:], r))

    token[...] = jnp.zeros_like(token)
    if step == 2:
        out[...] = acc[...].astype(BF16)


TOKEN = jax.ShapeDtypeStruct((8, 128), F32)


def gram(step, where, own, other, ups=(), after=()):
    rows = own.shape[2]
    packed = (rows // 2, rows * 5 // 2)
    return local(
        functools.partial(gram_kernel, step),
        where,
        (own, other, *ups),
        [jax.ShapeDtypeStruct(packed, BF16 if step == 2 else F32), TOKEN],
        [pltpu.VMEM(packed, F32)] if step == 2 else [],
        after,
    )


def project_kernel(where, *refs):
    ins, stash, (proj, m0, by1, by2) = refs[:14], refs[14], refs[16:]
    i = pl.program_id(0)
    rank = stash.shape[2]

    @pl.when(i == 0)
    def _():
        for acc in (proj, m0, by1, by2):
            acc[...] = jnp.zeros_like(acc)
        by1[:rank] = stash[0, 1]
        by2[:rank] = stash[0, 2]

    for g, u, d, d1, u2, b, a in (ins[0::2], ins[1::2]):
        two = b[...]
        proj[:rank] += nt(u[0, 0], g[...])
        proj[rank:] += nt(two, g[...])
        m0[...] += nt(two, d[0, 0])
        by1[rank:, :rank] += nt(b[:rank], d1[0, 0])
        by2[rank:, :rank] += nt(u2[0, 0], a[...])


def project(where, grad, adapter_down, adapter_up, b, b_sib, ahead, ahead_sib, stashed, after):
    tok, width = grad.shape
    rank = adapter_up.shape[2]
    each = ahead.shape[1] - width // 2
    grid = width // 2 // each
    mine, sib = (lambda w: w[CORE]), (lambda w: 1 - w[CORE])

    def half(span, side):
        return pl.BlockSpec(
            (1, 1, rank, each), lambda i, w: (span(w), 0, 0, side(w) * grid + i)
        )

    def weights(span):
        return [half(span, mine), half(span, sib)]

    g_spec = lambda side: pl.BlockSpec((tok, each), lambda i, w: (0, side(w) * grid + i))
    got = lambda skip: pl.BlockSpec((rank, each), lambda i, w: (0, i + skip))
    per = grid // 2
    quarter = pl.BlockSpec((2 * rank, each), lambda i, w: ((i // per + w[PAIR]) % 2, i % per))
    one = lambda w: 1
    shapes = ((3 * rank, tok), (2 * rank, rank), (2 * rank, tok), (2 * rank, tok))
    return call(
        project_kernel,
        where,
        (
            grad, grad, adapter_up, adapter_up, adapter_down, adapter_down,
            adapter_down, adapter_down, adapter_up, adapter_up,
            b, b_sib, ahead, ahead_sib, stashed, after,
        ),
        [g_spec(mine), g_spec(sib)]
        + weights(one)
        + weights(one)
        + weights(lambda w: w[B1])
        + weights(lambda w: w[B2])
        + [quarter] * 2
        + [got(1)] * 2
        + [pl.BlockSpec(stashed.shape, lambda i, w: (0, 0, 0, 0))]
        + [pl.BlockSpec(after.shape, lambda i, w: (0, 0))],
        [jax.ShapeDtypeStruct(shape, F32) for shape in shapes],
        [pl.BlockSpec(shape, lambda i, w: (0, 0)) for shape in shapes],
        (grid,),
    )


def back_kernel(where, proj, m0, by1, by2, q0, *rest):
    outs = rest[-3:]
    rank = m0.shape[1]

    def dz_of(grad_act, q):
        sigma = jax.nn.sigmoid(q)
        return (grad_act * sigma * (1.0 + q * (1.0 - sigma))).astype(BF16)

    def exact(m, d):
        return jnp.dot(
            m, d.astype(F32), precision=lax.Precision.HIGHEST, preferred_element_type=F32
        )

    m12 = jnp.where(where[SEC] == 0, by2[rank:, :rank], by1[rank:, :rank])
    dz0 = dz_of(proj[:rank], q0[0, 0])
    dz1 = dz_of(proj[rank:2 * rank] + exact(m0[:rank], dz0), by1[:rank])
    dz2 = dz_of(proj[2 * rank:] + exact(m0[rank:], dz0) + exact(m12, dz1), by2[:rank])
    for out, dz in zip(outs, (dz0, dz1, dz2)):
        out[...] = nt(dz, dz)


def back(where, proj, m0, by1, by2, stashed, after):
    rank = m0.shape[1]
    return local(
        back_kernel,
        where,
        (proj, m0, by1, by2, stashed),
        [jax.ShapeDtypeStruct((rank, rank), F32)] * 3,
        (),
        (after,),
    )


def merge_kernel(where, a, b, after, out, token):
    out[...] = (a[...] + b[...].astype(F32)).astype(BF16)
    token[...] = jnp.zeros_like(token)


def merge(where, a, b, after):
    return local(
        merge_kernel, where, (a, b), [jax.ShapeDtypeStruct(a.shape, BF16), TOKEN], (), (after,)
    )


def curvature_kernel(where, outer0, outer1, outer2, out, token):
    rank = outer0.shape[0]
    f1 = where[B1].astype(F32)
    f2 = where[B2].astype(F32)
    zero = outer1[...] * (1.0 - f1) + outer2[...] * (1.0 - f2)
    one = outer0[...] + outer1[...] * f1 + outer2[...] * f2
    both = jnp.concatenate([zero, one], axis=1)
    for k in range(out.shape[0]):
        out[k] = both
    token[...] = jnp.zeros_like(token)


def curvature(where, outers, replicas):
    rank = outers[0].shape[0]
    return local(
        curvature_kernel, where, outers,
        [jax.ShapeDtypeStruct((replicas, rank, 2 * rank), F32), TOKEN],
    )


def statistics_kernel(tokens, where, old, parts, after, out):
    rank = old.shape[2]
    total = parts[0]
    for k in range(1, parts.shape[0]):
        total = total + parts[k]
    later = where[B1] + where[B2]
    for span, held in enumerate((2 - later, 1 + later)):
        held = jnp.full((rank, rank), held.astype(F32), F32)
        was = old[span, 0]
        share = total[:, span * rank:(span + 1) * rank] / (jnp.maximum(held, 1.0) * tokens)
        out[span, 0] = jnp.where(held > 0.0, 0.75 * was + 0.25 * share, was)


def statistics(where, old, parts, tokens, after):
    return local(
        functools.partial(statistics_kernel, tokens),
        where,
        (old, parts),
        jax.ShapeDtypeStruct(old.shape, F32),
        (),
        (after,),
    )


def put_rows(factor_scale, old, out, buf, sems, first_col, pieces):
    hlf = buf.shape[0] // 2
    cols = pl.ds(pl.multiple_of(first_col, 2 * hlf), 2 * hlf)
    sent = []
    for i, values in enumerate(pieces):
        rows = pl.ds(i * hlf, hlf)
        at = 0
        for value in values():
            here = slice(at, at + value.shape[1])
            was = old[rows, pl.ds(pl.multiple_of(first_col + at, hlf), value.shape[1])]
            buf[rows, here] = 0.75 * was + factor_scale * value
            at += value.shape[1]
        copy = pltpu.make_async_copy(buf.at[rows], out.at[rows, cols], sems.at[i])
        copy.start()
        sent.append(copy)
    for copy in sent:
        copy.wait()


def add_kernel(cut, where, here, came, after, out):
    out[...] = here[:, cut:] + came[:, cut:].astype(F32)


def cross_part(where, here, came, after):
    hlf, width = here.shape
    cut = 3 * hlf
    return local(
        functools.partial(add_kernel, cut), where, (here, came),
        jax.ShapeDtypeStruct((hlf, width - cut), F32), (), (after,),
    )


def square_kernel(factor_scale, where, old, here, came, after, out, buf, sems):
    hlf = here.shape[0]
    rows = 2 * hlf

    def packed(lo, hi):
        return here[:, lo:hi] + came[:, lo:hi].astype(F32)

    put_rows(
        factor_scale, old, out, buf, sems, where[CORE] * rows,
        (
            lambda: [packed(0, hlf), packed(hlf, rows)],
            lambda: [packed(hlf, rows).T, packed(rows, rows + hlf)],
        ),
    )


def cross_kernel(factor_scale, where, old, mine, sib, done, out, token, buf, sems):
    core = where[CORE]
    hlf, rows = mine.shape

    def put(pieces):
        put_rows(factor_scale, old, out, buf, sems, (1 - core) * rows, pieces)

    @pl.when(core == 0)
    def _():
        put(tuple((lambda part=part: [part[:, :hlf], part[:, hlf:]]) for part in (mine, sib)))

    @pl.when(core == 1)
    def _():
        put(
            tuple(
                (lambda a=a: [sib[:, a:a + hlf].T, mine[:, a:a + hlf].T]) for a in (0, hlf)
            )
        )

    token[...] = jnp.zeros_like(token)


def update(factor_scale, where, old, here, came, mine, sib, after):
    total = old.shape[0]
    shape = jax.ShapeDtypeStruct(old.shape, F32)
    scratch = [pltpu.VMEM((total, total), F32), pltpu.SemaphoreType.DMA((2,))]
    vmem = pl.BlockSpec(memory_space=pltpu.VMEM)
    done = local(
        functools.partial(square_kernel, factor_scale), where, (old, here, came), shape, scratch,
        (after,), out_specs=ANY,
    )
    return pl.pallas_call(
        functools.partial(cross_kernel, factor_scale),
        in_specs=[pl.BlockSpec(memory_space=pltpu.SMEM)] + [vmem] * 3 + [ANY],
        out_specs=[ANY, vmem],
        out_shape=[shape, TOKEN],
        scratch_shapes=scratch,
        input_output_aliases={4: 0},
        compiler_params=pltpu.CompilerParams(vmem_limit_bytes=24 << 20),
        cost_estimate=pl.CostEstimate(flops=0, transcendentals=0, bytes_accessed=0),
    )(where, old, mine, sib, done)


def shards(
    entering, returning, adapter_down, adapter_up, stashed, doc_ids, input_factor, output_factor
):
    sec = lax.axis_index("section")
    rep = lax.axis_index("dp")
    sections = lax.axis_size("section")
    replicas = lax.axis_size("dp")
    tok = entering.shape[1]
    steps_count = stashed.shape[1]
    rank = stashed.shape[2]
    rows, block = input_factor.shape[1:]
    tokens = tok * replicas

    def first(home):
        return (home < sections // 2).astype(jnp.int32)

    x0 = entering[0]
    f1 = first((sec + sections - 1) % sections) + (sec == 0).astype(jnp.int32)
    b1 = (sec + 1 < sections).astype(jnp.int32)
    b2 = (sec + 2 < sections).astype(jnp.int32)
    where = jnp.stack(
        [rep // 2, rep % 2, sec, first(sec), f1, b1, b2, rep // 4 % 2]
    ).astype(jnp.int32)

    with jax.named_scope("weights"):
        pieces, gate0 = split(where, x0, adapter_down, doc_ids, replicas, 8)
        ahead, behind1, behind2 = pack(where, adapter_down, adapter_up, block, gate0)
        ahead = shift(ahead, "section", -1)
        behind1 = shift(behind1, "section", 1)
        behind2 = shift(behind2, "section", 2)
        ahead = tie(ahead, behind1, behind2, space=pltpu.VMEM)
        ahead_sib = swap_cores(ahead)
        behind = join(where, behind1, behind2)
        behind_pair = swap_chips(behind)

    with jax.named_scope("gates"):
        x1 = next_activation(where, x0, adapter_up, gate0)
        sent = gates(where, x1, ahead, ahead_sib, gate0, replicas)
        ups_own, ups_oth = up_columns(where, adapter_up, ahead, rows, sent)

    with jax.named_scope("columns"):
        own = tie(lax.all_to_all(pieces, "dp", 0, 0), sent, ups_own, space=pltpu.VMEM)
        other = swap_cores(own)
        got = lax.all_to_all(sent, "dp", 0, 0)

    with jax.named_scope("factor"):
        ups = (got, ups_own, ups_oth)
        step2, token2 = gram(2, where, own, other, ups)
        from2 = shift(step2, "section", 1)
        step1, token1 = gram(1, where, own, other, ups, (token2,))

    with jax.named_scope("backward"):
        behind = join(where, behind, behind_pair, (got,))
        behind_sib = swap_cores(behind)
        proj, m0, by1, by2 = project(
            where, returning[0], adapter_down, adapter_up, behind, behind_sib, ahead, ahead_sib,
            stashed, token1,
        )
        by1 = shift(by1, "section", 1)
        by2 = shift(by2, "section", 2)

    with jax.named_scope("factor"):
        from1, token3 = merge(where, step1, from2, m0)
        from1 = shift(from1, "section", 1)
        step0, token0 = gram(0, where, own, other, (), (token3,))

    with jax.named_scope("backward"):
        outer0, outer1, outer2 = back(where, proj, m0, by1, by2, stashed, token0)
        outer1 = shift(outer1, "section", -1)
        outer2 = shift(outer2, "section", -2)
        share, token4 = curvature(where, (outer0, outer1, outer2), replicas)
        shares = lax.all_to_all(share, "dp", 0, 0)

    with jax.named_scope("factor"):
        mine = cross_part(where, step0, from1, token4)
        sib = swap_cores(mine)
        factor_scale = 0.25 / (steps_count * tokens)
        input_factor_new, last = update(
            factor_scale, where, input_factor[0], step0, from1, mine, sib, token4
        )

    with jax.named_scope("backward"):
        output_factor_new = statistics(where, output_factor, shares, tokens, last)
    return (input_factor_new[None], output_factor_new)


def solution(mesh):
    in_specs = (
        P("section", "dp", None),
        P("section", "dp", None),
        P(None, "section", None, None),
        P(None, "section", None, None),
        P("section", None, None, "dp"),
        P(None, "dp"),
        P("section", "dp", None),
        P(None, "section", None, None),
    )
    out_specs = (P("section", "dp", None), P(None, "section", None, None))
    return jax.shard_map(shards, mesh=mesh, in_specs=in_specs, out_specs=out_specs, check_vma=False)
```

```python
import functools

import jax
import jax.numpy as jnp
from jax import lax
from jax.experimental import pallas as pl
from jax.experimental.pallas import tpu as pltpu
from jax.sharding import PartitionSpec as P

F32 = jnp.float32
BF16 = jnp.bfloat16
ANY = pl.BlockSpec(memory_space=pl.ANY)
TOKEN = jax.ShapeDtypeStruct((8, 128), F32)


def shift(block, axis, distance):
    count = lax.axis_size(axis)
    return lax.ppermute(block, axis, [(i, (i + distance) % count) for i in range(count)])


def swap_cores(block):
    count = lax.axis_size("dp")
    return lax.ppermute(block, "dp", [(i, i ^ 1) for i in range(count)])


def swap_chips(block):
    count = lax.axis_size("dp")
    return lax.ppermute(block, "dp", [(i, i ^ 4) for i in range(count)])


def nt(a, b):
    return lax.dot_general(a, b, (((1,), (1,)), ((), ())), preferred_element_type=F32)


def tn(a, b):
    return lax.dot_general(a, b, (((0,), (0,)), ((), ())), preferred_element_type=F32)


def call(kernel, where, operands, in_specs, outs, out_specs, grid, scratch=(), aliases={}):
    spec = pltpu.PrefetchScalarGridSpec(
        num_scalar_prefetch=1,
        grid=grid,
        in_specs=in_specs,
        out_specs=out_specs,
        scratch_shapes=list(scratch),
    )
    return pl.pallas_call(
        kernel,
        grid_spec=spec,
        out_shape=outs,
        input_output_aliases=aliases,
        compiler_params=pltpu.CompilerParams(dimension_semantics=("arbitrary",) * len(grid)),
        cost_estimate=pl.CostEstimate(flops=0, transcendentals=0, bytes_accessed=0),
    )(where, *operands)


def tie_kernel(x, *rest):
    del x, rest


def tie(x, *after, space=pltpu.HBM):
    spec = pl.BlockSpec(memory_space=space)
    return pl.pallas_call(
        tie_kernel,
        in_specs=[spec] + [ANY] * len(after),
        out_specs=spec,
        out_shape=jax.ShapeDtypeStruct(x.shape, x.dtype),
        input_output_aliases={0: 0},
        compiler_params=pltpu.CompilerParams(vmem_limit_bytes=8 << 20),
        cost_estimate=pl.CostEstimate(flops=0, transcendentals=0, bytes_accessed=0),
    )(x, *after)


CHIP, CORE, SEC, C0, F1, B1, B2, PAIR = range(8)


def split_kernel(where, x, down, ids, out, gate, acc):
    i = pl.program_id(0)
    pieces, _, cols = out.shape
    tok, rank = gate.shape

    @pl.when(i == 0)
    def _():
        acc[...] = jnp.zeros_like(acc)

    acc[...] += nt(x[...], down[0, 0])
    row = ids[pl.ds(where[SEC], 1), :].astype(F32)
    row = jnp.broadcast_to(row, (out.shape[1] - tok, tok)).astype(BF16)
    for k in range(pieces):
        out[k, :tok, :] = x[:, k * cols:(k + 1) * cols]
        out[k, tok:, :tok] = row
        out[k, tok:, tok:] = jnp.zeros((out.shape[1] - tok, cols - tok), BF16)

    @pl.when(i == pl.num_programs(0) - 1)
    def _():
        z = acc[...]
        gate[...] = (z * jax.nn.sigmoid(z)).astype(BF16)


def split(where, x, adapter_down, doc_ids, pieces, extra):
    tok, width = x.shape
    rank = adapter_down.shape[2]
    cols = width // pieces
    grid = 4
    each = width // grid
    return call(
        split_kernel,
        where,
        (x, adapter_down, doc_ids),
        [
            pl.BlockSpec((tok, each), lambda i, w: (0, i)),
            pl.BlockSpec((1, 1, rank, each), lambda i, w: (w[C0], 0, 0, i)),
            pl.BlockSpec(doc_ids.shape, lambda i, w: (0, 0)),
        ],
        [
            jax.ShapeDtypeStruct((pieces, tok + extra, cols), BF16),
            jax.ShapeDtypeStruct((tok, rank), BF16),
        ],
        [
            pl.BlockSpec((pieces // grid, tok + extra, cols), lambda i, w: (i, 0, 0)),
            pl.BlockSpec((tok, rank), lambda i, w: (0, 0)),
        ],
        (grid,),
        [pltpu.VMEM((tok, rank), F32)],
    )


def pack_kernel(where, up_f, down_f, up_b1, up_b2, after, ahead, behind1, behind2):
    cols = up_f.shape[3]
    ahead[:, :cols] = up_f[0, 0]
    ahead[:, cols:] = down_f[0, 0]
    behind1[...] = up_b1[0, 0]
    behind2[...] = up_b2[0, 0]


def pack(where, adapter_down, adapter_up, block, after):
    rank, width = adapter_down.shape[2:]
    half = width // 2
    part = lambda span: pl.BlockSpec(
        (1, 1, rank, half // 2), lambda i, w: (w[span], 0, 0, 2 * w[CORE] + w[PAIR])
    )
    shapes = ((rank, block + half), (rank, half // 2), (rank, half // 2))
    return call(
        pack_kernel,
        where,
        (adapter_up, adapter_down, adapter_up, adapter_up, after),
        [
            pl.BlockSpec((1, 1, rank, block), lambda i, w: (w[F1], 0, 0, w[CHIP])),
            pl.BlockSpec((1, 1, rank, half), lambda i, w: (w[F1], 0, 0, w[CORE])),
            part(B1),
            part(B2),
            pl.BlockSpec(after.shape, lambda i, w: (0, 0)),
        ],
        [jax.ShapeDtypeStruct(shape, BF16) for shape in shapes],
        [pl.BlockSpec(shape, lambda i, w: (0, 0)) for shape in shapes],
        (1,),
    )


def ahead_kernel(where, x, up, gate0, u0o, u0s, x1, own, oth, token):
    add = jnp.dot(gate0[...], up[0, 0], preferred_element_type=F32)
    x1[...] = (x[...].astype(F32) + add).astype(BF16)

    @pl.when(pl.program_id(0) == 0)
    def _():
        own[...] = u0o[0, 0]
        oth[...] = u0s[0, 0]
        token[...] = jnp.zeros_like(token)


def next_activation(where, x, adapter_up, gate0, rows):
    tok, width = x.shape
    rank = gate0.shape[1]
    grid = 4
    each = width // grid
    u0 = lambda side: pl.BlockSpec(
        (1, 1, rank, rows), lambda i, w: (w[C0], 0, 0, 2 * w[CHIP] + side(w))
    )
    one = lambda shape: pl.BlockSpec(shape, lambda i, w: (0, 0))
    return call(
        ahead_kernel,
        where,
        (x, adapter_up, gate0, adapter_up, adapter_up),
        [
            pl.BlockSpec((tok, each), lambda i, w: (0, i)),
            pl.BlockSpec((1, 1, rank, each), lambda i, w: (w[C0], 0, 0, i)),
            one((tok, rank)),
            u0(lambda w: w[CORE]),
            u0(lambda w: 1 - w[CORE]),
        ],
        [
            jax.ShapeDtypeStruct((tok, width), BF16),
            jax.ShapeDtypeStruct((rank, rows), BF16),
            jax.ShapeDtypeStruct((rank, rows), BF16),
            TOKEN,
        ],
        [
            pl.BlockSpec((tok, each), lambda i, w: (0, i)),
            one((rank, rows)),
            one((rank, rows)),
            one(TOKEN.shape),
        ],
        (grid,),
    )


def gate_kernel(where, x1, mine, sib, gate0, sent):
    core = where[CORE]
    half = x1.shape[1] // 2
    skip = mine.shape[1] - half
    z = nt(x1[:, pl.ds(pl.multiple_of(core * half, half), half)], mine[:, skip:])
    z += nt(x1[:, pl.ds(pl.multiple_of((1 - core) * half, half), half)], sib[:, skip:])
    gate1 = (z * jax.nn.sigmoid(z)).astype(BF16)
    both = jnp.concatenate([gate0[...], gate1], axis=1)
    for k in range(sent.shape[0]):
        sent[k] = both


def gates(where, x1, ahead_mine, ahead_sib, gate0, replicas):
    tok, rank = gate0.shape
    return local(
        gate_kernel,
        where,
        (x1, ahead_mine, ahead_sib, gate0),
        jax.ShapeDtypeStruct((replicas, tok, 2 * rank), BF16),
    )


def local(kernel, where, operands, outs, scratch=(), after=(), aliases={}, out_specs=None):
    vmem = pl.BlockSpec(memory_space=pltpu.VMEM)
    out_vmem = [vmem] * len(outs) if isinstance(outs, list) else vmem
    return pl.pallas_call(
        kernel,
        in_specs=[pl.BlockSpec(memory_space=pltpu.SMEM)]
        + [vmem] * len(operands)
        + [vmem] * len(after),
        out_specs=out_specs or out_vmem,
        out_shape=outs,
        scratch_shapes=list(scratch),
        input_output_aliases=aliases,
        compiler_params=pltpu.CompilerParams(vmem_limit_bytes=24 << 20),
        cost_estimate=pl.CostEstimate(flops=0, transcendentals=0, bytes_accessed=0),
    )(where, *operands, *after)


def join_kernel(where, a, b, *rest):
    out = rest[-1]
    out[:a.shape[0]] = a[...]
    out[a.shape[0]:] = b[...]


def join(where, a, b, after=()):
    shape = (a.shape[0] + b.shape[0], a.shape[1])
    return local(
        join_kernel, where, (a, b), jax.ShapeDtypeStruct(shape, a.dtype), (), after
    )


def scale_columns(own, tok):
    replicas = own.shape[0]
    ids = [own[k, tok:tok + 1, :tok].astype(F32) for k in range(replicas)]
    doc = lax.broadcasted_iota(jnp.int32, (2 * replicas, tok), 0).astype(F32)
    hits = jnp.zeros((2 * replicas, tok), F32)
    for row in ids:
        hits += (doc == row).astype(F32)
    count = jnp.maximum(jnp.sum(hits, axis=1, keepdims=True), 1.0)
    table = jnp.sqrt(jnp.sqrt(tok / count))
    scales = [jnp.sum(jnp.where(doc == row, table, 0.0), axis=0, keepdims=True) for row in ids]
    return jnp.concatenate(scales + [jnp.zeros((tok - replicas, tok), F32)], axis=0).T


def gram_kernel(step, where, own, other, *rest):
    core = where[CORE]
    replicas, long, rows = own.shape
    if step:
        got, up_own, up_oth, ahead = rest[:4]
        ups_own, ups_oth = up_own[...], up_oth[...]
    if step == 2:
        one = lambda side: ahead[:, pl.ds(pl.multiple_of(side * rows, rows), rows)]
        ups_own = jnp.concatenate([ups_own, one(core)], axis=0)
        ups_oth = jnp.concatenate([ups_oth, one(1 - core)], axis=0)
    rest = rest[4 if step else 0:]
    tok = long - 8
    hlf = rows // 2
    per = 4
    if step == 2:
        out, token, acc = rest[-3:]
    else:
        acc, token = rest[-2:]
    columns = scale_columns(own, tok)

    for i in range(replicas // per):
        ks = range(i * per, (i + 1) * per)

        def rebuilt(ref, ups):
            act = jnp.concatenate([ref[k, :tok, :] for k in ks], axis=0).astype(F32)
            if step:
                gate = jnp.concatenate([got[k] for k in ks], axis=0)[:, :ups.shape[0]]
                add = jnp.dot(gate, ups, preferred_element_type=F32)
                act = (act + add).astype(BF16).astype(F32)
            scale = [jnp.broadcast_to(columns[:, k:k + 1], (tok, rows)) for k in ks]
            return (jnp.concatenate(scale, axis=0) * act).astype(BF16)

        def put(lo, val):
            hi = lo + val.shape[1]
            acc[:, lo:hi] = val if i == 0 else acc[:, lo:hi] + val

        r = rebuilt(own, ups_own if step else None)
        q = rebuilt(other, ups_oth if step else None)
        put(0, tn(r[:, :hlf], r))
        put(rows, tn(r[:, hlf:], r[:, hlf:]))

        @pl.when(core == 0)
        def _():
            put(rows + hlf, tn(r[:, :hlf], q))

        @pl.when(core == 1)
        def _():
            put(rows + hlf, tn(q[:, hlf:], r))

    token[...] = jnp.zeros_like(token)
    if step == 2:
        out[...] = acc[...].astype(BF16)


def gram(step, where, own, other, ups=(), after=()):
    rows = own.shape[2]
    packed = (rows // 2, rows * 5 // 2)
    return local(
        functools.partial(gram_kernel, step),
        where,
        (own, other, *ups),
        [jax.ShapeDtypeStruct(packed, BF16 if step == 2 else F32), TOKEN],
        [pltpu.VMEM(packed, F32)] if step == 2 else [],
        after,
    )


def project_kernel(where, *refs):
    ins, stash, (proj, m0, by1, by2) = refs[:14], refs[14], refs[16:]
    i = pl.program_id(0)
    rank = stash.shape[2]

    @pl.when(i == 0)
    def _():
        for acc in (proj, m0, by1, by2):
            acc[...] = jnp.zeros_like(acc)
        by1[:rank] = stash[0, 1]
        by2[:rank] = stash[0, 2]

    for g, u, d, d1, u2, b, a in (ins[0::2], ins[1::2]):
        two = b[...]
        proj[:rank] += nt(u[0, 0], g[...])
        proj[rank:] += nt(two, g[...])
        m0[...] += nt(two, d[0, 0])
        by1[rank:, :rank] += nt(b[:rank], d1[0, 0])
        by2[rank:, :rank] += nt(u2[0, 0], a[...])


def project(where, grad, adapter_down, adapter_up, b, b_sib, ahead, ahead_sib, stashed, after):
    tok, width = grad.shape
    rank = adapter_up.shape[2]
    each = ahead.shape[1] - width // 2
    grid = width // 2 // each
    mine, sib = (lambda w: w[CORE]), (lambda w: 1 - w[CORE])

    def half(span, side):
        return pl.BlockSpec(
            (1, 1, rank, each), lambda i, w: (span(w), 0, 0, side(w) * grid + i)
        )

    def weights(span):
        return [half(span, mine), half(span, sib)]

    g_spec = lambda side: pl.BlockSpec((tok, each), lambda i, w: (0, side(w) * grid + i))
    got = lambda skip: pl.BlockSpec((rank, each), lambda i, w: (0, i + skip))
    per = grid // 2
    quarter = pl.BlockSpec((2 * rank, each), lambda i, w: ((i // per + w[PAIR]) % 2, i % per))
    one = lambda w: 1
    shapes = ((3 * rank, tok), (2 * rank, rank), (2 * rank, tok), (2 * rank, tok))
    return call(
        project_kernel,
        where,
        (
            grad, grad, adapter_up, adapter_up, adapter_down, adapter_down,
            adapter_down, adapter_down, adapter_up, adapter_up,
            b, b_sib, ahead, ahead_sib, stashed, after,
        ),
        [g_spec(mine), g_spec(sib)]
        + weights(one)
        + weights(one)
        + weights(lambda w: w[B1])
        + weights(lambda w: w[B2])
        + [quarter] * 2
        + [got(1)] * 2
        + [pl.BlockSpec(stashed.shape, lambda i, w: (0, 0, 0, 0))]
        + [pl.BlockSpec(after.shape, lambda i, w: (0, 0))],
        [jax.ShapeDtypeStruct(shape, F32) for shape in shapes],
        [pl.BlockSpec(shape, lambda i, w: (0, 0)) for shape in shapes],
        (grid,),
    )


def back_kernel(where, proj, m0, by1, by2, q0, *rest):
    outs = rest[-3:]
    rank = m0.shape[1]

    def dz_of(grad_act, q):
        sigma = jax.nn.sigmoid(q)
        return (grad_act * sigma * (1.0 + q * (1.0 - sigma))).astype(BF16)

    def exact(m, d):
        return jnp.dot(
            m, d.astype(F32), precision=lax.Precision.HIGHEST, preferred_element_type=F32
        )

    m12 = jnp.where(where[SEC] == 0, by2[rank:, :rank], by1[rank:, :rank])
    dz0 = dz_of(proj[:rank], q0[0, 0])
    dz1 = dz_of(proj[rank:2 * rank] + exact(m0[:rank], dz0), by1[:rank])
    dz2 = dz_of(proj[2 * rank:] + exact(m0[rank:], dz0) + exact(m12, dz1), by2[:rank])
    for out, dz in zip(outs, (dz0, dz1, dz2)):
        out[...] = nt(dz, dz)


def back(where, proj, m0, by1, by2, stashed, after):
    rank = m0.shape[1]
    return local(
        back_kernel,
        where,
        (proj, m0, by1, by2, stashed),
        [jax.ShapeDtypeStruct((rank, rank), F32)] * 3,
        (),
        (after,),
    )


def merge_kernel(where, a, b, *rest):
    out, token = rest[-2:]
    out[...] = (a[...] + b[...].astype(F32)).astype(BF16)
    token[...] = jnp.zeros_like(token)


def merge(where, a, b, after):
    return local(
        merge_kernel, where, (a, b), [jax.ShapeDtypeStruct(a.shape, BF16), TOKEN], (), after
    )


def curvature_kernel(where, outer0, outer1, outer2, out, token):
    rank = outer0.shape[0]
    f1 = where[B1].astype(F32)
    f2 = where[B2].astype(F32)
    zero = outer1[...] * (1.0 - f1) + outer2[...] * (1.0 - f2)
    one = outer0[...] + outer1[...] * f1 + outer2[...] * f2
    both = jnp.concatenate([zero, one], axis=1)
    for k in range(out.shape[0]):
        out[k] = both
    token[...] = jnp.zeros_like(token)


def curvature(where, outers, replicas):
    rank = outers[0].shape[0]
    return local(
        curvature_kernel, where, outers,
        [jax.ShapeDtypeStruct((replicas, rank, 2 * rank), F32), TOKEN],
    )


def statistics_kernel(tokens, where, old, parts, after, out):
    rank = old.shape[2]
    total = parts[0]
    for k in range(1, parts.shape[0]):
        total = total + parts[k]
    later = where[B1] + where[B2]
    for span, held in enumerate((2 - later, 1 + later)):
        held = jnp.full((rank, rank), held.astype(F32), F32)
        was = old[span, 0]
        share = total[:, span * rank:(span + 1) * rank] / (jnp.maximum(held, 1.0) * tokens)
        out[span, 0] = jnp.where(held > 0.0, 0.75 * was + 0.25 * share, was)


def statistics(where, old, parts, tokens, after):
    return local(
        functools.partial(statistics_kernel, tokens),
        where,
        (old, parts),
        jax.ShapeDtypeStruct(old.shape, F32),
        (),
        (after,),
    )


def put_rows(factor_scale, old, out, buf, sems, first_col, pieces):
    hlf = buf.shape[0] // 2
    cols = pl.ds(pl.multiple_of(first_col, 2 * hlf), 2 * hlf)
    sent = []
    for i, values in enumerate(pieces):
        rows = pl.ds(i * hlf, hlf)
        at = 0
        for value in values():
            here = slice(at, at + value.shape[1])
            was = old[rows, pl.ds(pl.multiple_of(first_col + at, hlf), value.shape[1])]
            buf[rows, here] = 0.75 * was + factor_scale * value
            at += value.shape[1]
        copy = pltpu.make_async_copy(buf.at[rows], out.at[rows, cols], sems.at[i])
        copy.start()
        sent.append(copy)
    for copy in sent:
        copy.wait()


def add_kernel(cut, where, here, came, after, out):
    out[...] = here[:, cut:] + came[:, cut:].astype(F32)


def cross_part(where, here, came, after):
    hlf, width = here.shape
    cut = 3 * hlf
    return local(
        functools.partial(add_kernel, cut), where, (here, came),
        jax.ShapeDtypeStruct((hlf, width - cut), F32), (), (after,),
    )


def square_kernel(factor_scale, where, old, here, came, after, out, buf, sems):
    hlf = here.shape[0]
    rows = 2 * hlf

    def packed(lo, hi):
        return here[:, lo:hi] + came[:, lo:hi].astype(F32)

    put_rows(
        factor_scale, old, out, buf, sems, where[CORE] * rows,
        (
            lambda: [packed(0, hlf), packed(hlf, rows)],
            lambda: [packed(hlf, rows).T, packed(rows, rows + hlf)],
        ),
    )


def cross_kernel(factor_scale, where, old, mine, sib, done, out, token, buf, sems):
    core = where[CORE]
    hlf, rows = mine.shape

    def put(pieces):
        put_rows(factor_scale, old, out, buf, sems, (1 - core) * rows, pieces)

    @pl.when(core == 0)
    def _():
        put(tuple((lambda part=part: [part[:, :hlf], part[:, hlf:]]) for part in (mine, sib)))

    @pl.when(core == 1)
    def _():
        put(
            tuple(
                (lambda a=a: [sib[:, a:a + hlf].T, mine[:, a:a + hlf].T]) for a in (0, hlf)
            )
        )

    token[...] = jnp.zeros_like(token)


def update(factor_scale, where, old, here, came, mine, sib, after):
    total = old.shape[0]
    shape = jax.ShapeDtypeStruct(old.shape, F32)
    scratch = [pltpu.VMEM((total, total), F32), pltpu.SemaphoreType.DMA((2,))]
    vmem = pl.BlockSpec(memory_space=pltpu.VMEM)
    done = local(
        functools.partial(square_kernel, factor_scale), where, (old, here, came), shape, scratch,
        (after,), out_specs=ANY,
    )
    return pl.pallas_call(
        functools.partial(cross_kernel, factor_scale),
        in_specs=[pl.BlockSpec(memory_space=pltpu.SMEM)] + [vmem] * 3 + [ANY],
        out_specs=[ANY, vmem],
        out_shape=[shape, TOKEN],
        scratch_shapes=scratch,
        input_output_aliases={4: 0},
        compiler_params=pltpu.CompilerParams(vmem_limit_bytes=24 << 20),
        cost_estimate=pl.CostEstimate(flops=0, transcendentals=0, bytes_accessed=0),
    )(where, old, mine, sib, done)


def shards(
    entering, returning, adapter_down, adapter_up, stashed, doc_ids, input_factor, output_factor
):
    sec = lax.axis_index("section")
    rep = lax.axis_index("dp")
    sections = lax.axis_size("section")
    replicas = lax.axis_size("dp")
    tok = entering.shape[1]
    steps_count = stashed.shape[1]
    rank = stashed.shape[2]
    rows, block = input_factor.shape[1:]
    tokens = tok * replicas

    def first(home):
        return (home < sections // 2).astype(jnp.int32)

    x0 = entering[0]
    f1 = first((sec + sections - 1) % sections) + (sec == 0).astype(jnp.int32)
    b1 = (sec + 1 < sections).astype(jnp.int32)
    b2 = (sec + 2 < sections).astype(jnp.int32)
    where = jnp.stack(
        [rep // 2, rep % 2, sec, first(sec), f1, b1, b2, rep // 4 % 2]
    ).astype(jnp.int32)

    with jax.named_scope("weights"):
        pieces, gate0 = split(where, x0, adapter_down, doc_ids, replicas, 8)
        ahead, behind1, behind2 = pack(where, adapter_down, adapter_up, block, gate0)
        ahead = shift(ahead, "section", -1)
        behind1 = shift(behind1, "section", 1)
        behind2 = shift(behind2, "section", 2)
        x1, up_own, up_oth, token5 = next_activation(where, x0, adapter_up, gate0, rows)
        ahead = tie(ahead, behind1, behind2, token5, space=pltpu.VMEM)
        ahead_sib = swap_cores(ahead)
        behind = join(where, behind1, behind2)
        behind_pair = swap_chips(behind)

    with jax.named_scope("gates"):
        sent = gates(where, x1, ahead, ahead_sib, gate0, replicas)

    with jax.named_scope("columns"):
        own = tie(lax.all_to_all(pieces, "dp", 0, 0), sent, behind_pair, space=pltpu.VMEM)
        other = swap_cores(own)
        got = lax.all_to_all(sent, "dp", 0, 0)

    with jax.named_scope("factor"):
        ups = (got, up_own, up_oth, ahead)
        step0, token0 = gram(0, where, own, other)
        step2, token2 = gram(2, where, own, other, ups, (token0,))
        from2 = shift(step2, "section", 1)

    with jax.named_scope("backward"):
        behind = join(where, behind, behind_pair)
        behind_sib = swap_cores(behind)
        proj, m0, by1, by2 = project(
            where, returning[0], adapter_down, adapter_up, behind, behind_sib, ahead, ahead_sib,
            stashed, token2,
        )
        by1 = shift(by1, "section", 1)
        by2 = shift(by2, "section", 2)

    with jax.named_scope("factor"):
        step1, token1 = gram(1, where, own, other, ups, (m0,))
        from1, token3 = merge(where, step1, from2, (token1, by1, by2))
        from1 = shift(from1, "section", 1)

    with jax.named_scope("backward"):
        outer0, outer1, outer2 = back(where, proj, m0, by1, by2, stashed, token3)
        outer1 = shift(outer1, "section", -1)
        outer2 = shift(outer2, "section", -2)
        share, token4 = curvature(where, (outer0, outer1, outer2), replicas)
        shares = lax.all_to_all(share, "dp", 0, 0)

    with jax.named_scope("factor"):
        mine = cross_part(where, step0, from1, shares)
        sib = swap_cores(mine)
        factor_scale = 0.25 / (steps_count * tokens)
        input_factor_new, last = update(
            factor_scale, where, input_factor[0], step0, from1, mine, sib, token4
        )

    with jax.named_scope("backward"):
        output_factor_new = statistics(where, output_factor, shares, tokens, last)
    return (input_factor_new[None], output_factor_new)


def solution(mesh):
    in_specs = (
        P("section", "dp", None),
        P("section", "dp", None),
        P(None, "section", None, None),
        P(None, "section", None, None),
        P("section", None, None, "dp"),
        P(None, "dp"),
        P("section", "dp", None),
        P(None, "section", None, None),
    )
    out_specs = (P("section", "dp", None), P(None, "section", None, None))
    return jax.shard_map(shards, mesh=mesh, in_specs=in_specs, out_specs=out_specs, check_vma=False)
```

```python
import functools

import jax
import jax.numpy as jnp
from jax import lax
from jax.experimental import pallas as pl
from jax.experimental.pallas import tpu as pltpu
from jax.sharding import PartitionSpec as P

F32 = jnp.float32
BF16 = jnp.bfloat16
ANY = pl.BlockSpec(memory_space=pl.ANY)
TOKEN = jax.ShapeDtypeStruct((8, 128), F32)


def shift(block, axis, distance):
    count = lax.axis_size(axis)
    return lax.ppermute(block, axis, [(i, (i + distance) % count) for i in range(count)])


def swap_cores(block):
    count = lax.axis_size("dp")
    return lax.ppermute(block, "dp", [(i, i ^ 1) for i in range(count)])


def swap_chips(block):
    count = lax.axis_size("dp")
    return lax.ppermute(block, "dp", [(i, i ^ 4) for i in range(count)])


def nt(a, b):
    return lax.dot_general(a, b, (((1,), (1,)), ((), ())), preferred_element_type=F32)


def tn(a, b):
    return lax.dot_general(a, b, (((0,), (0,)), ((), ())), preferred_element_type=F32)


def call(kernel, where, operands, in_specs, outs, out_specs, grid, scratch=(), aliases={}):
    spec = pltpu.PrefetchScalarGridSpec(
        num_scalar_prefetch=1,
        grid=grid,
        in_specs=in_specs,
        out_specs=out_specs,
        scratch_shapes=list(scratch),
    )
    return pl.pallas_call(
        kernel,
        grid_spec=spec,
        out_shape=outs,
        input_output_aliases=aliases,
        compiler_params=pltpu.CompilerParams(dimension_semantics=("arbitrary",) * len(grid)),
        cost_estimate=pl.CostEstimate(flops=0, transcendentals=0, bytes_accessed=0),
    )(where, *operands)


def tie_kernel(x, *rest):
    del x, rest


def tie(x, *after, space=pltpu.HBM):
    spec = pl.BlockSpec(memory_space=space)
    return pl.pallas_call(
        tie_kernel,
        in_specs=[spec] + [ANY] * len(after),
        out_specs=spec,
        out_shape=jax.ShapeDtypeStruct(x.shape, x.dtype),
        input_output_aliases={0: 0},
        compiler_params=pltpu.CompilerParams(vmem_limit_bytes=8 << 20),
        cost_estimate=pl.CostEstimate(flops=0, transcendentals=0, bytes_accessed=0),
    )(x, *after)


CHIP, CORE, SEC, C0, F1, B1, B2, PAIR = range(8)


def split_kernel(where, x, down, ids, out, gate, acc):
    i = pl.program_id(0)
    pieces, _, cols = out.shape
    tok, rank = gate.shape

    @pl.when(i == 0)
    def _():
        acc[...] = jnp.zeros_like(acc)

    acc[...] += nt(x[...], down[0, 0])
    row = ids[pl.ds(where[SEC], 1), :].astype(F32)
    row = jnp.broadcast_to(row, (out.shape[1] - tok, tok)).astype(BF16)
    for k in range(pieces):
        out[k, :tok, :] = x[:, k * cols:(k + 1) * cols]
        out[k, tok:, :tok] = row
        out[k, tok:, tok:] = jnp.zeros((out.shape[1] - tok, cols - tok), BF16)

    @pl.when(i == pl.num_programs(0) - 1)
    def _():
        z = acc[...]
        gate[...] = (z * jax.nn.sigmoid(z)).astype(BF16)


def split(where, x, adapter_down, doc_ids, pieces, extra):
    tok, width = x.shape
    rank = adapter_down.shape[2]
    cols = width // pieces
    grid = 8
    each = width // grid
    return call(
        split_kernel,
        where,
        (x, adapter_down, doc_ids),
        [
            pl.BlockSpec((tok, each), lambda i, w: (0, i)),
            pl.BlockSpec((1, 1, rank, each), lambda i, w: (w[C0], 0, 0, i)),
            pl.BlockSpec(doc_ids.shape, lambda i, w: (0, 0)),
        ],
        [
            jax.ShapeDtypeStruct((pieces, tok + extra, cols), BF16),
            jax.ShapeDtypeStruct((tok, rank), BF16),
        ],
        [
            pl.BlockSpec((pieces // grid, tok + extra, cols), lambda i, w: (i, 0, 0)),
            pl.BlockSpec((tok, rank), lambda i, w: (0, 0)),
        ],
        (grid,),
        [pltpu.VMEM((tok, rank), F32)],
    )


def pack_kernel(where, up_f, down_f, up_b1, up_b2, after, ahead, behind1, behind2):
    cols = up_f.shape[3]
    ahead[:, :cols] = up_f[0, 0]
    ahead[:, cols:] = down_f[0, 0]
    behind1[...] = up_b1[0, 0]
    behind2[...] = up_b2[0, 0]


def pack(where, adapter_down, adapter_up, block, after):
    rank, width = adapter_down.shape[2:]
    half = width // 2
    part = lambda span: pl.BlockSpec(
        (1, 1, rank, half // 2), lambda i, w: (w[span], 0, 0, 2 * w[CORE] + w[PAIR])
    )
    shapes = ((rank, block + half), (rank, half // 2), (rank, half // 2))
    return call(
        pack_kernel,
        where,
        (adapter_up, adapter_down, adapter_up, adapter_up, after),
        [
            pl.BlockSpec((1, 1, rank, block), lambda i, w: (w[F1], 0, 0, w[CHIP])),
            pl.BlockSpec((1, 1, rank, half), lambda i, w: (w[F1], 0, 0, w[CORE])),
            part(B1),
            part(B2),
            pl.BlockSpec(after.shape, lambda i, w: (0, 0)),
        ],
        [jax.ShapeDtypeStruct(shape, BF16) for shape in shapes],
        [pl.BlockSpec(shape, lambda i, w: (0, 0)) for shape in shapes],
        (1,),
    )


def ahead_kernel(where, x, up, gate0, u0o, u0s, x1, own, oth, token):
    add = jnp.dot(gate0[...], up[0, 0], preferred_element_type=F32)
    x1[...] = (x[...].astype(F32) + add).astype(BF16)

    @pl.when(pl.program_id(0) == 0)
    def _():
        own[...] = u0o[0, 0]
        oth[...] = u0s[0, 0]
        token[...] = jnp.zeros_like(token)


def next_activation(where, x, adapter_up, gate0, rows):
    tok, width = x.shape
    rank = gate0.shape[1]
    grid = 4
    each = width // grid
    u0 = lambda side: pl.BlockSpec(
        (1, 1, rank, rows), lambda i, w: (w[C0], 0, 0, 2 * w[CHIP] + side(w))
    )
    one = lambda shape: pl.BlockSpec(shape, lambda i, w: (0, 0))
    return call(
        ahead_kernel,
        where,
        (x, adapter_up, gate0, adapter_up, adapter_up),
        [
            pl.BlockSpec((tok, each), lambda i, w: (0, i)),
            pl.BlockSpec((1, 1, rank, each), lambda i, w: (w[C0], 0, 0, i)),
            one((tok, rank)),
            u0(lambda w: w[CORE]),
            u0(lambda w: 1 - w[CORE]),
        ],
        [
            jax.ShapeDtypeStruct((tok, width), BF16),
            jax.ShapeDtypeStruct((rank, rows), BF16),
            jax.ShapeDtypeStruct((rank, rows), BF16),
            TOKEN,
        ],
        [
            pl.BlockSpec((tok, each), lambda i, w: (0, i)),
            one((rank, rows)),
            one((rank, rows)),
            one(TOKEN.shape),
        ],
        (grid,),
    )


def gate_kernel(where, x1, mine, sib, gate0, sent):
    core = where[CORE]
    half = x1.shape[1] // 2
    skip = mine.shape[1] - half
    z = nt(x1[:, pl.ds(pl.multiple_of(core * half, half), half)], mine[:, skip:])
    z += nt(x1[:, pl.ds(pl.multiple_of((1 - core) * half, half), half)], sib[:, skip:])
    gate1 = (z * jax.nn.sigmoid(z)).astype(BF16)
    both = jnp.concatenate([gate0[...], gate1], axis=1)
    for k in range(sent.shape[0]):
        sent[k] = both


def gates(where, x1, ahead_mine, ahead_sib, gate0, replicas):
    tok, rank = gate0.shape
    return local(
        gate_kernel,
        where,
        (x1, ahead_mine, ahead_sib, gate0),
        jax.ShapeDtypeStruct((replicas, tok, 2 * rank), BF16),
    )


def local(kernel, where, operands, outs, scratch=(), after=(), aliases={}, out_specs=None):
    vmem = pl.BlockSpec(memory_space=pltpu.VMEM)
    out_vmem = [vmem] * len(outs) if isinstance(outs, list) else vmem
    return pl.pallas_call(
        kernel,
        in_specs=[pl.BlockSpec(memory_space=pltpu.SMEM)]
        + [vmem] * len(operands)
        + [vmem] * len(after),
        out_specs=out_specs or out_vmem,
        out_shape=outs,
        scratch_shapes=list(scratch),
        input_output_aliases=aliases,
        compiler_params=pltpu.CompilerParams(vmem_limit_bytes=24 << 20),
        cost_estimate=pl.CostEstimate(flops=0, transcendentals=0, bytes_accessed=0),
    )(where, *operands, *after)


def join_kernel(where, a, b, *rest):
    out = rest[-1]
    out[:a.shape[0]] = a[...]
    out[a.shape[0]:] = b[...]


def join(where, a, b, after=()):
    shape = (a.shape[0] + b.shape[0], a.shape[1])
    return local(
        join_kernel, where, (a, b), jax.ShapeDtypeStruct(shape, a.dtype), (), after
    )


def scale_columns(own, tok):
    replicas = own.shape[0]
    ids = [own[k, tok:tok + 1, :tok].astype(F32) for k in range(replicas)]
    doc = lax.broadcasted_iota(jnp.int32, (2 * replicas, tok), 0).astype(F32)
    hits = jnp.zeros((2 * replicas, tok), F32)
    for row in ids:
        hits += (doc == row).astype(F32)
    count = jnp.maximum(jnp.sum(hits, axis=1, keepdims=True), 1.0)
    table = jnp.sqrt(jnp.sqrt(tok / count))
    scales = [jnp.sum(jnp.where(doc == row, table, 0.0), axis=0, keepdims=True) for row in ids]
    return jnp.concatenate(scales + [jnp.zeros((tok - replicas, tok), F32)], axis=0).T


def gram_kernel(step, where, own, other, *rest):
    core = where[CORE]
    replicas, long, rows = own.shape
    if step:
        got, up_own, up_oth, ahead = rest[:4]
        ups_own, ups_oth = up_own[...], up_oth[...]
    if step == 2:
        one = lambda side: ahead[:, pl.ds(pl.multiple_of(side * rows, rows), rows)]
        ups_own = jnp.concatenate([ups_own, one(core)], axis=0)
        ups_oth = jnp.concatenate([ups_oth, one(1 - core)], axis=0)
    rest = rest[4 if step else 0:]
    tok = long - 8
    hlf = rows // 2
    per = 4
    if step == 2:
        out, token, acc = rest[-3:]
    else:
        acc, token = rest[-2:]
    columns = scale_columns(own, tok)

    for i in range(replicas // per):
        ks = range(i * per, (i + 1) * per)

        def rebuilt(ref, ups):
            act = jnp.concatenate([ref[k, :tok, :] for k in ks], axis=0).astype(F32)
            if step:
                gate = jnp.concatenate([got[k] for k in ks], axis=0)[:, :ups.shape[0]]
                add = jnp.dot(gate, ups, preferred_element_type=F32)
                act = (act + add).astype(BF16).astype(F32)
            scale = [jnp.broadcast_to(columns[:, k:k + 1], (tok, rows)) for k in ks]
            return (jnp.concatenate(scale, axis=0) * act).astype(BF16)

        def put(lo, val):
            hi = lo + val.shape[1]
            acc[:, lo:hi] = val if i == 0 else acc[:, lo:hi] + val

        r = rebuilt(own, ups_own if step else None)
        q = rebuilt(other, ups_oth if step else None)
        put(0, tn(r[:, :hlf], r))
        put(rows, tn(r[:, hlf:], r[:, hlf:]))

        @pl.when(core == 0)
        def _():
            put(rows + hlf, tn(r[:, :hlf], q))

        @pl.when(core == 1)
        def _():
            put(rows + hlf, tn(q[:, hlf:], r))

    token[...] = jnp.zeros_like(token)
    if step == 2:
        out[...] = acc[...].astype(BF16)


def gram(step, where, own, other, ups=(), after=()):
    rows = own.shape[2]
    packed = (rows // 2, rows * 5 // 2)
    return local(
        functools.partial(gram_kernel, step),
        where,
        (own, other, *ups),
        [jax.ShapeDtypeStruct(packed, BF16 if step == 2 else F32), TOKEN],
        [pltpu.VMEM(packed, F32)] if step == 2 else [],
        after,
    )


def project_kernel(where, *refs):
    ins, stash, (proj, m0, by1, by2) = refs[:14], refs[14], refs[16:]
    i = pl.program_id(0)
    rank = stash.shape[2]

    @pl.when(i == 0)
    def _():
        for acc in (proj, m0, by1, by2):
            acc[...] = jnp.zeros_like(acc)
        by1[:rank] = stash[0, 1]
        by2[:rank] = stash[0, 2]

    for g, u, d, d1, u2, b, a in (ins[0::2], ins[1::2]):
        two = b[...]
        proj[:rank] += nt(u[0, 0], g[...])
        proj[rank:] += nt(two, g[...])
        m0[...] += nt(two, d[0, 0])
        by1[rank:, :rank] += nt(b[:rank], d1[0, 0])
        by2[rank:, :rank] += nt(u2[0, 0], a[...])


def project(where, grad, adapter_down, adapter_up, b, b_sib, ahead, ahead_sib, stashed, after):
    tok, width = grad.shape
    rank = adapter_up.shape[2]
    each = ahead.shape[1] - width // 2
    grid = width // 2 // each
    mine, sib = (lambda w: w[CORE]), (lambda w: 1 - w[CORE])

    def half(span, side):
        return pl.BlockSpec(
            (1, 1, rank, each), lambda i, w: (span(w), 0, 0, side(w) * grid + i)
        )

    def weights(span):
        return [half(span, mine), half(span, sib)]

    g_spec = lambda side: pl.BlockSpec((tok, each), lambda i, w: (0, side(w) * grid + i))
    got = lambda skip: pl.BlockSpec((rank, each), lambda i, w: (0, i + skip))
    per = grid // 2
    quarter = pl.BlockSpec((2 * rank, each), lambda i, w: ((i // per + w[PAIR]) % 2, i % per))
    one = lambda w: 1
    shapes = ((3 * rank, tok), (2 * rank, rank), (2 * rank, tok), (2 * rank, tok))
    return call(
        project_kernel,
        where,
        (
            grad, grad, adapter_up, adapter_up, adapter_down, adapter_down,
            adapter_down, adapter_down, adapter_up, adapter_up,
            b, b_sib, ahead, ahead_sib, stashed, after,
        ),
        [g_spec(mine), g_spec(sib)]
        + weights(one)
        + weights(one)
        + weights(lambda w: w[B1])
        + weights(lambda w: w[B2])
        + [quarter] * 2
        + [got(1)] * 2
        + [pl.BlockSpec(stashed.shape, lambda i, w: (0, 0, 0, 0))]
        + [pl.BlockSpec(after.shape, lambda i, w: (0, 0))],
        [jax.ShapeDtypeStruct(shape, F32) for shape in shapes],
        [pl.BlockSpec(shape, lambda i, w: (0, 0)) for shape in shapes],
        (grid,),
    )


def back_kernel(where, proj, m0, by1, by2, q0, *rest):
    outs = rest[-3:]
    rank = m0.shape[1]

    def dz_of(grad_act, q):
        sigma = jax.nn.sigmoid(q)
        return (grad_act * sigma * (1.0 + q * (1.0 - sigma))).astype(BF16)

    def exact(m, d):
        return jnp.dot(
            m, d.astype(F32), precision=lax.Precision.HIGHEST, preferred_element_type=F32
        )

    m12 = jnp.where(where[SEC] == 0, by2[rank:, :rank], by1[rank:, :rank])
    dz0 = dz_of(proj[:rank], q0[0, 0])
    dz1 = dz_of(proj[rank:2 * rank] + exact(m0[:rank], dz0), by1[:rank])
    dz2 = dz_of(proj[2 * rank:] + exact(m0[rank:], dz0) + exact(m12, dz1), by2[:rank])
    for out, dz in zip(outs, (dz0, dz1, dz2)):
        out[...] = nt(dz, dz)


def back(where, proj, m0, by1, by2, stashed, after):
    rank = m0.shape[1]
    return local(
        back_kernel,
        where,
        (proj, m0, by1, by2, stashed),
        [jax.ShapeDtypeStruct((rank, rank), F32)] * 3,
        (),
        (after,),
    )


def merge_kernel(where, a, b, *rest):
    out, token = rest[-2:]
    out[...] = (a[...] + b[...].astype(F32)).astype(BF16)
    token[...] = jnp.zeros_like(token)


def merge(where, a, b, after):
    return local(
        merge_kernel, where, (a, b), [jax.ShapeDtypeStruct(a.shape, BF16), TOKEN], (), after
    )


def curvature_kernel(where, outer0, outer1, outer2, out, token):
    rank = outer0.shape[0]
    f1 = where[B1].astype(F32)
    f2 = where[B2].astype(F32)
    zero = outer1[...] * (1.0 - f1) + outer2[...] * (1.0 - f2)
    one = outer0[...] + outer1[...] * f1 + outer2[...] * f2
    both = jnp.concatenate([zero, one], axis=1)
    for k in range(out.shape[0]):
        out[k] = both
    token[...] = jnp.zeros_like(token)


def curvature(where, outers, replicas):
    rank = outers[0].shape[0]
    return local(
        curvature_kernel, where, outers,
        [jax.ShapeDtypeStruct((replicas, rank, 2 * rank), F32), TOKEN],
    )


def statistics_kernel(tokens, where, old, parts, after, out):
    rank = old.shape[2]
    total = parts[0]
    for k in range(1, parts.shape[0]):
        total = total + parts[k]
    later = where[B1] + where[B2]
    for span, held in enumerate((2 - later, 1 + later)):
        held = jnp.full((rank, rank), held.astype(F32), F32)
        was = old[span, 0]
        share = total[:, span * rank:(span + 1) * rank] / (jnp.maximum(held, 1.0) * tokens)
        out[span, 0] = jnp.where(held > 0.0, 0.75 * was + 0.25 * share, was)


def statistics(where, old, parts, tokens, after):
    return local(
        functools.partial(statistics_kernel, tokens),
        where,
        (old, parts),
        jax.ShapeDtypeStruct(old.shape, F32),
        (),
        (after,),
    )


def put_rows(factor_scale, old, out, buf, sems, first_col, pieces):
    hlf = buf.shape[0] // 2
    cols = pl.ds(pl.multiple_of(first_col, 2 * hlf), 2 * hlf)
    sent = []
    for i, values in enumerate(pieces):
        rows = pl.ds(i * hlf, hlf)
        at = 0
        for value in values():
            here = slice(at, at + value.shape[1])
            was = old[rows, pl.ds(pl.multiple_of(first_col + at, hlf), value.shape[1])]
            buf[rows, here] = 0.75 * was + factor_scale * value
            at += value.shape[1]
        copy = pltpu.make_async_copy(buf.at[rows], out.at[rows, cols], sems.at[i])
        copy.start()
        sent.append(copy)
    for copy in sent:
        copy.wait()


def add_kernel(cut, where, here, came, after, out):
    out[...] = here[:, cut:] + came[:, cut:].astype(F32)


def cross_part(where, here, came, after):
    hlf, width = here.shape
    cut = 3 * hlf
    return local(
        functools.partial(add_kernel, cut), where, (here, came),
        jax.ShapeDtypeStruct((hlf, width - cut), F32), (), (after,),
    )


def square_kernel(factor_scale, where, old, here, came, after, out, buf, sems):
    hlf = here.shape[0]
    rows = 2 * hlf

    def packed(lo, hi):
        return here[:, lo:hi] + came[:, lo:hi].astype(F32)

    put_rows(
        factor_scale, old, out, buf, sems, where[CORE] * rows,
        (
            lambda: [packed(0, hlf), packed(hlf, rows)],
            lambda: [packed(hlf, rows).T, packed(rows, rows + hlf)],
        ),
    )


def cross_kernel(factor_scale, where, old, mine, sib, done, out, token, buf, sems):
    core = where[CORE]
    hlf, rows = mine.shape

    def put(pieces):
        put_rows(factor_scale, old, out, buf, sems, (1 - core) * rows, pieces)

    @pl.when(core == 0)
    def _():
        put(tuple((lambda part=part: [part[:, :hlf], part[:, hlf:]]) for part in (mine, sib)))

    @pl.when(core == 1)
    def _():
        put(
            tuple(
                (lambda a=a: [sib[:, a:a + hlf].T, mine[:, a:a + hlf].T]) for a in (0, hlf)
            )
        )

    token[...] = jnp.zeros_like(token)


def update(factor_scale, where, old, here, came, mine, sib, after):
    total = old.shape[0]
    shape = jax.ShapeDtypeStruct(old.shape, F32)
    scratch = [pltpu.VMEM((total, total), F32), pltpu.SemaphoreType.DMA((2,))]
    vmem = pl.BlockSpec(memory_space=pltpu.VMEM)
    done = local(
        functools.partial(square_kernel, factor_scale), where, (old, here, came), shape, scratch,
        (after,), out_specs=ANY,
    )
    return pl.pallas_call(
        functools.partial(cross_kernel, factor_scale),
        in_specs=[pl.BlockSpec(memory_space=pltpu.SMEM)] + [vmem] * 3 + [ANY],
        out_specs=[ANY, vmem],
        out_shape=[shape, TOKEN],
        scratch_shapes=scratch,
        input_output_aliases={4: 0},
        compiler_params=pltpu.CompilerParams(vmem_limit_bytes=24 << 20),
        cost_estimate=pl.CostEstimate(flops=0, transcendentals=0, bytes_accessed=0),
    )(where, old, mine, sib, done)


def shards(
    entering, returning, adapter_down, adapter_up, stashed, doc_ids, input_factor, output_factor
):
    sec = lax.axis_index("section")
    rep = lax.axis_index("dp")
    sections = lax.axis_size("section")
    replicas = lax.axis_size("dp")
    tok = entering.shape[1]
    steps_count = stashed.shape[1]
    rank = stashed.shape[2]
    rows, block = input_factor.shape[1:]
    tokens = tok * replicas

    def first(home):
        return (home < sections // 2).astype(jnp.int32)

    x0 = entering[0]
    f1 = first((sec + sections - 1) % sections) + (sec == 0).astype(jnp.int32)
    b1 = (sec + 1 < sections).astype(jnp.int32)
    b2 = (sec + 2 < sections).astype(jnp.int32)
    where = jnp.stack(
        [rep // 2, rep % 2, sec, first(sec), f1, b1, b2, rep // 4 % 2]
    ).astype(jnp.int32)

    with jax.named_scope("weights"):
        pieces, gate0 = split(where, x0, adapter_down, doc_ids, replicas, 8)
        ahead, behind1, behind2 = pack(where, adapter_down, adapter_up, block, gate0)
        ahead = shift(ahead, "section", -1)
        behind1 = shift(behind1, "section", 1)
        behind2 = shift(behind2, "section", 2)
        x1, up_own, up_oth, token5 = next_activation(where, x0, adapter_up, gate0, rows)
        ahead = tie(ahead, behind1, behind2, token5, space=pltpu.VMEM)
        ahead_sib = swap_cores(ahead)
        behind = join(where, behind1, behind2)
        behind_pair = swap_chips(behind)

    with jax.named_scope("gates"):
        sent = gates(where, x1, ahead, ahead_sib, gate0, replicas)

    with jax.named_scope("columns"):
        own = tie(lax.all_to_all(pieces, "dp", 0, 0), sent, space=pltpu.VMEM)
        other = swap_cores(own)
        got = lax.all_to_all(sent, "dp", 0, 0)

    with jax.named_scope("factor"):
        ups = (got, up_own, up_oth, ahead)
        step0, token0 = gram(0, where, own, other)
        step2, token2 = gram(2, where, own, other, ups, (token0,))
        from2 = shift(step2, "section", 1)

    with jax.named_scope("backward"):
        behind = join(where, behind, behind_pair, (token0,))
        behind_sib = swap_cores(behind)
        proj, m0, by1, by2 = project(
            where, returning[0], adapter_down, adapter_up, behind, behind_sib, ahead, ahead_sib,
            stashed, token2,
        )
        by1 = shift(by1, "section", 1)
        by2 = shift(by2, "section", 2)

    with jax.named_scope("factor"):
        step1, token1 = gram(1, where, own, other, ups, (m0,))
        from1, token3 = merge(where, step1, from2, (token1, by1, by2))
        from1 = shift(from1, "section", 1)

    with jax.named_scope("backward"):
        outer0, outer1, outer2 = back(where, proj, m0, by1, by2, stashed, token3)
        outer1 = shift(outer1, "section", -1)
        outer2 = shift(outer2, "section", -2)
        share, token4 = curvature(where, (outer0, outer1, outer2), replicas)
        shares = lax.all_to_all(share, "dp", 0, 0)

    with jax.named_scope("factor"):
        mine = cross_part(where, step0, from1, shares)
        sib = swap_cores(mine)
        factor_scale = 0.25 / (steps_count * tokens)
        input_factor_new, last = update(
            factor_scale, where, input_factor[0], step0, from1, mine, sib, token4
        )

    with jax.named_scope("backward"):
        output_factor_new = statistics(where, output_factor, shares, tokens, last)
    return (input_factor_new[None], output_factor_new)


def solution(mesh):
    in_specs = (
        P("section", "dp", None),
        P("section", "dp", None),
        P(None, "section", None, None),
        P(None, "section", None, None),
        P("section", None, None, "dp"),
        P(None, "dp"),
        P("section", "dp", None),
        P(None, "section", None, None),
    )
    out_specs = (P("section", "dp", None), P(None, "section", None, None))
    return jax.shard_map(shards, mesh=mesh, in_specs=in_specs, out_specs=out_specs, check_vma=False)
```

```python
import functools

import jax
import jax.numpy as jnp
from jax import lax
from jax.experimental import pallas as pl
from jax.experimental.pallas import tpu as pltpu
from jax.sharding import PartitionSpec as P

F32 = jnp.float32
BF16 = jnp.bfloat16
ANY = pl.BlockSpec(memory_space=pl.ANY)
TOKEN = jax.ShapeDtypeStruct((8, 128), F32)


def shift(block, axis, distance):
    count = lax.axis_size(axis)
    return lax.ppermute(block, axis, [(i, (i + distance) % count) for i in range(count)])


def swap_cores(block):
    count = lax.axis_size("dp")
    return lax.ppermute(block, "dp", [(i, i ^ 1) for i in range(count)])


def swap_chips(block):
    count = lax.axis_size("dp")
    return lax.ppermute(block, "dp", [(i, i ^ 4) for i in range(count)])


def nt(a, b):
    return lax.dot_general(a, b, (((1,), (1,)), ((), ())), preferred_element_type=F32)


def tn(a, b):
    return lax.dot_general(a, b, (((0,), (0,)), ((), ())), preferred_element_type=F32)


def call(kernel, where, operands, in_specs, outs, out_specs, grid, scratch=(), aliases={}):
    spec = pltpu.PrefetchScalarGridSpec(
        num_scalar_prefetch=1,
        grid=grid,
        in_specs=in_specs,
        out_specs=out_specs,
        scratch_shapes=list(scratch),
    )
    return pl.pallas_call(
        kernel,
        grid_spec=spec,
        out_shape=outs,
        input_output_aliases=aliases,
        compiler_params=pltpu.CompilerParams(dimension_semantics=("arbitrary",) * len(grid)),
        cost_estimate=pl.CostEstimate(flops=0, transcendentals=0, bytes_accessed=0),
    )(where, *operands)


def tie_kernel(x, *rest):
    del x, rest


def tie(x, *after, space=pltpu.HBM):
    spec = pl.BlockSpec(memory_space=space)
    return pl.pallas_call(
        tie_kernel,
        in_specs=[spec] + [ANY] * len(after),
        out_specs=spec,
        out_shape=jax.ShapeDtypeStruct(x.shape, x.dtype),
        input_output_aliases={0: 0},
        compiler_params=pltpu.CompilerParams(vmem_limit_bytes=8 << 20),
        cost_estimate=pl.CostEstimate(flops=0, transcendentals=0, bytes_accessed=0),
    )(x, *after)


CHIP, CORE, SEC, C0, F1, B1, B2, PAIR = range(8)


def split_kernel(where, x, down, ids, out, gate, acc):
    i = pl.program_id(0)
    pieces, _, cols = out.shape
    tok, rank = gate.shape

    @pl.when(i == 0)
    def _():
        acc[...] = jnp.zeros_like(acc)

    acc[...] += nt(x[...], down[0, 0])
    row = ids[pl.ds(where[SEC], 1), :].astype(F32)
    row = jnp.broadcast_to(row, (out.shape[1] - tok, tok)).astype(BF16)
    for k in range(pieces):
        out[k, :tok, :] = x[:, k * cols:(k + 1) * cols]
        out[k, tok:, :tok] = row
        out[k, tok:, tok:] = jnp.zeros((out.shape[1] - tok, cols - tok), BF16)

    @pl.when(i == pl.num_programs(0) - 1)
    def _():
        z = acc[...]
        gate[...] = (z * jax.nn.sigmoid(z)).astype(BF16)


def split(where, x, adapter_down, doc_ids, pieces, extra):
    tok, width = x.shape
    rank = adapter_down.shape[2]
    cols = width // pieces
    grid = 4
    each = width // grid
    return call(
        split_kernel,
        where,
        (x, adapter_down, doc_ids),
        [
            pl.BlockSpec((tok, each), lambda i, w: (0, i)),
            pl.BlockSpec((1, 1, rank, each), lambda i, w: (w[C0], 0, 0, i)),
            pl.BlockSpec(doc_ids.shape, lambda i, w: (0, 0)),
        ],
        [
            jax.ShapeDtypeStruct((pieces, tok + extra, cols), BF16),
            jax.ShapeDtypeStruct((tok, rank), BF16),
        ],
        [
            pl.BlockSpec((pieces // grid, tok + extra, cols), lambda i, w: (i, 0, 0)),
            pl.BlockSpec((tok, rank), lambda i, w: (0, 0)),
        ],
        (grid,),
        [pltpu.VMEM((tok, rank), F32)],
    )


def pack_kernel(where, up_f, down_f, up_b1, up_b2, after, ahead, behind1, behind2):
    cols = up_f.shape[3]
    ahead[:, :cols] = up_f[0, 0]
    ahead[:, cols:] = down_f[0, 0]
    behind1[...] = up_b1[0, 0]
    behind2[...] = up_b2[0, 0]


def pack(where, adapter_down, adapter_up, block, after):
    rank, width = adapter_down.shape[2:]
    half = width // 2
    part = lambda span: pl.BlockSpec(
        (1, 1, rank, half // 2), lambda i, w: (w[span], 0, 0, 2 * w[CORE] + w[PAIR])
    )
    shapes = ((rank, block + half), (rank, half // 2), (rank, half // 2))
    return call(
        pack_kernel,
        where,
        (adapter_up, adapter_down, adapter_up, adapter_up, after),
        [
            pl.BlockSpec((1, 1, rank, block), lambda i, w: (w[F1], 0, 0, w[CHIP])),
            pl.BlockSpec((1, 1, rank, half), lambda i, w: (w[F1], 0, 0, w[CORE])),
            part(B1),
            part(B2),
            pl.BlockSpec(after.shape, lambda i, w: (0, 0)),
        ],
        [jax.ShapeDtypeStruct(shape, BF16) for shape in shapes],
        [pl.BlockSpec(shape, lambda i, w: (0, 0)) for shape in shapes],
        (1,),
    )


def ahead_kernel(where, x, up, gate0, u0o, u0s, x1, own, oth, token):
    add = jnp.dot(gate0[...], up[0, 0], preferred_element_type=F32)
    x1[...] = (x[...].astype(F32) + add).astype(BF16)

    @pl.when(pl.program_id(0) == 0)
    def _():
        own[...] = u0o[0, 0]
        oth[...] = u0s[0, 0]
        token[...] = jnp.zeros_like(token)


def next_activation(where, x, adapter_up, gate0, rows):
    tok, width = x.shape
    rank = gate0.shape[1]
    grid = 4
    each = width // grid
    u0 = lambda side: pl.BlockSpec(
        (1, 1, rank, rows), lambda i, w: (w[C0], 0, 0, 2 * w[CHIP] + side(w))
    )
    one = lambda shape: pl.BlockSpec(shape, lambda i, w: (0, 0))
    return call(
        ahead_kernel,
        where,
        (x, adapter_up, gate0, adapter_up, adapter_up),
        [
            pl.BlockSpec((tok, each), lambda i, w: (0, i)),
            pl.BlockSpec((1, 1, rank, each), lambda i, w: (w[C0], 0, 0, i)),
            one((tok, rank)),
            u0(lambda w: w[CORE]),
            u0(lambda w: 1 - w[CORE]),
        ],
        [
            jax.ShapeDtypeStruct((tok, width), BF16),
            jax.ShapeDtypeStruct((rank, rows), BF16),
            jax.ShapeDtypeStruct((rank, rows), BF16),
            TOKEN,
        ],
        [
            pl.BlockSpec((tok, each), lambda i, w: (0, i)),
            one((rank, rows)),
            one((rank, rows)),
            one(TOKEN.shape),
        ],
        (grid,),
    )


def gate_kernel(where, x1, mine, sib, gate0, after, sent):
    core = where[CORE]
    half = x1.shape[1] // 2
    skip = mine.shape[1] - half
    z = nt(x1[:, pl.ds(pl.multiple_of(core * half, half), half)], mine[:, skip:])
    z += nt(x1[:, pl.ds(pl.multiple_of((1 - core) * half, half), half)], sib[:, skip:])
    gate1 = (z * jax.nn.sigmoid(z)).astype(BF16)
    both = jnp.concatenate([gate0[...], gate1], axis=1)
    for k in range(sent.shape[0]):
        sent[k] = both


def gates(where, x1, ahead_mine, ahead_sib, gate0, replicas, after):
    tok, rank = gate0.shape
    return local(
        gate_kernel,
        where,
        (x1, ahead_mine, ahead_sib, gate0),
        jax.ShapeDtypeStruct((replicas, tok, 2 * rank), BF16),
        (),
        (after,),
    )


def local(kernel, where, operands, outs, scratch=(), after=(), aliases={}, out_specs=None):
    vmem = pl.BlockSpec(memory_space=pltpu.VMEM)
    out_vmem = [vmem] * len(outs) if isinstance(outs, list) else vmem
    return pl.pallas_call(
        kernel,
        in_specs=[pl.BlockSpec(memory_space=pltpu.SMEM)]
        + [vmem] * len(operands)
        + [vmem] * len(after),
        out_specs=out_specs or out_vmem,
        out_shape=outs,
        scratch_shapes=list(scratch),
        input_output_aliases=aliases,
        compiler_params=pltpu.CompilerParams(vmem_limit_bytes=24 << 20),
        cost_estimate=pl.CostEstimate(flops=0, transcendentals=0, bytes_accessed=0),
    )(where, *operands, *after)


def join_kernel(where, a, b, *rest):
    out = rest[-1]
    out[:a.shape[0]] = a[...]
    out[a.shape[0]:] = b[...]


def join(where, a, b, after=()):
    shape = (a.shape[0] + b.shape[0], a.shape[1])
    return local(
        join_kernel, where, (a, b), jax.ShapeDtypeStruct(shape, a.dtype), (), after
    )


def scale_columns(own, tok):
    replicas = own.shape[0]
    ids = [own[k, tok:tok + 1, :tok].astype(F32) for k in range(replicas)]
    doc = lax.broadcasted_iota(jnp.int32, (2 * replicas, tok), 0).astype(F32)
    hits = jnp.zeros((2 * replicas, tok), F32)
    for row in ids:
        hits += (doc == row).astype(F32)
    count = jnp.maximum(jnp.sum(hits, axis=1, keepdims=True), 1.0)
    table = jnp.sqrt(jnp.sqrt(tok / count))
    scales = [jnp.sum(jnp.where(doc == row, table, 0.0), axis=0, keepdims=True) for row in ids]
    return jnp.concatenate(scales + [jnp.zeros((tok - replicas, tok), F32)], axis=0).T


def gram_kernel(step, where, own, other, *rest):
    core = where[CORE]
    replicas, long, rows = own.shape
    if step:
        got, up_own, up_oth, ahead = rest[:4]
        ups_own, ups_oth = up_own[...], up_oth[...]
    if step == 2:
        one = lambda side: ahead[:, pl.ds(pl.multiple_of(side * rows, rows), rows)]
        ups_own = jnp.concatenate([ups_own, one(core)], axis=0)
        ups_oth = jnp.concatenate([ups_oth, one(1 - core)], axis=0)
    rest = rest[4 if step else 0:]
    tok = long - 8
    hlf = rows // 2
    per = 4
    if step == 2:
        out, token, acc = rest[-3:]
    else:
        acc, token = rest[-2:]
    columns = scale_columns(own, tok)

    for i in range(replicas // per):
        ks = range(i * per, (i + 1) * per)

        def rebuilt(ref, ups):
            act = jnp.concatenate([ref[k, :tok, :] for k in ks], axis=0).astype(F32)
            if step:
                gate = jnp.concatenate([got[k] for k in ks], axis=0)[:, :ups.shape[0]]
                add = jnp.dot(gate, ups, preferred_element_type=F32)
                act = act + add
            scale = [jnp.broadcast_to(columns[:, k:k + 1], (tok, rows)) for k in ks]
            return (jnp.concatenate(scale, axis=0) * act).astype(BF16)

        def put(lo, val):
            hi = lo + val.shape[1]
            acc[:, lo:hi] = val if i == 0 else acc[:, lo:hi] + val

        r = rebuilt(own, ups_own if step else None)
        q = rebuilt(other, ups_oth if step else None)
        put(0, tn(r[:, :hlf], r))
        put(rows, tn(r[:, hlf:], r[:, hlf:]))

        @pl.when(core == 0)
        def _():
            put(rows + hlf, tn(r[:, :hlf], q))

        @pl.when(core == 1)
        def _():
            put(rows + hlf, tn(q[:, hlf:], r))

    token[...] = jnp.zeros_like(token)
    if step == 2:
        out[...] = acc[...].astype(BF16)


def gram(step, where, own, other, ups=(), after=()):
    rows = own.shape[2]
    packed = (rows // 2, rows * 5 // 2)
    return local(
        functools.partial(gram_kernel, step),
        where,
        (own, other, *ups),
        [jax.ShapeDtypeStruct(packed, BF16 if step == 2 else F32), TOKEN],
        [pltpu.VMEM(packed, F32)] if step == 2 else [],
        after,
    )


def project_kernel(where, *refs):
    ins, stash, (proj, m0, by1, by2) = refs[:14], refs[14], refs[16:]
    i = pl.program_id(0)
    rank = stash.shape[2]

    @pl.when(i == 0)
    def _():
        for acc in (proj, m0, by1, by2):
            acc[...] = jnp.zeros_like(acc)
        by1[:rank] = stash[0, 1]
        by2[:rank] = stash[0, 2]

    for g, u, d, d1, u2, b, a in (ins[0::2], ins[1::2]):
        two = b[...]
        proj[:rank] += nt(u[0, 0], g[...])
        proj[rank:] += nt(two, g[...])
        m0[...] += nt(two, d[0, 0])
        by1[rank:, :rank] += nt(b[:rank], d1[0, 0])
        by2[rank:, :rank] += nt(u2[0, 0], a[...])


def project(where, grad, adapter_down, adapter_up, b, b_sib, ahead, ahead_sib, stashed, after):
    tok, width = grad.shape
    rank = adapter_up.shape[2]
    each = ahead.shape[1] - width // 2
    grid = width // 2 // each
    mine, sib = (lambda w: w[CORE]), (lambda w: 1 - w[CORE])

    def half(span, side):
        return pl.BlockSpec(
            (1, 1, rank, each), lambda i, w: (span(w), 0, 0, side(w) * grid + i)
        )

    def weights(span):
        return [half(span, mine), half(span, sib)]

    g_spec = lambda side: pl.BlockSpec((tok, each), lambda i, w: (0, side(w) * grid + i))
    got = lambda skip: pl.BlockSpec((rank, each), lambda i, w: (0, i + skip))
    per = grid // 2
    quarter = pl.BlockSpec((2 * rank, each), lambda i, w: ((i // per + w[PAIR]) % 2, i % per))
    one = lambda w: 1
    shapes = ((3 * rank, tok), (2 * rank, rank), (2 * rank, tok), (2 * rank, tok))
    return call(
        project_kernel,
        where,
        (
            grad, grad, adapter_up, adapter_up, adapter_down, adapter_down,
            adapter_down, adapter_down, adapter_up, adapter_up,
            b, b_sib, ahead, ahead_sib, stashed, after,
        ),
        [g_spec(mine), g_spec(sib)]
        + weights(one)
        + weights(one)
        + weights(lambda w: w[B1])
        + weights(lambda w: w[B2])
        + [quarter] * 2
        + [got(1)] * 2
        + [pl.BlockSpec(stashed.shape, lambda i, w: (0, 0, 0, 0))]
        + [pl.BlockSpec(after.shape, lambda i, w: (0, 0))],
        [jax.ShapeDtypeStruct(shape, F32) for shape in shapes],
        [pl.BlockSpec(shape, lambda i, w: (0, 0)) for shape in shapes],
        (grid,),
    )


def back_kernel(where, proj, m0, by1, by2, q0, *rest):
    outs = rest[-3:]
    rank = m0.shape[1]

    def dz_of(grad_act, q):
        sigma = jax.nn.sigmoid(q)
        return (grad_act * sigma * (1.0 + q * (1.0 - sigma))).astype(BF16)

    def exact(m, d):
        return jnp.dot(
            m, d.astype(F32), precision=lax.Precision.HIGHEST, preferred_element_type=F32
        )

    m12 = jnp.where(where[SEC] == 0, by2[rank:, :rank], by1[rank:, :rank])
    dz0 = dz_of(proj[:rank], q0[0, 0])
    dz1 = dz_of(proj[rank:2 * rank] + exact(m0[:rank], dz0), by1[:rank])
    dz2 = dz_of(proj[2 * rank:] + exact(m0[rank:], dz0) + exact(m12, dz1), by2[:rank])
    for out, dz in zip(outs, (dz0, dz1, dz2)):
        out[...] = nt(dz, dz)


def back(where, proj, m0, by1, by2, stashed, after):
    rank = m0.shape[1]
    return local(
        back_kernel,
        where,
        (proj, m0, by1, by2, stashed),
        [jax.ShapeDtypeStruct((rank, rank), F32)] * 3,
        (),
        (after,),
    )


def merge_kernel(where, a, b, *rest):
    out, token = rest[-2:]
    out[...] = (a[...] + b[...].astype(F32)).astype(BF16)
    token[...] = jnp.zeros_like(token)


def merge(where, a, b, after):
    return local(
        merge_kernel, where, (a, b), [jax.ShapeDtypeStruct(a.shape, BF16), TOKEN], (), after
    )


def curvature_kernel(where, outer0, outer1, outer2, out, token):
    rank = outer0.shape[0]
    f1 = where[B1].astype(F32)
    f2 = where[B2].astype(F32)
    zero = outer1[...] * (1.0 - f1) + outer2[...] * (1.0 - f2)
    one = outer0[...] + outer1[...] * f1 + outer2[...] * f2
    both = jnp.concatenate([zero, one], axis=1)
    for k in range(out.shape[0]):
        out[k] = both
    token[...] = jnp.zeros_like(token)


def curvature(where, outers, replicas):
    rank = outers[0].shape[0]
    return local(
        curvature_kernel, where, outers,
        [jax.ShapeDtypeStruct((replicas, rank, 2 * rank), F32), TOKEN],
    )


def statistics_kernel(tokens, where, old, parts, after, out):
    rank = old.shape[2]
    total = parts[0]
    for k in range(1, parts.shape[0]):
        total = total + parts[k]
    later = where[B1] + where[B2]
    for span, held in enumerate((2 - later, 1 + later)):
        held = jnp.full((rank, rank), held.astype(F32), F32)
        was = old[span, 0]
        share = total[:, span * rank:(span + 1) * rank] / (jnp.maximum(held, 1.0) * tokens)
        out[span, 0] = jnp.where(held > 0.0, 0.75 * was + 0.25 * share, was)


def statistics(where, old, parts, tokens, after):
    return local(
        functools.partial(statistics_kernel, tokens),
        where,
        (old, parts),
        jax.ShapeDtypeStruct(old.shape, F32),
        (),
        (after,),
    )


def put_rows(factor_scale, old, out, buf, sems, first_col, pieces):
    hlf = buf.shape[0] // 2
    cols = pl.ds(pl.multiple_of(first_col, 2 * hlf), 2 * hlf)
    sent = []
    for i, values in enumerate(pieces):
        rows = pl.ds(i * hlf, hlf)
        at = 0
        for value in values():
            here = slice(at, at + value.shape[1])
            was = old[rows, pl.ds(pl.multiple_of(first_col + at, hlf), value.shape[1])]
            buf[rows, here] = 0.75 * was + factor_scale * value
            at += value.shape[1]
        copy = pltpu.make_async_copy(buf.at[rows], out.at[rows, cols], sems.at[i])
        copy.start()
        sent.append(copy)
    for copy in sent:
        copy.wait()


def add_kernel(cut, where, here, came, after, out):
    out[...] = here[:, cut:] + came[:, cut:].astype(F32)


def cross_part(where, here, came, after):
    hlf, width = here.shape
    cut = 3 * hlf
    return local(
        functools.partial(add_kernel, cut), where, (here, came),
        jax.ShapeDtypeStruct((hlf, width - cut), F32), (), (after,),
    )


def square_kernel(factor_scale, where, old, here, came, after, out, buf, sems):
    hlf = here.shape[0]
    rows = 2 * hlf

    def packed(lo, hi):
        return here[:, lo:hi] + came[:, lo:hi].astype(F32)

    put_rows(
        factor_scale, old, out, buf, sems, where[CORE] * rows,
        (
            lambda: [packed(0, hlf), packed(hlf, rows)],
            lambda: [packed(hlf, rows).T, packed(rows, rows + hlf)],
        ),
    )


def cross_kernel(factor_scale, where, old, mine, sib, done, out, token, buf, sems):
    core = where[CORE]
    hlf, rows = mine.shape

    def put(pieces):
        put_rows(factor_scale, old, out, buf, sems, (1 - core) * rows, pieces)

    @pl.when(core == 0)
    def _():
        put(tuple((lambda part=part: [part[:, :hlf], part[:, hlf:]]) for part in (mine, sib)))

    @pl.when(core == 1)
    def _():
        put(
            tuple(
                (lambda a=a: [sib[:, a:a + hlf].T, mine[:, a:a + hlf].T]) for a in (0, hlf)
            )
        )

    token[...] = jnp.zeros_like(token)


def update(factor_scale, where, old, here, came, mine, sib, after):
    total = old.shape[0]
    shape = jax.ShapeDtypeStruct(old.shape, F32)
    scratch = [pltpu.VMEM((total, total), F32), pltpu.SemaphoreType.DMA((2,))]
    vmem = pl.BlockSpec(memory_space=pltpu.VMEM)
    done = local(
        functools.partial(square_kernel, factor_scale), where, (old, here, came), shape, scratch,
        (after,), out_specs=ANY,
    )
    return pl.pallas_call(
        functools.partial(cross_kernel, factor_scale),
        in_specs=[pl.BlockSpec(memory_space=pltpu.SMEM)] + [vmem] * 3 + [ANY],
        out_specs=[ANY, vmem],
        out_shape=[shape, TOKEN],
        scratch_shapes=scratch,
        input_output_aliases={4: 0},
        compiler_params=pltpu.CompilerParams(vmem_limit_bytes=24 << 20),
        cost_estimate=pl.CostEstimate(flops=0, transcendentals=0, bytes_accessed=0),
    )(where, old, mine, sib, done)


def shards(
    entering, returning, adapter_down, adapter_up, stashed, doc_ids, input_factor, output_factor
):
    sec = lax.axis_index("section")
    rep = lax.axis_index("dp")
    sections = lax.axis_size("section")
    replicas = lax.axis_size("dp")
    tok = entering.shape[1]
    steps_count = stashed.shape[1]
    rank = stashed.shape[2]
    rows, block = input_factor.shape[1:]
    tokens = tok * replicas

    def first(home):
        return (home < sections // 2).astype(jnp.int32)

    x0 = entering[0]
    f1 = first((sec + sections - 1) % sections) + (sec == 0).astype(jnp.int32)
    b1 = (sec + 1 < sections).astype(jnp.int32)
    b2 = (sec + 2 < sections).astype(jnp.int32)
    where = jnp.stack(
        [rep // 2, rep % 2, sec, first(sec), f1, b1, b2, rep // 4 % 2]
    ).astype(jnp.int32)

    with jax.named_scope("weights"):
        pieces, gate0 = split(where, x0, adapter_down, doc_ids, replicas, 8)
        ahead, behind1, behind2 = pack(where, adapter_down, adapter_up, block, gate0)
        ahead = shift(ahead, "section", -1)
        behind1 = shift(behind1, "section", 1)
        behind2 = shift(behind2, "section", 2)
        x1, up_own, up_oth, token5 = next_activation(where, x0, adapter_up, gate0, rows)
        ahead = tie(ahead, behind1, behind2, token5, space=pltpu.VMEM)
        ahead_sib = swap_cores(ahead)
        behind = join(where, behind1, behind2)
        behind_pair = swap_chips(behind)

    with jax.named_scope("gates"):
        sent = gates(where, x1, ahead, ahead_sib, gate0, replicas, behind)

    with jax.named_scope("columns"):
        own = tie(lax.all_to_all(pieces, "dp", 0, 0), sent, space=pltpu.VMEM)
        other = swap_cores(own)
        got = lax.all_to_all(sent, "dp", 0, 0)

    with jax.named_scope("factor"):
        ups = (got, up_own, up_oth, ahead)
        step0, token0 = gram(0, where, own, other)
        step2, token2 = gram(2, where, own, other, ups, (token0,))
        from2 = shift(step2, "section", 1)

    with jax.named_scope("backward"):
        behind = join(where, behind, behind_pair, (token0,))
        behind_sib = swap_cores(behind)
        proj, m0, by1, by2 = project(
            where, returning[0], adapter_down, adapter_up, behind, behind_sib, ahead, ahead_sib,
            stashed, token2,
        )
        by1 = shift(by1, "section", 1)
        by2 = shift(by2, "section", 2)

    with jax.named_scope("factor"):
        step1, token1 = gram(1, where, own, other, ups, (m0,))
        from1, token3 = merge(where, step1, from2, (token1, by1, by2))
        from1 = shift(from1, "section", 1)

    with jax.named_scope("backward"):
        outer0, outer1, outer2 = back(where, proj, m0, by1, by2, stashed, token3)
        outer1 = shift(outer1, "section", -1)
        outer2 = shift(outer2, "section", -2)
        share, token4 = curvature(where, (outer0, outer1, outer2), replicas)
        shares = lax.all_to_all(share, "dp", 0, 0)

    with jax.named_scope("factor"):
        mine = cross_part(where, step0, from1, shares)
        sib = swap_cores(mine)
        factor_scale = 0.25 / (steps_count * tokens)
        input_factor_new, last = update(
            factor_scale, where, input_factor[0], step0, from1, mine, sib, token4
        )

    with jax.named_scope("backward"):
        output_factor_new = statistics(where, output_factor, shares, tokens, last)
    return (input_factor_new[None], output_factor_new)


def solution(mesh):
    in_specs = (
        P("section", "dp", None),
        P("section", "dp", None),
        P(None, "section", None, None),
        P(None, "section", None, None),
        P("section", None, None, "dp"),
        P(None, "dp"),
        P("section", "dp", None),
        P(None, "section", None, None),
    )
    out_specs = (P("section", "dp", None), P(None, "section", None, None))
    return jax.shard_map(shards, mesh=mesh, in_specs=in_specs, out_specs=out_specs, check_vma=False)
```

```python
import functools

import jax
import jax.numpy as jnp
from jax import lax
from jax.experimental import pallas as pl
from jax.experimental.pallas import tpu as pltpu
from jax.sharding import PartitionSpec as P

F32 = jnp.float32
BF16 = jnp.bfloat16
ANY = pl.BlockSpec(memory_space=pl.ANY)
TOKEN = jax.ShapeDtypeStruct((8, 128), F32)


def shift(block, axis, distance):
    count = lax.axis_size(axis)
    return lax.ppermute(block, axis, [(i, (i + distance) % count) for i in range(count)])


def swap_cores(block):
    count = lax.axis_size("dp")
    return lax.ppermute(block, "dp", [(i, i ^ 1) for i in range(count)])


def swap_chips(block):
    count = lax.axis_size("dp")
    return lax.ppermute(block, "dp", [(i, i ^ 4) for i in range(count)])


def nt(a, b):
    return lax.dot_general(a, b, (((1,), (1,)), ((), ())), preferred_element_type=F32)


def tn(a, b):
    return lax.dot_general(a, b, (((0,), (0,)), ((), ())), preferred_element_type=F32)


def call(kernel, where, operands, in_specs, outs, out_specs, grid, scratch=(), aliases={}):
    spec = pltpu.PrefetchScalarGridSpec(
        num_scalar_prefetch=1,
        grid=grid,
        in_specs=in_specs,
        out_specs=out_specs,
        scratch_shapes=list(scratch),
    )
    return pl.pallas_call(
        kernel,
        grid_spec=spec,
        out_shape=outs,
        input_output_aliases=aliases,
        compiler_params=pltpu.CompilerParams(dimension_semantics=("arbitrary",) * len(grid)),
        cost_estimate=pl.CostEstimate(flops=0, transcendentals=0, bytes_accessed=0),
    )(where, *operands)


def tie_kernel(x, *rest):
    del x, rest


def tie(x, *after, space=pltpu.HBM):
    spec = pl.BlockSpec(memory_space=space)
    return pl.pallas_call(
        tie_kernel,
        in_specs=[spec] + [ANY] * len(after),
        out_specs=spec,
        out_shape=jax.ShapeDtypeStruct(x.shape, x.dtype),
        input_output_aliases={0: 0},
        compiler_params=pltpu.CompilerParams(vmem_limit_bytes=8 << 20),
        cost_estimate=pl.CostEstimate(flops=0, transcendentals=0, bytes_accessed=0),
    )(x, *after)


CHIP, CORE, SEC, C0, F1, B1, B2, PAIR = range(8)


def split_kernel(where, x, down, ids, out, gate, acc):
    i = pl.program_id(0)
    pieces, _, cols = out.shape
    tok, rank = gate.shape

    @pl.when(i == 0)
    def _():
        acc[...] = jnp.zeros_like(acc)

    acc[...] += nt(x[...], down[0, 0])
    row = ids[pl.ds(where[SEC], 1), :].astype(F32)
    row = jnp.broadcast_to(row, (out.shape[1] - tok, tok)).astype(BF16)
    for k in range(pieces):
        out[k, :tok, :] = x[:, k * cols:(k + 1) * cols]
        out[k, tok:, :tok] = row
        out[k, tok:, tok:] = jnp.zeros((out.shape[1] - tok, cols - tok), BF16)

    @pl.when(i == pl.num_programs(0) - 1)
    def _():
        z = acc[...]
        gate[...] = (z * jax.nn.sigmoid(z)).astype(BF16)


def split(where, x, adapter_down, doc_ids, pieces, extra):
    tok, width = x.shape
    rank = adapter_down.shape[2]
    cols = width // pieces
    grid = 4
    each = width // grid
    return call(
        split_kernel,
        where,
        (x, adapter_down, doc_ids),
        [
            pl.BlockSpec((tok, each), lambda i, w: (0, i)),
            pl.BlockSpec((1, 1, rank, each), lambda i, w: (w[C0], 0, 0, i)),
            pl.BlockSpec(doc_ids.shape, lambda i, w: (0, 0)),
        ],
        [
            jax.ShapeDtypeStruct((pieces, tok + extra, cols), BF16),
            jax.ShapeDtypeStruct((tok, rank), BF16),
        ],
        [
            pl.BlockSpec((pieces // grid, tok + extra, cols), lambda i, w: (i, 0, 0)),
            pl.BlockSpec((tok, rank), lambda i, w: (0, 0)),
        ],
        (grid,),
        [pltpu.VMEM((tok, rank), F32)],
    )


def pack_kernel(where, up_f, down_f, up_b1, up_b2, after, ahead, behind1, behind2):
    half = down_f.shape[3]
    ahead[:, :half] = down_f[0, 0]
    ahead[:, half:] = up_f[0, 0]
    behind1[...] = up_b1[0, 0]
    behind2[...] = up_b2[0, 0]


def pack(where, adapter_down, adapter_up, rows, after):
    rank, width = adapter_down.shape[2:]
    half = width // 2
    part = lambda span: pl.BlockSpec(
        (1, 1, rank, half // 2), lambda i, w: (w[span], 0, 0, 2 * w[CORE] + w[PAIR])
    )
    shapes = ((rank, half + rows), (rank, half // 2), (rank, half // 2))
    return call(
        pack_kernel,
        where,
        (adapter_up, adapter_down, adapter_up, adapter_up, after),
        [
            pl.BlockSpec((1, 1, rank, rows), lambda i, w: (w[F1], 0, 0, 2 * w[CHIP] + w[CORE])),
            pl.BlockSpec((1, 1, rank, half), lambda i, w: (w[F1], 0, 0, w[CORE])),
            part(B1),
            part(B2),
            pl.BlockSpec(after.shape, lambda i, w: (0, 0)),
        ],
        [jax.ShapeDtypeStruct(shape, BF16) for shape in shapes],
        [pl.BlockSpec(shape, lambda i, w: (0, 0)) for shape in shapes],
        (1,),
    )


def ahead_kernel(where, x, up, gate0, u0o, u0s, x1, own, oth, token):
    add = jnp.dot(gate0[...], up[0, 0], preferred_element_type=F32)
    x1[...] = (x[...].astype(F32) + add).astype(BF16)

    @pl.when(pl.program_id(0) == 0)
    def _():
        own[...] = u0o[0, 0]
        oth[...] = u0s[0, 0]
        token[...] = jnp.zeros_like(token)


def next_activation(where, x, adapter_up, gate0, rows):
    tok, width = x.shape
    rank = gate0.shape[1]
    grid = 4
    each = width // grid
    u0 = lambda side: pl.BlockSpec(
        (1, 1, rank, rows), lambda i, w: (w[C0], 0, 0, 2 * w[CHIP] + side(w))
    )
    one = lambda shape: pl.BlockSpec(shape, lambda i, w: (0, 0))
    return call(
        ahead_kernel,
        where,
        (x, adapter_up, gate0, adapter_up, adapter_up),
        [
            pl.BlockSpec((tok, each), lambda i, w: (0, i)),
            pl.BlockSpec((1, 1, rank, each), lambda i, w: (w[C0], 0, 0, i)),
            one((tok, rank)),
            u0(lambda w: w[CORE]),
            u0(lambda w: 1 - w[CORE]),
        ],
        [
            jax.ShapeDtypeStruct((tok, width), BF16),
            jax.ShapeDtypeStruct((rank, rows), BF16),
            jax.ShapeDtypeStruct((rank, rows), BF16),
            TOKEN,
        ],
        [
            pl.BlockSpec((tok, each), lambda i, w: (0, i)),
            one((rank, rows)),
            one((rank, rows)),
            one(TOKEN.shape),
        ],
        (grid,),
    )


def gate_kernel(where, x1, mine, sib, gate0, after, sent):
    core = where[CORE]
    half = x1.shape[1] // 2
    z = nt(x1[:, pl.ds(pl.multiple_of(core * half, half), half)], mine[:, :half])
    z += nt(x1[:, pl.ds(pl.multiple_of((1 - core) * half, half), half)], sib[:, :half])
    gate1 = (z * jax.nn.sigmoid(z)).astype(BF16)
    both = jnp.concatenate([gate0[...], gate1], axis=1)
    for k in range(sent.shape[0]):
        sent[k] = both


def gates(where, x1, ahead_mine, ahead_sib, gate0, replicas, after):
    tok, rank = gate0.shape
    return local(
        gate_kernel,
        where,
        (x1, ahead_mine, ahead_sib, gate0),
        jax.ShapeDtypeStruct((replicas, tok, 2 * rank), BF16),
        (),
        (after,),
    )


def local(kernel, where, operands, outs, scratch=(), after=(), aliases={}, out_specs=None):
    vmem = pl.BlockSpec(memory_space=pltpu.VMEM)
    out_vmem = [vmem] * len(outs) if isinstance(outs, list) else vmem
    return pl.pallas_call(
        kernel,
        in_specs=[pl.BlockSpec(memory_space=pltpu.SMEM)]
        + [vmem] * len(operands)
        + [vmem] * len(after),
        out_specs=out_specs or out_vmem,
        out_shape=outs,
        scratch_shapes=list(scratch),
        input_output_aliases=aliases,
        compiler_params=pltpu.CompilerParams(vmem_limit_bytes=24 << 20),
        cost_estimate=pl.CostEstimate(flops=0, transcendentals=0, bytes_accessed=0),
    )(where, *operands, *after)


def join_kernel(where, a, b, *rest):
    out = rest[-1]
    out[:a.shape[0]] = a[...]
    out[a.shape[0]:] = b[...]


def join(where, a, b, after=()):
    shape = (a.shape[0] + b.shape[0], a.shape[1])
    return local(
        join_kernel, where, (a, b), jax.ShapeDtypeStruct(shape, a.dtype), (), after
    )


def scale_columns(own, tok):
    replicas = own.shape[0]
    ids = [own[k, tok:tok + 1, :tok].astype(F32) for k in range(replicas)]
    doc = lax.broadcasted_iota(jnp.int32, (2 * replicas, tok), 0).astype(F32)
    hits = jnp.zeros((2 * replicas, tok), F32)
    for row in ids:
        hits += (doc == row).astype(F32)
    count = jnp.maximum(jnp.sum(hits, axis=1, keepdims=True), 1.0)
    table = jnp.sqrt(jnp.sqrt(tok / count))
    scales = [jnp.sum(jnp.where(doc == row, table, 0.0), axis=0, keepdims=True) for row in ids]
    return jnp.concatenate(scales + [jnp.zeros((tok - replicas, tok), F32)], axis=0).T


def gram_kernel(step, where, own, other, *rest):
    core = where[CORE]
    replicas, long, rows = own.shape
    if step:
        got, up_own, up_oth, ahead, ahead_sib = rest[:5]
        ups_own, ups_oth = up_own[...], up_oth[...]
    if step == 2:
        ups_own = jnp.concatenate([ups_own, ahead[:, ahead.shape[1] - rows:]], axis=0)
        ups_oth = jnp.concatenate([ups_oth, ahead_sib[:, ahead.shape[1] - rows:]], axis=0)
    rest = rest[5 if step else 0:]
    tok = long - 8
    hlf = rows // 2
    per = 4
    if step == 2:
        out, token, acc = rest[-3:]
    else:
        acc, token = rest[-2:]
    columns = scale_columns(own, tok)

    for i in range(replicas // per):
        ks = range(i * per, (i + 1) * per)

        def rebuilt(ref, ups):
            act = jnp.concatenate([ref[k, :tok, :] for k in ks], axis=0).astype(F32)
            if step:
                gate = jnp.concatenate([got[k] for k in ks], axis=0)[:, :ups.shape[0]]
                add = jnp.dot(gate, ups, preferred_element_type=F32)
                act = act + add
            scale = [jnp.broadcast_to(columns[:, k:k + 1], (tok, rows)) for k in ks]
            return (jnp.concatenate(scale, axis=0) * act).astype(BF16)

        def put(lo, val):
            hi = lo + val.shape[1]
            acc[:, lo:hi] = val if i == 0 else acc[:, lo:hi] + val

        r = rebuilt(own, ups_own if step else None)
        q = rebuilt(other, ups_oth if step else None)
        put(0, tn(r[:, :hlf], r))
        put(rows, tn(r[:, hlf:], r[:, hlf:]))

        @pl.when(core == 0)
        def _():
            put(rows + hlf, tn(r[:, :hlf], q))

        @pl.when(core == 1)
        def _():
            put(rows + hlf, tn(q[:, hlf:], r))

    token[...] = jnp.zeros_like(token)
    if step == 2:
        out[...] = acc[...].astype(BF16)


def gram(step, where, own, other, ups=(), after=()):
    rows = own.shape[2]
    packed = (rows // 2, rows * 5 // 2)
    return local(
        functools.partial(gram_kernel, step),
        where,
        (own, other, *ups),
        [jax.ShapeDtypeStruct(packed, BF16 if step == 2 else F32), TOKEN],
        [pltpu.VMEM(packed, F32)] if step == 2 else [],
        after,
    )


def project_kernel(where, *refs):
    ins, stash, (proj, m0, by1, by2) = refs[:14], refs[14], refs[16:]
    i = pl.program_id(0)
    rank = stash.shape[2]

    @pl.when(i == 0)
    def _():
        for acc in (proj, m0, by1, by2):
            acc[...] = jnp.zeros_like(acc)
        by1[:rank] = stash[0, 1]
        by2[:rank] = stash[0, 2]

    for g, u, d, d1, u2, b, a in (ins[0::2], ins[1::2]):
        two = b[...]
        proj[:rank] += nt(u[0, 0], g[...])
        proj[rank:] += nt(two, g[...])
        m0[...] += nt(two, d[0, 0])
        by1[rank:, :rank] += nt(b[:rank], d1[0, 0])
        by2[rank:, :rank] += nt(u2[0, 0], a[...])


def project(where, grad, adapter_down, adapter_up, b, b_sib, ahead, ahead_sib, stashed, after):
    tok, width = grad.shape
    rank = adapter_up.shape[2]
    grid = 4
    each = width // 2 // grid
    mine, sib = (lambda w: w[CORE]), (lambda w: 1 - w[CORE])

    def half(span, side):
        return pl.BlockSpec(
            (1, 1, rank, each), lambda i, w: (span(w), 0, 0, side(w) * grid + i)
        )

    def weights(span):
        return [half(span, mine), half(span, sib)]

    g_spec = lambda side: pl.BlockSpec((tok, each), lambda i, w: (0, side(w) * grid + i))
    got = pl.BlockSpec((rank, each), lambda i, w: (0, i))
    per = grid // 2
    quarter = pl.BlockSpec((2 * rank, each), lambda i, w: ((i // per + w[PAIR]) % 2, i % per))
    one = lambda w: 1
    shapes = ((3 * rank, tok), (2 * rank, rank), (2 * rank, tok), (2 * rank, tok))
    return call(
        project_kernel,
        where,
        (
            grad, grad, adapter_up, adapter_up, adapter_down, adapter_down,
            adapter_down, adapter_down, adapter_up, adapter_up,
            b, b_sib, ahead, ahead_sib, stashed, after,
        ),
        [g_spec(mine), g_spec(sib)]
        + weights(one)
        + weights(one)
        + weights(lambda w: w[B1])
        + weights(lambda w: w[B2])
        + [quarter] * 2
        + [got] * 2
        + [pl.BlockSpec(stashed.shape, lambda i, w: (0, 0, 0, 0))]
        + [pl.BlockSpec(after.shape, lambda i, w: (0, 0))],
        [jax.ShapeDtypeStruct(shape, F32) for shape in shapes],
        [pl.BlockSpec(shape, lambda i, w: (0, 0)) for shape in shapes],
        (grid,),
    )


def back_kernel(where, proj, m0, by1, by2, q0, *rest):
    outs = rest[-3:]
    rank = m0.shape[1]

    def dz_of(grad_act, q):
        sigma = jax.nn.sigmoid(q)
        return (grad_act * sigma * (1.0 + q * (1.0 - sigma))).astype(BF16)

    def exact(m, d):
        return jnp.dot(
            m, d.astype(F32), precision=lax.Precision.HIGHEST, preferred_element_type=F32
        )

    m12 = jnp.where(where[SEC] == 0, by2[rank:, :rank], by1[rank:, :rank])
    dz0 = dz_of(proj[:rank], q0[0, 0])
    dz1 = dz_of(proj[rank:2 * rank] + exact(m0[:rank], dz0), by1[:rank])
    dz2 = dz_of(proj[2 * rank:] + exact(m0[rank:], dz0) + exact(m12, dz1), by2[:rank])
    for out, dz in zip(outs, (dz0, dz1, dz2)):
        out[...] = nt(dz, dz)


def back(where, proj, m0, by1, by2, stashed, after):
    rank = m0.shape[1]
    return local(
        back_kernel,
        where,
        (proj, m0, by1, by2, stashed),
        [jax.ShapeDtypeStruct((rank, rank), F32)] * 3,
        (),
        (after,),
    )


def merge_kernel(where, a, b, *rest):
    out, token = rest[-2:]
    out[...] = (a[...] + b[...].astype(F32)).astype(BF16)
    token[...] = jnp.zeros_like(token)


def merge(where, a, b, after):
    return local(
        merge_kernel, where, (a, b), [jax.ShapeDtypeStruct(a.shape, BF16), TOKEN], (), after
    )


def curvature_kernel(where, outer0, outer1, outer2, out, token):
    rank = outer0.shape[0]
    f1 = where[B1].astype(F32)
    f2 = where[B2].astype(F32)
    zero = outer1[...] * (1.0 - f1) + outer2[...] * (1.0 - f2)
    one = outer0[...] + outer1[...] * f1 + outer2[...] * f2
    both = jnp.concatenate([zero, one], axis=1)
    for k in range(out.shape[0]):
        out[k] = both
    token[...] = jnp.zeros_like(token)


def curvature(where, outers, replicas):
    rank = outers[0].shape[0]
    return local(
        curvature_kernel, where, outers,
        [jax.ShapeDtypeStruct((replicas, rank, 2 * rank), F32), TOKEN],
    )


def statistics_kernel(tokens, where, old, parts, after, out):
    rank = old.shape[2]
    total = parts[0]
    for k in range(1, parts.shape[0]):
        total = total + parts[k]
    later = where[B1] + where[B2]
    for span, held in enumerate((2 - later, 1 + later)):
        held = jnp.full((rank, rank), held.astype(F32), F32)
        was = old[span, 0]
        share = total[:, span * rank:(span + 1) * rank] / (jnp.maximum(held, 1.0) * tokens)
        out[span, 0] = jnp.where(held > 0.0, 0.75 * was + 0.25 * share, was)


def statistics(where, old, parts, tokens, after):
    return local(
        functools.partial(statistics_kernel, tokens),
        where,
        (old, parts),
        jax.ShapeDtypeStruct(old.shape, F32),
        (),
        (after,),
    )


def put_rows(factor_scale, old, out, buf, sems, first_col, pieces):
    hlf = buf.shape[0] // 2
    cols = pl.ds(pl.multiple_of(first_col, 2 * hlf), 2 * hlf)
    sent = []
    for i, values in enumerate(pieces):
        rows = pl.ds(i * hlf, hlf)
        at = 0
        for value in values():
            here = slice(at, at + value.shape[1])
            was = old[rows, pl.ds(pl.multiple_of(first_col + at, hlf), value.shape[1])]
            buf[rows, here] = 0.75 * was + factor_scale * value
            at += value.shape[1]
        copy = pltpu.make_async_copy(buf.at[rows], out.at[rows, cols], sems.at[i])
        copy.start()
        sent.append(copy)
    for copy in sent:
        copy.wait()


def add_kernel(cut, where, here, came, after, out):
    out[...] = here[:, cut:] + came[:, cut:].astype(F32)


def cross_part(where, here, came, after):
    hlf, width = here.shape
    cut = 3 * hlf
    return local(
        functools.partial(add_kernel, cut), where, (here, came),
        jax.ShapeDtypeStruct((hlf, width - cut), F32), (), (after,),
    )


def square_kernel(factor_scale, where, old, here, came, after, out, buf, sems):
    hlf = here.shape[0]
    rows = 2 * hlf

    def packed(lo, hi):
        return here[:, lo:hi] + came[:, lo:hi].astype(F32)

    put_rows(
        factor_scale, old, out, buf, sems, where[CORE] * rows,
        (
            lambda: [packed(0, hlf), packed(hlf, rows)],
            lambda: [packed(hlf, rows).T, packed(rows, rows + hlf)],
        ),
    )


def cross_kernel(factor_scale, where, old, mine, sib, done, out, token, buf, sems):
    core = where[CORE]
    hlf, rows = mine.shape

    def put(pieces):
        put_rows(factor_scale, old, out, buf, sems, (1 - core) * rows, pieces)

    @pl.when(core == 0)
    def _():
        put(tuple((lambda part=part: [part[:, :hlf], part[:, hlf:]]) for part in (mine, sib)))

    @pl.when(core == 1)
    def _():
        put(
            tuple(
                (lambda a=a: [sib[:, a:a + hlf].T, mine[:, a:a + hlf].T]) for a in (0, hlf)
            )
        )

    token[...] = jnp.zeros_like(token)


def update(factor_scale, where, old, here, came, mine, sib, after):
    total = old.shape[0]
    shape = jax.ShapeDtypeStruct(old.shape, F32)
    scratch = [pltpu.VMEM((total, total), F32), pltpu.SemaphoreType.DMA((2,))]
    vmem = pl.BlockSpec(memory_space=pltpu.VMEM)
    done = local(
        functools.partial(square_kernel, factor_scale), where, (old, here, came), shape, scratch,
        (after,), out_specs=ANY,
    )
    return pl.pallas_call(
        functools.partial(cross_kernel, factor_scale),
        in_specs=[pl.BlockSpec(memory_space=pltpu.SMEM)] + [vmem] * 3 + [ANY],
        out_specs=[ANY, vmem],
        out_shape=[shape, TOKEN],
        scratch_shapes=scratch,
        input_output_aliases={4: 0},
        compiler_params=pltpu.CompilerParams(vmem_limit_bytes=24 << 20),
        cost_estimate=pl.CostEstimate(flops=0, transcendentals=0, bytes_accessed=0),
    )(where, old, mine, sib, done)


def shards(
    entering, returning, adapter_down, adapter_up, stashed, doc_ids, input_factor, output_factor
):
    sec = lax.axis_index("section")
    rep = lax.axis_index("dp")
    sections = lax.axis_size("section")
    replicas = lax.axis_size("dp")
    tok = entering.shape[1]
    steps_count = stashed.shape[1]
    rank = stashed.shape[2]
    rows, block = input_factor.shape[1:]
    tokens = tok * replicas

    def first(home):
        return (home < sections // 2).astype(jnp.int32)

    x0 = entering[0]
    f1 = first((sec + sections - 1) % sections) + (sec == 0).astype(jnp.int32)
    b1 = (sec + 1 < sections).astype(jnp.int32)
    b2 = (sec + 2 < sections).astype(jnp.int32)
    where = jnp.stack(
        [rep // 2, rep % 2, sec, first(sec), f1, b1, b2, rep // 4 % 2]
    ).astype(jnp.int32)

    with jax.named_scope("weights"):
        pieces, gate0 = split(where, x0, adapter_down, doc_ids, replicas, 8)
        ahead, behind1, behind2 = pack(where, adapter_down, adapter_up, rows, gate0)
        ahead = shift(ahead, "section", -1)
        behind1 = shift(behind1, "section", 1)
        behind2 = shift(behind2, "section", 2)
        x1, up_own, up_oth, token5 = next_activation(where, x0, adapter_up, gate0, rows)
        ahead = tie(ahead, behind1, behind2, token5, space=pltpu.VMEM)
        ahead_sib = swap_cores(ahead)
        behind = join(where, behind1, behind2)
        behind_pair = swap_chips(behind)

    with jax.named_scope("gates"):
        sent = gates(where, x1, ahead, ahead_sib, gate0, replicas, behind)

    with jax.named_scope("columns"):
        own = tie(lax.all_to_all(pieces, "dp", 0, 0), sent, space=pltpu.VMEM)
        other = swap_cores(own)
        got = lax.all_to_all(sent, "dp", 0, 0)

    with jax.named_scope("factor"):
        ups = (got, up_own, up_oth, ahead, ahead_sib)
        step0, token0 = gram(0, where, own, other)
        step2, token2 = gram(2, where, own, other, ups, (token0,))
        from2 = shift(step2, "section", 1)

    with jax.named_scope("backward"):
        behind = join(where, behind, behind_pair, (token0,))
        behind_sib = swap_cores(behind)
        proj, m0, by1, by2 = project(
            where, returning[0], adapter_down, adapter_up, behind, behind_sib, ahead, ahead_sib,
            stashed, token2,
        )
        by1 = shift(by1, "section", 1)
        by2 = shift(by2, "section", 2)

    with jax.named_scope("factor"):
        step1, token1 = gram(1, where, own, other, ups, (m0,))
        from1, token3 = merge(where, step1, from2, (token1, by1, by2))
        from1 = shift(from1, "section", 1)

    with jax.named_scope("backward"):
        outer0, outer1, outer2 = back(where, proj, m0, by1, by2, stashed, token3)
        outer1 = shift(outer1, "section", -1)
        outer2 = shift(outer2, "section", -2)
        share, token4 = curvature(where, (outer0, outer1, outer2), replicas)
        shares = lax.all_to_all(share, "dp", 0, 0)

    with jax.named_scope("factor"):
        mine = cross_part(where, step0, from1, shares)
        sib = swap_cores(mine)
        factor_scale = 0.25 / (steps_count * tokens)
        input_factor_new, last = update(
            factor_scale, where, input_factor[0], step0, from1, mine, sib, token4
        )

    with jax.named_scope("backward"):
        output_factor_new = statistics(where, output_factor, shares, tokens, last)
    return (input_factor_new[None], output_factor_new)


def solution(mesh):
    in_specs = (
        P("section", "dp", None),
        P("section", "dp", None),
        P(None, "section", None, None),
        P(None, "section", None, None),
        P("section", None, None, "dp"),
        P(None, "dp"),
        P("section", "dp", None),
        P(None, "section", None, None),
    )
    out_specs = (P("section", "dp", None), P(None, "section", None, None))
    return jax.shard_map(shards, mesh=mesh, in_specs=in_specs, out_specs=out_specs, check_vma=False)
```

```python
import functools

import jax
import jax.numpy as jnp
from jax import lax
from jax.experimental import pallas as pl
from jax.experimental.pallas import tpu as pltpu
from jax.sharding import PartitionSpec as P

F32 = jnp.float32
BF16 = jnp.bfloat16
ANY = pl.BlockSpec(memory_space=pl.ANY)
TOKEN = jax.ShapeDtypeStruct((8, 128), F32)


def shift(block, axis, distance):
    count = lax.axis_size(axis)
    return lax.ppermute(block, axis, [(i, (i + distance) % count) for i in range(count)])


def swap_cores(block):
    count = lax.axis_size("dp")
    return lax.ppermute(block, "dp", [(i, i ^ 1) for i in range(count)])


def swap_chips(block):
    count = lax.axis_size("dp")
    return lax.ppermute(block, "dp", [(i, i ^ 4) for i in range(count)])


def nt(a, b):
    return lax.dot_general(a, b, (((1,), (1,)), ((), ())), preferred_element_type=F32)


def tn(a, b):
    return lax.dot_general(a, b, (((0,), (0,)), ((), ())), preferred_element_type=F32)


def call(kernel, where, operands, in_specs, outs, out_specs, grid, scratch=(), aliases={}):
    spec = pltpu.PrefetchScalarGridSpec(
        num_scalar_prefetch=1,
        grid=grid,
        in_specs=in_specs,
        out_specs=out_specs,
        scratch_shapes=list(scratch),
    )
    return pl.pallas_call(
        kernel,
        grid_spec=spec,
        out_shape=outs,
        input_output_aliases=aliases,
        compiler_params=pltpu.CompilerParams(dimension_semantics=("arbitrary",) * len(grid)),
        cost_estimate=pl.CostEstimate(flops=0, transcendentals=0, bytes_accessed=0),
    )(where, *operands)


def tie_kernel(x, *rest):
    del x, rest


def tie(x, *after, space=pltpu.HBM):
    spec = pl.BlockSpec(memory_space=space)
    return pl.pallas_call(
        tie_kernel,
        in_specs=[spec] + [ANY] * len(after),
        out_specs=spec,
        out_shape=jax.ShapeDtypeStruct(x.shape, x.dtype),
        input_output_aliases={0: 0},
        compiler_params=pltpu.CompilerParams(vmem_limit_bytes=8 << 20),
        cost_estimate=pl.CostEstimate(flops=0, transcendentals=0, bytes_accessed=0),
    )(x, *after)


CHIP, CORE, SEC, C0, F1, B1, B2, PAIR = range(8)


def split_kernel(where, x, down, ids, out, gate, acc):
    i = pl.program_id(0)
    pieces, _, cols = out.shape
    tok, rank = gate.shape

    @pl.when(i == 0)
    def _():
        acc[...] = jnp.zeros_like(acc)

    acc[...] += nt(x[...], down[0, 0])
    row = ids[pl.ds(where[SEC], 1), :].astype(F32)
    row = jnp.broadcast_to(row, (out.shape[1] - tok, tok)).astype(BF16)
    for k in range(pieces):
        out[k, :tok, :] = x[:, k * cols:(k + 1) * cols]
        out[k, tok:, :tok] = row
        out[k, tok:, tok:] = jnp.zeros((out.shape[1] - tok, cols - tok), BF16)

    @pl.when(i == pl.num_programs(0) - 1)
    def _():
        z = acc[...]
        gate[...] = (z * jax.nn.sigmoid(z)).astype(BF16)


def split(where, x, adapter_down, doc_ids, pieces, extra):
    tok, width = x.shape
    rank = adapter_down.shape[2]
    cols = width // pieces
    grid = 2
    each = width // grid
    return call(
        split_kernel,
        where,
        (x, adapter_down, doc_ids),
        [
            pl.BlockSpec((tok, each), lambda i, w: (0, i)),
            pl.BlockSpec((1, 1, rank, each), lambda i, w: (w[C0], 0, 0, i)),
            pl.BlockSpec(doc_ids.shape, lambda i, w: (0, 0)),
        ],
        [
            jax.ShapeDtypeStruct((pieces, tok + extra, cols), BF16),
            jax.ShapeDtypeStruct((tok, rank), BF16),
        ],
        [
            pl.BlockSpec((pieces // grid, tok + extra, cols), lambda i, w: (i, 0, 0)),
            pl.BlockSpec((tok, rank), lambda i, w: (0, 0)),
        ],
        (grid,),
        [pltpu.VMEM((tok, rank), F32)],
    )


def pack_kernel(where, up_f, down_f, up_b1, up_b2, after, ahead, behind1, behind2):
    cols = up_f.shape[3]
    ahead[:, :cols] = up_f[0, 0]
    ahead[:, cols:] = down_f[0, 0]
    behind1[...] = up_b1[0, 0]
    behind2[...] = up_b2[0, 0]


def pack(where, adapter_down, adapter_up, block, after):
    rank, width = adapter_down.shape[2:]
    half = width // 2
    part = lambda span: pl.BlockSpec(
        (1, 1, rank, half // 2), lambda i, w: (w[span], 0, 0, 2 * w[CORE] + w[PAIR])
    )
    shapes = ((rank, block + half), (rank, half // 2), (rank, half // 2))
    return call(
        pack_kernel,
        where,
        (adapter_up, adapter_down, adapter_up, adapter_up, after),
        [
            pl.BlockSpec((1, 1, rank, block), lambda i, w: (w[F1], 0, 0, w[CHIP])),
            pl.BlockSpec((1, 1, rank, half), lambda i, w: (w[F1], 0, 0, w[CORE])),
            part(B1),
            part(B2),
            pl.BlockSpec(after.shape, lambda i, w: (0, 0)),
        ],
        [jax.ShapeDtypeStruct(shape, BF16) for shape in shapes],
        [pl.BlockSpec(shape, lambda i, w: (0, 0)) for shape in shapes],
        (1,),
    )


def ahead_kernel(where, x, up, gate0, u0o, u0s, x1, own, oth, token):
    add = jnp.dot(gate0[...], up[0, 0], preferred_element_type=F32)
    x1[...] = (x[...].astype(F32) + add).astype(BF16)

    @pl.when(pl.program_id(0) == 0)
    def _():
        own[...] = u0o[0, 0]
        oth[...] = u0s[0, 0]
        token[...] = jnp.zeros_like(token)


def next_activation(where, x, adapter_up, gate0, rows):
    tok, width = x.shape
    rank = gate0.shape[1]
    grid = 4
    each = width // grid
    u0 = lambda side: pl.BlockSpec(
        (1, 1, rank, rows), lambda i, w: (w[C0], 0, 0, 2 * w[CHIP] + side(w))
    )
    one = lambda shape: pl.BlockSpec(shape, lambda i, w: (0, 0))
    return call(
        ahead_kernel,
        where,
        (x, adapter_up, gate0, adapter_up, adapter_up),
        [
            pl.BlockSpec((tok, each), lambda i, w: (0, i)),
            pl.BlockSpec((1, 1, rank, each), lambda i, w: (w[C0], 0, 0, i)),
            one((tok, rank)),
            u0(lambda w: w[CORE]),
            u0(lambda w: 1 - w[CORE]),
        ],
        [
            jax.ShapeDtypeStruct((tok, width), BF16),
            jax.ShapeDtypeStruct((rank, rows), BF16),
            jax.ShapeDtypeStruct((rank, rows), BF16),
            TOKEN,
        ],
        [
            pl.BlockSpec((tok, each), lambda i, w: (0, i)),
            one((rank, rows)),
            one((rank, rows)),
            one(TOKEN.shape),
        ],
        (grid,),
    )


def gate_kernel(where, x1, mine, sib, gate0, after, sent):
    core = where[CORE]
    half = x1.shape[1] // 2
    skip = mine.shape[1] - half
    z = nt(x1[:, pl.ds(pl.multiple_of(core * half, half), half)], mine[:, skip:])
    z += nt(x1[:, pl.ds(pl.multiple_of((1 - core) * half, half), half)], sib[:, skip:])
    gate1 = (z * jax.nn.sigmoid(z)).astype(BF16)
    both = jnp.concatenate([gate0[...], gate1], axis=1)
    for k in range(sent.shape[0]):
        sent[k] = both


def gates(where, x1, ahead_mine, ahead_sib, gate0, replicas, after):
    tok, rank = gate0.shape
    return local(
        gate_kernel,
        where,
        (x1, ahead_mine, ahead_sib, gate0),
        jax.ShapeDtypeStruct((replicas, tok, 2 * rank), BF16),
        (),
        (after,),
    )


def local(kernel, where, operands, outs, scratch=(), after=(), aliases={}, out_specs=None):
    vmem = pl.BlockSpec(memory_space=pltpu.VMEM)
    out_vmem = [vmem] * len(outs) if isinstance(outs, list) else vmem
    return pl.pallas_call(
        kernel,
        in_specs=[pl.BlockSpec(memory_space=pltpu.SMEM)]
        + [vmem] * len(operands)
        + [vmem] * len(after),
        out_specs=out_specs or out_vmem,
        out_shape=outs,
        scratch_shapes=list(scratch),
        input_output_aliases=aliases,
        compiler_params=pltpu.CompilerParams(vmem_limit_bytes=24 << 20),
        cost_estimate=pl.CostEstimate(flops=0, transcendentals=0, bytes_accessed=0),
    )(where, *operands, *after)


def join_kernel(where, a, b, *rest):
    out = rest[-1]
    out[:a.shape[0]] = a[...]
    out[a.shape[0]:] = b[...]


def join(where, a, b, after=()):
    shape = (a.shape[0] + b.shape[0], a.shape[1])
    return local(
        join_kernel, where, (a, b), jax.ShapeDtypeStruct(shape, a.dtype), (), after
    )


def scale_columns(own, tok):
    replicas = own.shape[0]
    ids = [own[k, tok:tok + 1, :tok].astype(F32) for k in range(replicas)]
    doc = lax.broadcasted_iota(jnp.int32, (2 * replicas, tok), 0).astype(F32)
    hits = jnp.zeros((2 * replicas, tok), F32)
    for row in ids:
        hits += (doc == row).astype(F32)
    count = jnp.maximum(jnp.sum(hits, axis=1, keepdims=True), 1.0)
    table = jnp.sqrt(jnp.sqrt(tok / count))
    scales = [jnp.sum(jnp.where(doc == row, table, 0.0), axis=0, keepdims=True) for row in ids]
    return jnp.concatenate(scales + [jnp.zeros((tok - replicas, tok), F32)], axis=0).T


def gram_kernel(step, where, own, other, *rest):
    core = where[CORE]
    replicas, long, rows = own.shape
    if step:
        got, up_own, up_oth, ahead = rest[:4]
        ups_own, ups_oth = up_own[...], up_oth[...]
    if step == 2:
        one = lambda side: ahead[:, pl.ds(pl.multiple_of(side * rows, rows), rows)]
        ups_own = jnp.concatenate([ups_own, one(core)], axis=0)
        ups_oth = jnp.concatenate([ups_oth, one(1 - core)], axis=0)
    rest = rest[4 if step else 0:]
    tok = long - 8
    hlf = rows // 2
    per = 4
    if step == 2:
        out, token, acc = rest[-3:]
    else:
        acc, token = rest[-2:]
    columns = scale_columns(own, tok)

    for i in range(replicas // per):
        ks = range(i * per, (i + 1) * per)

        def rebuilt(ref, ups):
            act = jnp.concatenate([ref[k, :tok, :] for k in ks], axis=0).astype(F32)
            if step:
                gate = jnp.concatenate([got[k] for k in ks], axis=0)[:, :ups.shape[0]]
                add = jnp.dot(gate, ups, preferred_element_type=F32)
                act = act + add
            scale = [jnp.broadcast_to(columns[:, k:k + 1], (tok, rows)) for k in ks]
            return (jnp.concatenate(scale, axis=0) * act).astype(BF16)

        def put(lo, val):
            hi = lo + val.shape[1]
            acc[:, lo:hi] = val if i == 0 else acc[:, lo:hi] + val

        r = rebuilt(own, ups_own if step else None)
        q = rebuilt(other, ups_oth if step else None)
        put(0, tn(r[:, :hlf], r))
        put(rows, tn(r[:, hlf:], r[:, hlf:]))

        @pl.when(core == 0)
        def _():
            put(rows + hlf, tn(r[:, :hlf], q))

        @pl.when(core == 1)
        def _():
            put(rows + hlf, tn(q[:, hlf:], r))

    token[...] = jnp.zeros_like(token)
    if step == 2:
        out[...] = acc[...].astype(BF16)


def gram(step, where, own, other, ups=(), after=()):
    rows = own.shape[2]
    packed = (rows // 2, rows * 5 // 2)
    return local(
        functools.partial(gram_kernel, step),
        where,
        (own, other, *ups),
        [jax.ShapeDtypeStruct(packed, BF16 if step == 2 else F32), TOKEN],
        [pltpu.VMEM(packed, F32)] if step == 2 else [],
        after,
    )


def project_kernel(where, *refs):
    ins, stash, (proj, m0, by1, by2) = refs[:14], refs[14], refs[16:]
    i = pl.program_id(0)
    rank = stash.shape[2]

    @pl.when(i == 0)
    def _():
        for acc in (proj, m0, by1, by2):
            acc[...] = jnp.zeros_like(acc)
        by1[:rank] = stash[0, 1]
        by2[:rank] = stash[0, 2]

    for g, u, d, d1, u2, b, a in (ins[0::2], ins[1::2]):
        two = b[...]
        proj[:rank] += nt(u[0, 0], g[...])
        proj[rank:] += nt(two, g[...])
        m0[...] += nt(two, d[0, 0])
        by1[rank:, :rank] += nt(b[:rank], d1[0, 0])
        by2[rank:, :rank] += nt(u2[0, 0], a[...])


def project(where, grad, adapter_down, adapter_up, b, b_sib, ahead, ahead_sib, stashed, after):
    tok, width = grad.shape
    rank = adapter_up.shape[2]
    each = ahead.shape[1] - width // 2
    grid = width // 2 // each
    mine, sib = (lambda w: w[CORE]), (lambda w: 1 - w[CORE])

    def half(span, side):
        return pl.BlockSpec(
            (1, 1, rank, each), lambda i, w: (span(w), 0, 0, side(w) * grid + i)
        )

    def weights(span):
        return [half(span, mine), half(span, sib)]

    g_spec = lambda side: pl.BlockSpec((tok, each), lambda i, w: (0, side(w) * grid + i))
    got = lambda skip: pl.BlockSpec((rank, each), lambda i, w: (0, i + skip))
    per = grid // 2
    quarter = pl.BlockSpec((2 * rank, each), lambda i, w: ((i // per + w[PAIR]) % 2, i % per))
    one = lambda w: 1
    shapes = ((3 * rank, tok), (2 * rank, rank), (2 * rank, tok), (2 * rank, tok))
    return call(
        project_kernel,
        where,
        (
            grad, grad, adapter_up, adapter_up, adapter_down, adapter_down,
            adapter_down, adapter_down, adapter_up, adapter_up,
            b, b_sib, ahead, ahead_sib, stashed, after,
        ),
        [g_spec(mine), g_spec(sib)]
        + weights(one)
        + weights(one)
        + weights(lambda w: w[B1])
        + weights(lambda w: w[B2])
        + [quarter] * 2
        + [got(1)] * 2
        + [pl.BlockSpec(stashed.shape, lambda i, w: (0, 0, 0, 0))]
        + [pl.BlockSpec(after.shape, lambda i, w: (0, 0))],
        [jax.ShapeDtypeStruct(shape, F32) for shape in shapes],
        [pl.BlockSpec(shape, lambda i, w: (0, 0)) for shape in shapes],
        (grid,),
    )


def back_kernel(where, proj, m0, by1, by2, q0, *rest):
    outs = rest[-3:]
    rank = m0.shape[1]

    def dz_of(grad_act, q):
        sigma = jax.nn.sigmoid(q)
        return (grad_act * sigma * (1.0 + q * (1.0 - sigma))).astype(BF16)

    def exact(m, d):
        return jnp.dot(
            m, d.astype(F32), precision=lax.Precision.HIGHEST, preferred_element_type=F32
        )

    m12 = jnp.where(where[SEC] == 0, by2[rank:, :rank], by1[rank:, :rank])
    dz0 = dz_of(proj[:rank], q0[0, 0])
    dz1 = dz_of(proj[rank:2 * rank] + exact(m0[:rank], dz0), by1[:rank])
    dz2 = dz_of(proj[2 * rank:] + exact(m0[rank:], dz0) + exact(m12, dz1), by2[:rank])
    for out, dz in zip(outs, (dz0, dz1, dz2)):
        out[...] = nt(dz, dz)


def back(where, proj, m0, by1, by2, stashed, after):
    rank = m0.shape[1]
    return local(
        back_kernel,
        where,
        (proj, m0, by1, by2, stashed),
        [jax.ShapeDtypeStruct((rank, rank), F32)] * 3,
        (),
        (after,),
    )


def merge_kernel(where, a, b, *rest):
    out, token = rest[-2:]
    out[...] = (a[...] + b[...].astype(F32)).astype(BF16)
    token[...] = jnp.zeros_like(token)


def merge(where, a, b, after):
    return local(
        merge_kernel, where, (a, b), [jax.ShapeDtypeStruct(a.shape, BF16), TOKEN], (), after
    )


def curvature_kernel(where, outer0, outer1, outer2, out, token):
    rank = outer0.shape[0]
    f1 = where[B1].astype(F32)
    f2 = where[B2].astype(F32)
    zero = outer1[...] * (1.0 - f1) + outer2[...] * (1.0 - f2)
    one = outer0[...] + outer1[...] * f1 + outer2[...] * f2
    both = jnp.concatenate([zero, one], axis=1)
    for k in range(out.shape[0]):
        out[k] = both
    token[...] = jnp.zeros_like(token)


def curvature(where, outers, replicas):
    rank = outers[0].shape[0]
    return local(
        curvature_kernel, where, outers,
        [jax.ShapeDtypeStruct((replicas, rank, 2 * rank), F32), TOKEN],
    )


def statistics_kernel(tokens, where, old, parts, after, out):
    rank = old.shape[2]
    total = parts[0]
    for k in range(1, parts.shape[0]):
        total = total + parts[k]
    later = where[B1] + where[B2]
    for span, held in enumerate((2 - later, 1 + later)):
        held = jnp.full((rank, rank), held.astype(F32), F32)
        was = old[span, 0]
        share = total[:, span * rank:(span + 1) * rank] / (jnp.maximum(held, 1.0) * tokens)
        out[span, 0] = jnp.where(held > 0.0, 0.75 * was + 0.25 * share, was)


def statistics(where, old, parts, tokens, after):
    return local(
        functools.partial(statistics_kernel, tokens),
        where,
        (old, parts),
        jax.ShapeDtypeStruct(old.shape, F32),
        (),
        (after,),
    )


def put_rows(factor_scale, old, out, buf, sems, first_col, pieces):
    hlf = buf.shape[0] // 2
    cols = pl.ds(pl.multiple_of(first_col, 2 * hlf), 2 * hlf)
    sent = []
    for i, values in enumerate(pieces):
        rows = pl.ds(i * hlf, hlf)
        at = 0
        for value in values():
            here = slice(at, at + value.shape[1])
            was = old[rows, pl.ds(pl.multiple_of(first_col + at, hlf), value.shape[1])]
            buf[rows, here] = 0.75 * was + factor_scale * value
            at += value.shape[1]
        copy = pltpu.make_async_copy(buf.at[rows], out.at[rows, cols], sems.at[i])
        copy.start()
        sent.append(copy)
    for copy in sent:
        copy.wait()


def add_kernel(cut, where, here, came, after, out):
    out[...] = here[:, cut:] + came[:, cut:].astype(F32)


def cross_part(where, here, came, after):
    hlf, width = here.shape
    cut = 3 * hlf
    return local(
        functools.partial(add_kernel, cut), where, (here, came),
        jax.ShapeDtypeStruct((hlf, width - cut), F32), (), (after,),
    )


def square_kernel(factor_scale, where, old, here, came, after, out, buf, sems):
    hlf = here.shape[0]
    rows = 2 * hlf

    def packed(lo, hi):
        return here[:, lo:hi] + came[:, lo:hi].astype(F32)

    put_rows(
        factor_scale, old, out, buf, sems, where[CORE] * rows,
        (
            lambda: [packed(0, hlf), packed(hlf, rows)],
            lambda: [packed(hlf, rows).T, packed(rows, rows + hlf)],
        ),
    )


def cross_kernel(factor_scale, where, old, mine, sib, done, out, token, buf, sems):
    core = where[CORE]
    hlf, rows = mine.shape

    def put(pieces):
        put_rows(factor_scale, old, out, buf, sems, (1 - core) * rows, pieces)

    @pl.when(core == 0)
    def _():
        put(tuple((lambda part=part: [part[:, :hlf], part[:, hlf:]]) for part in (mine, sib)))

    @pl.when(core == 1)
    def _():
        put(
            tuple(
                (lambda a=a: [sib[:, a:a + hlf].T, mine[:, a:a + hlf].T]) for a in (0, hlf)
            )
        )

    token[...] = jnp.zeros_like(token)


def update(factor_scale, where, old, here, came, mine, sib, after):
    total = old.shape[0]
    shape = jax.ShapeDtypeStruct(old.shape, F32)
    scratch = [pltpu.VMEM((total, total), F32), pltpu.SemaphoreType.DMA((2,))]
    vmem = pl.BlockSpec(memory_space=pltpu.VMEM)
    done = local(
        functools.partial(square_kernel, factor_scale), where, (old, here, came), shape, scratch,
        (after,), out_specs=ANY,
    )
    return pl.pallas_call(
        functools.partial(cross_kernel, factor_scale),
        in_specs=[pl.BlockSpec(memory_space=pltpu.SMEM)] + [vmem] * 3 + [ANY],
        out_specs=[ANY, vmem],
        out_shape=[shape, TOKEN],
        scratch_shapes=scratch,
        input_output_aliases={4: 0},
        compiler_params=pltpu.CompilerParams(vmem_limit_bytes=24 << 20),
        cost_estimate=pl.CostEstimate(flops=0, transcendentals=0, bytes_accessed=0),
    )(where, old, mine, sib, done)


def shards(
    entering, returning, adapter_down, adapter_up, stashed, doc_ids, input_factor, output_factor
):
    sec = lax.axis_index("section")
    rep = lax.axis_index("dp")
    sections = lax.axis_size("section")
    replicas = lax.axis_size("dp")
    tok = entering.shape[1]
    steps_count = stashed.shape[1]
    rank = stashed.shape[2]
    rows, block = input_factor.shape[1:]
    tokens = tok * replicas

    def first(home):
        return (home < sections // 2).astype(jnp.int32)

    x0 = entering[0]
    f1 = first((sec + sections - 1) % sections) + (sec == 0).astype(jnp.int32)
    b1 = (sec + 1 < sections).astype(jnp.int32)
    b2 = (sec + 2 < sections).astype(jnp.int32)
    where = jnp.stack(
        [rep // 2, rep % 2, sec, first(sec), f1, b1, b2, rep // 4 % 2]
    ).astype(jnp.int32)

    with jax.named_scope("weights"):
        pieces, gate0 = split(where, x0, adapter_down, doc_ids, replicas, 8)
        ahead, behind1, behind2 = pack(where, adapter_down, adapter_up, block, gate0)
        ahead = shift(ahead, "section", -1)
        behind1 = shift(behind1, "section", 1)
        behind2 = shift(behind2, "section", 2)
        x1, up_own, up_oth, token5 = next_activation(where, x0, adapter_up, gate0, rows)
        ahead = tie(ahead, behind1, behind2, token5, space=pltpu.VMEM)
        ahead_sib = swap_cores(ahead)
        behind = join(where, behind1, behind2)
        behind_pair = swap_chips(behind)

    with jax.named_scope("gates"):
        sent = gates(where, x1, ahead, ahead_sib, gate0, replicas, behind)

    with jax.named_scope("columns"):
        own = tie(lax.all_to_all(pieces, "dp", 0, 0), sent, space=pltpu.VMEM)
        other = swap_cores(own)
        got = lax.all_to_all(sent, "dp", 0, 0)

    with jax.named_scope("factor"):
        ups = (got, up_own, up_oth, ahead)
        step0, token0 = gram(0, where, own, other)
        step2, token2 = gram(2, where, own, other, ups, (token0,))
        from2 = shift(step2, "section", 1)

    with jax.named_scope("backward"):
        behind = join(where, behind, behind_pair, (token0,))
        behind_sib = swap_cores(behind)
        proj, m0, by1, by2 = project(
            where, returning[0], adapter_down, adapter_up, behind, behind_sib, ahead, ahead_sib,
            stashed, token2,
        )
        by1 = shift(by1, "section", 1)
        by2 = shift(by2, "section", 2)

    with jax.named_scope("factor"):
        step1, token1 = gram(1, where, own, other, ups, (m0,))
        from1, token3 = merge(where, step1, from2, (token1, by1, by2))
        from1 = shift(from1, "section", 1)

    with jax.named_scope("backward"):
        outer0, outer1, outer2 = back(where, proj, m0, by1, by2, stashed, token3)
        outer1 = shift(outer1, "section", -1)
        outer2 = shift(outer2, "section", -2)
        share, token4 = curvature(where, (outer0, outer1, outer2), replicas)
        shares = lax.all_to_all(share, "dp", 0, 0)

    with jax.named_scope("factor"):
        mine = cross_part(where, step0, from1, shares)
        sib = swap_cores(mine)
        factor_scale = 0.25 / (steps_count * tokens)
        input_factor_new, last = update(
            factor_scale, where, input_factor[0], step0, from1, mine, sib, token4
        )

    with jax.named_scope("backward"):
        output_factor_new = statistics(where, output_factor, shares, tokens, last)
    return (input_factor_new[None], output_factor_new)


def solution(mesh):
    in_specs = (
        P("section", "dp", None),
        P("section", "dp", None),
        P(None, "section", None, None),
        P(None, "section", None, None),
        P("section", None, None, "dp"),
        P(None, "dp"),
        P("section", "dp", None),
        P(None, "section", None, None),
    )
    out_specs = (P("section", "dp", None), P(None, "section", None, None))
    return jax.shard_map(shards, mesh=mesh, in_specs=in_specs, out_specs=out_specs, check_vma=False)
```
